32 devices in a mesh: head: 4 (over y, x), seq: 8 (over z, core).
Axes of the slice: x: 2, y: 2, z: 4, core: 2. Of those that a mesh axis runs over, the one named last changes fastest.
Arguments:
- inputs: bfloat16 [3072, 2048], P('seq'), may hold values from -6 to 6
- lengths: int32 [8, 2], P('seq'), may hold values from 1 to 246, 352 in all within a row
- first_gain: float32 [2048], replicated, may hold values from 0.25 to 1.75
- query_weight: bfloat16 [2048, 2048], P(None, 'head'), may hold values from -0.125 to 0.125
- key_weight: bfloat16 [2048, 2048], P(None, 'head'), may hold values from -0.125 to 0.125
- value_weight: bfloat16 [2048, 2048], P(None, 'head'), may hold values from -0.125 to 0.125
- gate_weight: bfloat16 [2048, 2048], P(None, 'head'), may hold values from -0.125 to 0.125
- rate_weight: bfloat16 [2048, 32], P(None, 'head'), may hold values from -0.125 to 0.125
- inner_weight: float32 [32, 64, 64], P('head'), may hold values from -0.75 to 0.75
- inner_offset: float32 [32, 64], P('head'), may hold values from -3 to 3
- inner_gain: float32 [32, 64], P('head'), may hold values from 0.25 to 1.75
- inner_shift: float32 [32, 64], P('head'), may hold values from -2 to 2
- post_gain: float32 [2048], P('head'), may hold values from 0.25 to 1.75
- post_shift: float32 [2048], P('head'), may hold values from -2 to 2
- out_weight: bfloat16 [2048, 2048], P('head'), may hold values from -0.25 to 0.25
- second_gain: float32 [2048], replicated, may hold values from 0.25 to 1.75
- feed_gate: bfloat16 [2048, 5504], P(None, 'head'), may hold values from -0.125 to 0.125
- feed_up: bfloat16 [2048, 5504], P(None, 'head'), may hold values from -0.125 to 0.125
- feed_down: bfloat16 [5504, 2048], P('head'), may hold values from -0.15625 to 0.15625
- out_grad: bfloat16 [3072, 2048], P('seq'), may hold values from -6 to 6
Outputs:
- output: bfloat16 [3072, 2048], P('seq')
- input_grad: bfloat16 [3072, 2048], P('seq')
- grad_first_gain: float32 [2048], P('seq')
- grad_query_weight: float32 [2048, 2048], P('seq', 'head')
- grad_key_weight: float32 [2048, 2048], P('seq', 'head')
- grad_value_weight: float32 [2048, 2048], P('seq', 'head')
- grad_gate_weight: float32 [2048, 2048], P('seq', 'head')
- grad_rate_weight: float32 [2048, 32], P('seq', 'head')
- grad_inner_weight: float32 [32, 64, 64], P('head', 'seq')
- grad_inner_offset: float32 [32, 64], P('head', 'seq')
- grad_inner_gain: float32 [32, 64], P('head', 'seq')
- grad_inner_shift: float32 [32, 64], P('head', 'seq')
- grad_post_gain: float32 [2048], P(('head', 'seq'))
- grad_post_shift: float32 [2048], P(('head', 'seq'))
- grad_out_weight: float32 [2048, 2048], P('head', 'seq')
- grad_second_gain: float32 [2048], P('seq')
- grad_feed_gate: float32 [2048, 5504], P('seq', 'head')
- grad_feed_up: float32 [2048, 5504], P('seq', 'head')
- grad_feed_down: float32 [5504, 2048], P('head', 'seq')
The draws below stay inside these ranges and needn't reach their ends.
Inputs may be any that keep to these rules, and one draw needn't show every extreme that they name: Each row holds the lengths of the 2 sequences of one index of seq; padded to multiples of 16 they sum to at most 384, and the longest of each row is at most 246.
All inputs are finite; a program needn't handle non-finite values.
Results may differ from the reference program's by a relative error of at most 0.022.
Values may be sent and summed in bfloat16 or wider, within the bound.
No kernel may reach another device: no remote copies, remote signals or barrier semaphores. Data moves between devices by JAX's collectives and lax.ppermute only.
A program may use at most 256 MiB of HBM per device.

```python
import math
import jax
import jax.numpy as jnp
import numpy as np
from jax import lax

D = 2048
HEADS = 32
HEAD_DIM = 64
FF = 5504
MB = 16
TOK_DEV = 384
SEQ_DEV = 2
LEN_MAX = 246
TOKENS = 3072
N_SEQ = 8


def steps_of(rng, extent, split, smallest, largest):
    def one(dim, shards_of):
        draws = jax.random.uniform(jax.random.fold_in(jax.random.fold_in(rng, 6), dim), (shards_of,), jnp.float32, smallest / len(split), largest / len(split))
        return jnp.repeat(jnp.exp(draws), extent[dim] // shards_of).reshape((-1,) + (1,) * (len(extent) - dim - 1))

    loudness = one(*split[0])
    for cut in split[1:]:
        loudness = loudness * one(*cut)
    return loudness


def length_profile(amount, total, limit, lean):
    loads = [(1 << 20) // math.isqrt(standing ** lean) + 1 for standing in range(2, amount + 1)]
    surplus, counts = total - limit - (amount - 1), [1] * (amount - 1)
    while surplus > 0:
        candidates = [i for i in range(amount - 1) if counts[i] < limit]
        pool, left = sum([loads[i] for i in candidates]), surplus
        for i in candidates:
            more = min(limit - counts[i], max(1, left * loads[i] // pool), surplus)
            counts[i] = counts[i] + more
            surplus = surplus - more
    return np.array([limit] + counts)


def uneven_parts(rng, count, total, most, lean):
    if count == 2:
        one = jax.random.randint(rng, (), max(1, total - most), min(most, total - 1) + 1)
        return jnp.stack([one, total - one])
    tallies = jnp.asarray(length_profile(count, total, most, lean), jnp.int32)
    couples = (count - 1) // 2
    donor, receiver = tallies[1:1 + 2 * couples:2], tallies[2:2 + 2 * couples:2]
    margin = jnp.minimum(donor - 1, most - receiver)
    shifted = jax.random.randint(jax.random.fold_in(rng, 1), (couples,), 0, 1 << 20) % (margin + 1)
    tallies = tallies.at[1:1 + 2 * couples:2].set(donor - shifted).at[2:2 + 2 * couples:2].set(receiver + shifted)
    return tallies[jax.random.permutation(jax.random.fold_in(rng, 2), count)]


def noise(key, extent, width, reach, shards=(), kind=jnp.bfloat16):
    drawn = jax.random.normal(key, extent, jnp.float32) * width
    if len(shards) > 0:
        drawn = steps_of(key, extent, shards, -0.22, 0.18) * drawn
    return jnp.clip(drawn, min=-reach, max=reach).astype(kind)


def setup_inputs(seed: int = 0) -> dict:
    keys = jax.random.split(jax.random.key(seed), 21)
    inputs = noise(keys[0], (TOKENS, D), 1.0, 6.0, ((0, 8),))
    lengths = jax.vmap(lambda own: uneven_parts(own, SEQ_DEV, TOK_DEV - MB * SEQ_DEV, LEN_MAX, 2))(jax.random.split(keys[1], N_SEQ)).reshape((N_SEQ, SEQ_DEV)).astype(jnp.int32)
    first_gain = jnp.clip(1.0 + 0.15 * jax.random.normal(keys[2], (D,), jnp.float32), 0.25, 1.75)
    query_weight = noise(keys[3], (D, D), D ** -0.5, 0.125, ((1, 4),))
    key_weight = noise(keys[4], (D, D), D ** -0.5, 0.125, ((1, 4),))
    value_weight = noise(keys[5], (D, D), D ** -0.5, 0.125, ((1, 4),))
    gate_weight = noise(keys[6], (D, D), D ** -0.5, 0.125, ((1, 4),))
    rate_weight = noise(keys[7], (D, HEADS), D ** -0.5, 0.125, ((1, 4),))
    inner_weight = noise(keys[8], (HEADS, HEAD_DIM, HEAD_DIM), HEAD_DIM ** -0.5, 0.75, ((0, 4),), jnp.float32)
    inner_offset = noise(keys[9], (HEADS, HEAD_DIM), 0.5, 3.0, ((0, 4),), jnp.float32)
    inner_gain = jnp.clip(1.0 + 0.15 * jax.random.normal(keys[10], (HEADS, HEAD_DIM), jnp.float32), 0.25, 1.75)
    inner_shift = noise(keys[11], (HEADS, HEAD_DIM), 0.3, 2.0, ((0, 4),), jnp.float32)
    post_gain = jnp.clip(1.0 + 0.15 * jax.random.normal(keys[12], (D,), jnp.float32), 0.25, 1.75)
    post_shift = noise(keys[13], (D,), 0.3, 2.0, ((0, 4),), jnp.float32)
    out_weight = noise(keys[14], (D, D), (D // 4) ** -0.5, 0.25, ((0, 4),))
    second_gain = jnp.clip(1.0 + 0.15 * jax.random.normal(keys[15], (D,), jnp.float32), 0.25, 1.75)
    feed_gate = noise(keys[16], (D, FF), D ** -0.5, 0.125, ((1, 4),))
    feed_up = noise(keys[17], (D, FF), D ** -0.5, 0.125, ((1, 4),))
    feed_down = noise(keys[18], (FF, D), (FF // 4) ** -0.5, 0.15625, ((0, 4),))
    out_grad = noise(keys[19], (TOKENS, D), 1.0, 6.0, ((0, 8),))
    return {"inputs": inputs, "lengths": lengths, "first_gain": first_gain, "query_weight": query_weight, "key_weight": key_weight, "value_weight": value_weight, "gate_weight": gate_weight, "rate_weight": rate_weight, "inner_weight": inner_weight, "inner_offset": inner_offset, "inner_gain": inner_gain, "inner_shift": inner_shift, "post_gain": post_gain, "post_shift": post_shift, "out_weight": out_weight, "second_gain": second_gain, "feed_gate": feed_gate, "feed_up": feed_up, "feed_down": feed_down, "out_grad": out_grad}


EPS = 1e-06

@jax.custom_vjp
def low(v):
    return lax.optimization_barrier(v.astype(jnp.bfloat16)).astype(jnp.float32)

@jax.custom_vjp
def low_back(v):
    return v

def low_keep(v):
    return (low(v), None)

def low_pass(kept, grad):
    return (grad,)

def back_keep(v):
    return (v, None)

def back_low(kept, grad):
    return (low(grad),)
low.defvjp(low_keep, low_pass)
low_back.defvjp(back_keep, back_low)

def dot_high(left, right):
    return jnp.dot(left, right, precision=lax.Precision.HIGHEST, preferred_element_type=jnp.float32)

def rms_scale(values, gain_by):
    return values * lax.rsqrt(lax.optimization_barrier(jnp.mean(values * values, axis=-1, keepdims=True)) + EPS) * gain_by

def layer_norm(values, gain_by, shift_by):
    centred = values - lax.optimization_barrier(jnp.mean(values, axis=-1, keepdims=True))
    inv_std = lax.rsqrt(lax.optimization_barrier(jnp.mean(centred * centred, axis=-1, keepdims=True)) + EPS)
    return centred * inv_std * gain_by + shift_by

def inner_grad(inner_preactivation, target, gain_by, shift_by):
    centred = inner_preactivation - lax.optimization_barrier(jnp.mean(inner_preactivation, axis=-1, keepdims=True))
    inv_std = lax.rsqrt(lax.optimization_barrier(jnp.mean(centred * centred, axis=-1, keepdims=True)) + EPS)
    normed = centred * inv_std
    scaled_logits = (normed * gain_by + shift_by - target) * gain_by
    return inv_std * (scaled_logits - lax.optimization_barrier(jnp.mean(scaled_logits, axis=-1, keepdims=True)) - normed * lax.optimization_barrier(jnp.mean(scaled_logits * normed, axis=-1, keepdims=True)))

def flags(lengths_row, token_count):
    padded = (lengths_row + MB - 1) // MB * MB
    offsets = (jnp.cumsum(padded) - padded).astype(jnp.int32)
    position = jnp.arange(token_count, dtype=jnp.int32)
    inside = (position[:, None] >= offsets[None, :]) & (position[:, None] < offsets[None, :] + lengths_row[None, :])
    valid = jnp.any(inside, axis=1).astype(jnp.float32)
    firsts = jnp.arange(token_count // MB, dtype=jnp.int32) * MB
    starts = jnp.any(firsts[:, None] == offsets[None, :], axis=1)
    return (valid, starts)

def mixer(query_in, key_in, value_in, gate_in, rate_logit, inner_weight, inner_offset, inner_gain, inner_shift, post_gain, post_shift, valid, starts):
    token_count = query_in.shape[0]
    head_count, head_width = inner_offset.shape
    block_count = token_count // MB
    precision_level = lax.Precision.HIGHEST

    def to_blocks(source):
        return source.reshape(block_count, MB, head_count, head_width).transpose(0, 2, 1, 3)
    step_rates = jax.nn.sigmoid(rate_logit) * valid[:, None] / head_width
    step_rates = step_rates.reshape(block_count, MB, head_count).transpose(0, 2, 1)
    causal = jnp.tril(jnp.ones((MB, MB), jnp.float32))
    gain_rows = inner_gain[:, None, :]
    shift_rows = inner_shift[:, None, :]

    def advance(carry, item):
        hidden_state_weight, hidden_state_bias = carry
        block_query_rows, block_key_rows, blk_value, blk_rate, restart = item
        hidden_state_weight = jnp.where(restart, inner_weight, hidden_state_weight)
        hidden_state_bias = jnp.where(restart, inner_offset, hidden_state_bias)
        inner_preactivation = jnp.einsum('cfg,cgy->cfy', block_key_rows, hidden_state_weight, precision=precision_level) + hidden_state_bias[:, None, :]
        inner_gradient_list = inner_grad(inner_preactivation, blk_value - block_key_rows, gain_rows, shift_rows)
        attention_logits = jnp.einsum('euc,elc->eul', block_query_rows, block_key_rows, precision=precision_level)
        mixing = (attention_logits + 1.0) * causal * blk_rate[:, None, :]
        inner_output = jnp.einsum('cfg,cgy->cfy', block_query_rows, hidden_state_weight, precision=precision_level) + hidden_state_bias[:, None, :]
        inner_output = inner_output - jnp.einsum('hmn,hne->hme', mixing, inner_gradient_list, precision=precision_level)
        result = block_query_rows + layer_norm(inner_output, gain_rows, shift_rows)
        scaled_logits = blk_rate[:, :, None] * block_key_rows
        updated_weight = hidden_state_weight - jnp.einsum('nxr,nxi->nri', scaled_logits, inner_gradient_list, precision=precision_level)
        next_bias = hidden_state_bias - lax.optimization_barrier(jnp.sum(blk_rate[:, :, None] * inner_gradient_list, axis=1))
        return ((updated_weight, next_bias), result)
    items = (to_blocks(query_in), to_blocks(key_in), to_blocks(value_in), step_rates, starts)
    unused, results = lax.scan(jax.checkpoint(advance), (inner_weight, inner_offset), items)
    results = layer_norm(results, post_gain.reshape(head_count, 1, head_width), post_shift.reshape(head_count, 1, head_width))
    mixed = results.transpose(0, 2, 1, 3).reshape(token_count, head_count * head_width)
    return mixed * jax.nn.gelu(gate_in, approximate=True) * valid[:, None]

def block(source, lengths_row, first_gain, query_weight, key_weight, value_weight, gate_weight, rate_weight, inner_weight, inner_offset, inner_gain, inner_shift, post_gain, post_shift, out_weight, second_gain, feed_gate, feed_up, feed_down):
    valid, starts = flags(lengths_row, source.shape[0])
    normed_one = low(rms_scale(source, first_gain))
    query = low(low_back(dot_high(normed_one, query_weight)))
    key_rows = low(low_back(dot_high(normed_one, key_weight)))
    value = low(low_back(dot_high(normed_one, value_weight)))
    gate = low(low_back(dot_high(normed_one, gate_weight)))
    rate_logit = dot_high(normed_one, rate_weight)
    mixed = low(mixer(query, key_rows, value, gate, rate_logit, inner_weight, inner_offset, inner_gain, inner_shift, post_gain, post_shift, valid, starts))
    branch = low_back(dot_high(mixed, out_weight))
    hidden_one = source + branch
    normed_two = low(rms_scale(hidden_one, second_gain))
    gate_pre = low_back(dot_high(normed_two, feed_gate))
    up_pre = low_back(dot_high(normed_two, feed_up))
    activ = low(jax.nn.silu(gate_pre) * up_pre)
    feed_out = low_back(dot_high(activ, feed_down))
    return hidden_one + feed_out

def reference(inputs, lengths, first_gain, query_weight, key_weight, value_weight, gate_weight, rate_weight, inner_weight, inner_offset, inner_gain, inner_shift, post_gain, post_shift, out_weight, second_gain, feed_gate, feed_up, feed_down, out_grad):
    weights = (first_gain, query_weight, key_weight, value_weight, gate_weight, rate_weight, inner_weight, inner_offset, inner_gain, inner_shift, post_gain, post_shift, out_weight, second_gain, feed_gate, feed_up, feed_down)
    weights = tuple((item.astype(jnp.float32) for item in weights))
    streams = inputs.astype(jnp.float32).reshape(N_SEQ, TOK_DEV, D)
    cotangents = out_grad.astype(jnp.float32).reshape(N_SEQ, TOK_DEV, D)

    def one_stream(totals, item):
        source, lengths_row, cotangent = item

        def forward(source_in, *params):
            return block(source_in, lengths_row, *params)
        result, backward = jax.vjp(forward, source, *weights)
        grads = backward(cotangent)
        totals = tuple((total + grad for total, grad in zip(totals, grads[1:])))
        return (totals, (result.astype(jnp.bfloat16), grads[0].astype(jnp.bfloat16)))
    zeros = tuple((jnp.zeros_like(item) for item in weights))
    totals, (results, input_grads) = lax.scan(one_stream, zeros, (streams, lengths, cotangents))
    return (results.reshape(TOKENS, D), input_grads.reshape(TOKENS, D), totals[0], totals[1], totals[2], totals[3], totals[4], totals[5], totals[6], totals[7], totals[8], totals[9], totals[10], totals[11], totals[12], totals[13], totals[14], totals[15], totals[16])
```

```python
import functools

import jax
import jax.numpy as jnp
from jax import lax
from jax.experimental import pallas as pl
from jax.experimental.pallas import tpu as pltpu
from jax.sharding import PartitionSpec as P

MB=16; EPS=1e-6
bf=jnp.bfloat16; f32=jnp.float32

def dot_nn(a,b): return lax.dot_general(a,b,(((1,),(0,)),((),())),preferred_element_type=f32)
def dot_nt(a,b): return lax.dot_general(a,b,(((1,),(1,)),((),())),preferred_element_type=f32)
def dot_tn(a,b): return lax.dot_general(a,b,(((0,),(0,)),((),())),preferred_element_type=f32)

def mean0(x): return jnp.mean(x,axis=0,keepdims=True)

def norm_parts(x):
    c=x-mean0(x)
    inv=lax.rsqrt(mean0(c*c)+EPS)
    return c*inv,inv

def norm_back(dy,n,inv):
    return inv*(dy-mean0(dy)-n*mean0(dy*n))

def split2(x):
    hi=x.astype(bf)
    return jnp.concatenate([hi,(x-hi.astype(f32)).astype(bf)],axis=0)

def two_rows(x):
    h=x.shape[0]//2
    return x[:h]+x[h:]

def stack_heads(rows,F):
    H=rows.shape[1]//F
    r=rows.astype(f32)
    return jnp.concatenate([r[:,h*F:(h+1)*F] for h in range(H)],axis=0).T

GC=0.7978845608028654; GA=0.044715
def gelu_parts(x):
    u=GC*(x+GA*x*x*x)
    t=jnp.tanh(u)
    val=0.5*x*(1.0+t)
    der=0.5*(1.0+t)+0.5*x*(1.0-t*t)*GC*(1.0+3.0*GA*x*x)
    return val,der

def plan_blocks(len_ref,NB):
    n0=(len_ref[0,0]+MB-1)//MB; n1=(len_ref[0,1]+MB-1)//MB
    return (n0,n1),(0,n0)

def lane_iota(shape,dim): return lax.broadcasted_iota(jnp.int32,shape,dim)

def valid_row(len_ref,counts,offs,blk,L):
    pos=blk*MB+lane_iota((1,L),1)%MB
    a=(pos>=offs[0]*MB)&(pos<offs[0]*MB+len_ref[0,0])
    b=(pos>=offs[1]*MB)&(pos<offs[1]*MB+len_ref[0,1])
    return a|b

def fill_bd(dst,blk,rows,row0,F):
    H=rows.shape[1]//F
    for h in range(H):
        dst[blk,row0+h*MB:row0+(h+1)*MB,h*F:(h+1)*F]=rows[:,h*F:(h+1)*F]

def same_head(L):
    return lane_iota((L,L),0)//MB==lane_iota((L,L),1)//MB

def head_lanes(H,L):
    return (lane_iota((H,L),0)==lane_iota((H,L),1)//MB).astype(f32)

HIGH=lax.Precision.HIGHEST
def spread(per_head,rep):
    return lax.dot_general(per_head,rep,(((0,),(0,)),((),())),precision=HIGH,preferred_element_type=f32)
def gather_heads(x,rep):
    return lax.dot_general(rep,x,(((1,),(1,)),((),())),precision=HIGH,preferred_element_type=f32)

def fwd_kernel(UN,len_ref,q_ref,k_ref,v_ref,g_ref,rlh_ref,w0_ref,b0_ref,gainh_ref,shifth_ref,pgh_ref,psh_ref,
               mixed_ref,zt_ref,rt_ref,wt_ref,mt_ref,
               kq,tt,rate,mtb,wst,bst,rl_ref,gain_ref,shift_ref,pg_ref,ps_ref):
    T,C=q_ref.shape; H,F=b0_ref.shape; L=H*MB; NB=T//MB
    rep=head_lanes(H,L)
    rl_ref[...]=lax.dot_general(rlh_ref[...],rep,(((1,),(0,)),((),())),precision=HIGH,preferred_element_type=f32)
    gain_ref[...]=spread(gainh_ref[...],rep); shift_ref[...]=spread(shifth_ref[...],rep)
    pg_ref[...]=spread(pgh_ref[...],rep); ps_ref[...]=spread(psh_ref[...],rep)
    counts,offs=plan_blocks(len_ref,NB)
    zero_kq=jnp.zeros((2*L,C),bf)
    onesbd=same_head(L).astype(f32).astype(bf)
    keep=same_head(L)&(lane_iota((L,L),0)<=lane_iota((L,L),1))
    pick=lane_iota((MB,L),0)==lane_iota((MB,L),1)%MB
    def clear(b,_):
        kq[b]=zero_kq
        return 0
    lax.fori_loop(0,NB+1,clear,0)
    tt[NB]=jnp.zeros((F,L),f32); rate[NB]=jnp.zeros((1,L),f32); mtb[NB]=jnp.zeros((L,2*L),bf)
    def pre_one(b):
        r=pl.multiple_of(b*MB,MB)
        kn=k_ref[pl.ds(r,MB),:]; qn=q_ref[pl.ds(r,MB),:]; vn=v_ref[pl.ds(r,MB),:]
        fill_bd(kq,b,kn,0,F); fill_bd(kq,b,qn,L,F)
        tt[b]=stack_heads(vn,F)-stack_heads(kn,F)
        ok=valid_row(len_ref,counts,offs,b,L)
        rl=jnp.sum(jnp.where(pick,rl_ref[pl.ds(r,MB),:],0.0),axis=0,keepdims=True)
        rate[b]=jnp.where(ok,jax.nn.sigmoid(rl)*(1.0/F),0.0)
        st=dot_nt(kq[b,0:L,:],kq[b,L:2*L,:])
        m=jnp.where(keep,st+1.0,0.0).astype(bf)
        mt_ref[b]=m
        mtb[b,:,0:L]=m; mtb[b,:,L:2*L]=onesbd
        rt_ref[b]=jnp.zeros((F,L),f32)
        zt_ref[b]=jnp.zeros((F,L),f32)
        wt_ref[b]=jnp.zeros((F,C),bf)
    def pre(i,_):
        for u in range(UN): pre_one(i*UN+u)
        return 0
    lax.fori_loop(0,NB//UN,pre,0)
    bias0=spread(b0_ref[...],rep)
    for h in range(H):
        wh=w0_ref[h].T
        for s in range(2): wst[s,:,h*F:(h+1)*F]=wh
    for s in range(2): bst[s]=bias0
    def step(i,_):
        for s in range(2):
            b=jnp.where(i<counts[s],offs[s]+i,NB)
            w=wst[s]; bias=bst[s]
            w2=split2(w)
            wt_ref[b]=w2[:F]
            zq=two_rows(dot_nt(w2,kq[b]))
            z=zq[:,:L]+bias; qw=zq[:,L:]+bias
            zt_ref[b]=z
            n,inv=norm_parts(z)
            p=(n*gain_ref[...]+shift_ref[...]-tt[b])*gain_ref[...]
            g=inv*(p-mean0(p)-n*mean0(p*n))
            gr=split2(g*rate[b])
            ob=two_rows(dot_nn(gr,mtb[b]))
            rt_ref[b]=qw-ob[:,:L]
            bst[s]=bias-ob[:,L:]
            wst[s]=w-two_rows(dot_nn(gr,kq[b,0:L,:]))
        return 0
    lax.fori_loop(0,jnp.maximum(counts[0],counts[1]),step,0)
    def post_one(b):
        r=pl.multiple_of(b*MB,MB)
        qt=stack_heads(q_ref[pl.ds(r,MB),:],F); gt=stack_heads(g_ref[pl.ds(r,MB),:],F)
        nr,_=norm_parts(rt_ref[b])
        io=qt+nr*gain_ref[...]+shift_ref[...]
        ni,_=norm_parts(io)
        act,_=gelu_parts(gt)
        ok=valid_row(len_ref,counts,offs,b,L)
        m=jnp.where(ok,act*(ni*pg_ref[...]+ps_ref[...]),0.0).T
        for h in range(H):
            mixed_ref[pl.ds(r,MB),h*F:(h+1)*F]=m[h*MB:(h+1)*MB,:].astype(bf)
    def post(i,_):
        for u in range(UN): post_one(i*UN+u)
        return 0
    lax.fori_loop(0,NB//UN,post,0)

def bwd_kernel(UN,len_ref,q_ref,k_ref,v_ref,g_ref,rlh_ref,dm_ref,zt_ref,rt_ref,wt_ref,mt_ref,gainh_ref,shifth_ref,pgh_ref,psh_ref,
               dq_ref,dk_ref,dv_ref,dg_ref,drlh_ref,dw0_ref,db0h_ref,dgainh_ref,dshifth_ref,dpgh_ref,dpsh_ref,
               kq,rate,ns,ps_,gs,xs,rs,ios,rows,zs,es,dws,wst,bst,rl_ref,gain_ref,shift_ref,pg_ref,ps_ref,
               dgain_ref,dshift_ref,dpg_ref,dps_ref,drl_ref):
    T,C=q_ref.shape; H,F=gainh_ref.shape; L=H*MB; NB=T//MB
    rep=head_lanes(H,L)
    rl_ref[...]=lax.dot_general(rlh_ref[...],rep,(((1,),(0,)),((),())),precision=HIGH,preferred_element_type=f32)
    gain_ref[...]=spread(gainh_ref[...],rep); shift_ref[...]=spread(shifth_ref[...],rep)
    pg_ref[...]=spread(pgh_ref[...],rep); ps_ref[...]=spread(psh_ref[...],rep)
    counts,offs=plan_blocks(len_ref,NB)
    zero_kq=jnp.zeros((2*L,C),bf)
    onesbd=same_head(L).astype(f32).astype(bf)
    keep=same_head(L)&(lane_iota((L,L),0)<=lane_iota((L,L),1))
    keep_t=same_head(L)&(lane_iota((L,L),1)<=lane_iota((L,L),0))
    pick=lane_iota((MB,L),0)==lane_iota((MB,L),1)%MB
    zfl=jnp.zeros((F,L),f32)
    def clear(b,_):
        kq[b]=zero_kq
        return 0
    lax.fori_loop(0,NB+1,clear,0)
    for ref in (ns,ps_,gs,xs,rs): ref[NB]=zfl
    rate[NB]=jnp.zeros((1,L),f32); rows[NB]=jnp.zeros((8,L),f32)
    for ref in (dgain_ref,dshift_ref,dpg_ref,dps_ref): ref[...]=zfl
    def pre_one(b):
        r=pl.multiple_of(b*MB,MB)
        kn=k_ref[pl.ds(r,MB),:]; qn=q_ref[pl.ds(r,MB),:]
        fill_bd(kq,b,kn,0,F); fill_bd(kq,b,qn,L,F)
        t=stack_heads(v_ref[pl.ds(r,MB),:],F)-stack_heads(kn,F)
        qt=stack_heads(qn,F); gt=stack_heads(g_ref[pl.ds(r,MB),:],F)
        dm=stack_heads(dm_ref[pl.ds(r,MB),:],F)
        ok=valid_row(len_ref,counts,offs,b,L)
        rl=jnp.sum(jnp.where(pick,rl_ref[pl.ds(r,MB),:],0.0),axis=0,keepdims=True)
        sg=jax.nn.sigmoid(rl)
        rt=jnp.where(ok,sg*(1.0/F),0.0)
        rate[b]=rt
        gain=gain_ref[...]; shift=shift_ref[...]
        n,inv=norm_parts(zt_ref[b])
        e=n*gain+shift-t
        p=e*gain
        mpn=mean0(p*n)
        g=inv*(p-mean0(p)-n*mpn)
        nr,invr=norm_parts(rt_ref[b])
        io=qt+nr*gain+shift
        ni,invi=norm_parts(io)
        act,der=gelu_parts(gt)
        lo=ni*pg_ref[...]+ps_ref[...]
        dgt=jnp.where(ok,dm*lo*der,0.0).T
        for h in range(H):
            dg_ref[pl.ds(r,MB),h*F:(h+1)*F]=dgt[h*MB:(h+1)*MB,:].astype(bf)
        dl=jnp.where(ok,dm*act,0.0)
        dio=norm_back(dl*pg_ref[...],ni,invi)
        dr=norm_back(dio*gain,nr,invr)
        drb=dr.astype(bf)
        ns[b]=n; ps_[b]=e; gs[b]=g; rs[b]=dr; ios[b]=dio
        xs[b]=dot_nt(drb,mt_ref[b])
        rows[b]=jnp.concatenate([inv,mpn,sg*(1.0-sg)*jnp.where(ok,1.0/F,0.0),jnp.zeros((5,L),f32)],axis=0)
        zs[b]=zfl; es[b]=zfl; dws[b]=jnp.zeros((F,C),bf)
        return dl,dl*ni,dio,dio*nr
    def pre(i,_):
        acc=None
        for u in range(UN):
            x=pre_one(i*UN+u)
            acc=x if acc is None else tuple(a+c for a,c in zip(acc,x))
        dps_ref[...]+=acc[0]; dpg_ref[...]+=acc[1]; dshift_ref[...]+=acc[2]; dgain_ref[...]+=acc[3]
        return 0
    lax.fori_loop(0,NB//UN,pre,0)
    for s in range(2):
        wst[s]=jnp.zeros((F,C),f32); bst[s]=zfl
    steps=jnp.maximum(counts[0],counts[1])
    def step(j,_):
        i=steps-1-j
        for s in range(2):
            b=jnp.where(i<counts[s],offs[s]+i,NB)
            w=wst[s]; bias=bst[s]
            w2=split2(w)
            dws[b]=w2[:F]
            x=two_rows(dot_nt(w2,kq[b,0:L,:]))+bias+xs[b]
            g=gs[b]; n=ns[b]; gain=gain_ref[...]; p=ps_[b]*gain
            row=rows[b]
            inv=row[0:1]; mpn=row[1:2]
            rows[b,3:4,:]=-jnp.sum(g*x,axis=0,keepdims=True)*row[2:3]
            h=-rate[b]*x
            da=inv*h
            m1=mean0(da*n); m2=mean0(da); m3=mean0(h*g)
            dp=da-m2-n*m1
            de=dp*gain
            dn=de*gain-da*mpn-p*m1
            dz=inv*(dn-mean0(dn)-n*(mean0(dn*n)+m3))
            zs[b]=dz; es[b]=dp
            dr=rs[b]
            zr=jnp.concatenate([dz,dr],axis=1)
            wst[s]=w+two_rows(dot_nn(split2(zr),kq[b]))
            bst[s]=bias+two_rows(dot_nn(split2(dz+dr),onesbd))
        return 0
    lax.fori_loop(0,steps,step,0)
    for h in range(H):
        dw0_ref[h]=(wst[0,:,h*F:(h+1)*F]+wst[1,:,h*F:(h+1)*F]).T
    db0h_ref[...]=gather_heads(bst[0]+bst[1],jnp.where(lane_iota((H,L),1)%MB==0,rep,0.0))
    def post_one(b):
        r=pl.multiple_of(b*MB,MB)
        dp=es[b]; row=rows[b]
        de=dp*gain_ref[...]
        dgain=dp*ps_[b]+de*ns[b]
        gr=(gs[b]*rate[b])
        drb=rs[b].astype(bf); grb=gr.astype(bf); dzb=zs[b].astype(bf)
        dst=jnp.where(keep,-dot_tn(grb,drb),0.0).astype(bf)
        dss=jnp.where(keep_t,-dot_tn(drb,grb),0.0).astype(bf)
        wt=wt_ref[b]
        kb=kq[b,0:L,:]; qb=kq[b,L:2*L,:]
        dqf=dot_tn(jnp.concatenate([drb,dst],axis=0),jnp.concatenate([wt,kb],axis=0))
        dkf=dot_tn(jnp.concatenate([dzb,(-gr).astype(bf),dss],axis=0),jnp.concatenate([wt,dws[b],qb],axis=0))
        det=de.T; dit=ios[b].T
        for h in range(H):
            rr=slice(h*MB,(h+1)*MB); cc=slice(h*F,(h+1)*F)
            dq_ref[pl.ds(r,MB),cc]=(dqf[rr,cc]+dit[rr,:]).astype(bf)
            dk_ref[pl.ds(r,MB),cc]=(dkf[rr,cc]+det[rr,:]).astype(bf)
            dv_ref[pl.ds(r,MB),cc]=(-det[rr,:]).astype(bf)
        drl_ref[pl.ds(r,MB),:]=jnp.where(pick,row[3:4],0.0)
        return dgain,de
    def post(i,_):
        acc=None
        for u in range(UN):
            x=post_one(i*UN+u)
            acc=x if acc is None else tuple(a+c for a,c in zip(acc,x))
        dgain_ref[...]+=acc[0]; dshift_ref[...]+=acc[1]
        return 0
    lax.fori_loop(0,NB//UN,post,0)
    dgainh_ref[...]=gather_heads(dgain_ref[...],rep); dshifth_ref[...]=gather_heads(dshift_ref[...],rep)
    dpgh_ref[...]=gather_heads(dpg_ref[...],rep); dpsh_ref[...]=gather_heads(dps_ref[...],rep)
    drlh_ref[...]=lax.dot_general(drl_ref[...],rep,(((1,),(1,)),((),())),precision=HIGH,preferred_element_type=f32)

VM=pl.BlockSpec(memory_space=pltpu.VMEM); SM=pl.BlockSpec(memory_space=pltpu.SMEM)

def mixer_fwd(lengths,q,k,v,g,rl,w0,b0,gain,shift,pg,ps,UN=2,interpret=False):
    T,C=q.shape; H,F=b0.shape; L=H*MB; NB=T//MB
    S=jax.ShapeDtypeStruct
    fl=pltpu.VMEM((F,L),f32)
    return pl.pallas_call(functools.partial(fwd_kernel,UN),
        out_shape=[S((T,C),bf),S((NB+1,F,L),f32),S((NB+1,F,L),f32),S((NB+1,F,C),bf),S((NB,L,L),bf)],
        in_specs=[SM]+[VM]*11,out_specs=[VM]*5,
        scratch_shapes=[pltpu.VMEM((NB+1,2*L,C),bf),pltpu.VMEM((NB+1,F,L),f32),pltpu.VMEM((NB+1,1,L),f32),
            pltpu.VMEM((NB+1,L,2*L),bf),pltpu.VMEM((2,F,C),f32),pltpu.VMEM((2,F,L),f32),pltpu.VMEM((T,L),f32),fl,fl,fl,fl],
        name='mixer_forward',interpret=interpret)(lengths,q,k,v,g,rl,w0,b0,gain,shift,pg,ps)

def mixer_bwd(lengths,q,k,v,g,rl,dm,zt,rt,wt,mt,gain,shift,pg,ps,UN=2,interpret=False):
    T,C=q.shape; H,F=gain.shape; L=H*MB; NB=T//MB
    S=jax.ShapeDtypeStruct
    fls=pltpu.VMEM((NB+1,F,L),f32); fl=pltpu.VMEM((F,L),f32)
    return pl.pallas_call(functools.partial(bwd_kernel,UN),
        out_shape=[S((T,C),bf)]*4+[S((T,H),f32),S((H,F,F),f32)]+[S((H,F),f32)]*5,
        in_specs=[SM]+[VM]*14,out_specs=[VM]*11,
        scratch_shapes=[pltpu.VMEM((NB+1,2*L,C),bf),pltpu.VMEM((NB+1,1,L),f32)]+[fls]*6+[
            pltpu.VMEM((NB+1,8,L),f32),fls,fls,pltpu.VMEM((NB+1,F,C),bf),pltpu.VMEM((2,F,C),f32),pltpu.VMEM((2,F,L),f32),
            pltpu.VMEM((T,L),f32)]+[fl]*8+[pltpu.VMEM((T,L),f32)],
        name='mixer_backward',interpret=interpret)(lengths,q,k,v,g,rl,dm,zt,rt,wt,mt,gain,shift,pg,ps)


def dot_f32(a, b):
    return jnp.dot(a, b, preferred_element_type=f32)


def rms_inv(x):
    return lax.rsqrt(jnp.mean(x * x, axis=-1, keepdims=True) + EPS)


class Links:
    def __init__(self, mesh):
        self.nh = mesh.shape["head"]
        self.nq = mesh.shape["seq"]
        self.nz = self.nq // 2
        self.bits = self.nh.bit_length() - 1
        self.orders = (tuple(range(self.bits - 1, -1, -1)), tuple(range(self.bits)))

    def place(self):
        self.h = lax.axis_index("head")
        self.s = lax.axis_index("seq")
        self.c = self.s % 2
        self.z = self.s // 2

    def bit(self, b):
        return (self.h >> b) & 1

    def partner(self, x, b):
        return lax.ppermute(x, "head", [(i, i ^ (1 << b)) for i in range(self.nh)])

    def sibling(self, x):
        return lax.ppermute(x, "seq", [(i, i ^ 1) for i in range(self.nq)])

    def head_scatter(self, x):
        rows, width = x.shape
        piece = rows // self.nh // 2
        x = x.reshape((2,) * self.bits + (2, piece, width))
        out = []
        for half, order in enumerate(self.orders):
            y = x[(slice(None),) * self.bits + (half,)]
            dims = list(range(self.bits - 1, -1, -1))
            for b in order:
                ax = dims.index(b)
                mine = lax.dynamic_index_in_dim(y, self.bit(b), ax, keepdims=False)
                other = lax.dynamic_index_in_dim(y, 1 - self.bit(b), ax, keepdims=False)
                y = mine + self.partner(other.astype(bf), b).astype(f32)
                dims.pop(ax)
            out.append(y)
        return jnp.concatenate(out, axis=0)

    def head_gather(self, x):
        rows, width = x.shape
        piece = rows // 2
        out = []
        for half, order in enumerate(self.orders):
            y = x[half * piece : (half + 1) * piece]
            dims = []
            for b in reversed(order):
                ax = sum(1 for d in dims if d > b)
                got = self.partner(y, b)
                low = self.bit(b) == 0
                y = jnp.stack([jnp.where(low, y, got), jnp.where(low, got, y)], axis=ax)
                dims.append(b)
            out.append(y)
        y = jnp.stack(out, axis=self.bits)
        return y.reshape(rows * self.nh, width)

    def head_total(self, x):
        for b in range(self.bits):
            x = x + self.partner(x, b)
        return x

    def own_rows(self, x):
        n = x.shape[0] // self.nh
        return lax.dynamic_slice_in_dim(x, self.h * n, n, axis=0)

    def blocks(self, x, core):
        rows, width = x.shape
        y = x.reshape(rows, self.nz, 2, width // self.nq)
        return lax.dynamic_index_in_dim(y, core, 2, keepdims=False).reshape(rows, width // 2)

    def both_blocks(self, x):
        return jnp.concatenate([self.blocks(x, self.c), self.sibling(self.blocks(x, 1 - self.c))], axis=0)

    def both(self, x):
        return jnp.concatenate([x, self.sibling(x)], axis=0)

    def line_reduce(self, parts, kind=bf):
        nz, z = self.nz, self.z

        def take(i):
            return lax.dynamic_index_in_dim(parts, jnp.clip(i, 0, nz - 1), 0, keepdims=False).astype(f32)

        def add(x, y):
            return x if y is None else x + y.astype(f32)

        up = down = None
        for t in range(1, nz):
            ups = [(2 * p + c, 2 * p + 2 + c) for p in range(min(t - 1, nz - 2) + 1) for c in range(2)]
            downs = [(2 * p + c, 2 * p - 2 + c) for p in range(max(nz - t, 1), nz) for c in range(2)]
            up = lax.ppermute(add(take(nz - t + z), up).astype(kind), "seq", ups)
            down = lax.ppermute(add(take(t - nz + z), down).astype(kind), "seq", downs)
        return add(add(take(z), up), down)

    def grad_rows(self, xb, n):
        p = lax.dot_general(xb, n, (((0,), (0,)), ((), ())), preferred_element_type=f32).astype(bf)
        return self.line_reduce(p.reshape(self.nz, -1, n.shape[1]))

    def grad_columns(self, n, xb):
        p = lax.dot_general(xb, n, (((0,), (0,)), ((), ())), preferred_element_type=f32).astype(bf)
        return self.line_reduce(p.reshape(self.nz, -1, n.shape[1])).T


def per_device(
    links,
    inputs,
    lengths,
    first_gain,
    query_weight,
    key_weight,
    value_weight,
    gate_weight,
    rate_weight,
    inner_weight,
    inner_offset,
    inner_gain,
    inner_shift,
    post_gain,
    post_shift,
    out_weight,
    second_gain,
    feed_gate,
    feed_up,
    feed_down,
    out_grad,
):
    links.place()
    nz, nq = links.nz, links.nq
    source = inputs.astype(f32)
    normed_one = (first_gain * (source * rms_inv(source))).astype(bf)
    query = dot_f32(normed_one, query_weight).astype(bf)
    key = dot_f32(normed_one, key_weight).astype(bf)
    value = dot_f32(normed_one, value_weight).astype(bf)
    gate = dot_f32(normed_one, gate_weight).astype(bf)
    rate_logit = dot_f32(normed_one, rate_weight)
    heads, width = inner_offset.shape
    pg, ps = post_gain.reshape(heads, width), post_shift.reshape(heads, width)
    mixed, zt, rt, wt, mt = mixer_fwd(
        lengths, query, key, value, gate, rate_logit, inner_weight, inner_offset, inner_gain, inner_shift, pg, ps
    )
    own_source = links.own_rows(inputs).astype(f32)
    own_upstream = links.own_rows(out_grad).astype(f32)
    activ_grad = lax.dot_general(out_grad, feed_down, (((1,), (1,)), ((), ())), preferred_element_type=f32)

    hidden = own_source + links.head_scatter(dot_f32(mixed, out_weight))
    r2 = rms_inv(hidden)
    normed_two = links.head_gather((second_gain * (hidden * r2)).astype(bf))

    gate_pre = dot_f32(normed_two, feed_gate)
    up_pre = dot_f32(normed_two, feed_up)
    sig = jax.nn.sigmoid(gate_pre)
    activ = (gate_pre * sig * up_pre).astype(bf)
    gate_pre_grad = (activ_grad * up_pre * sig * (1.0 + gate_pre * (1.0 - sig))).astype(bf)
    up_pre_grad = (activ_grad * gate_pre * sig).astype(bf)

    two = lax.dot_general(gate_pre_grad, feed_gate, (((1,), (1,)), ((), ())), preferred_element_type=f32)
    two = two + lax.dot_general(up_pre_grad, feed_up, (((1,), (1,)), ((), ())), preferred_element_type=f32)
    two = links.head_scatter(two)
    u = two * second_gain
    hidden_grad = own_upstream + r2 * u - hidden * (r2 * r2 * r2) * jnp.mean(u * hidden, axis=-1, keepdims=True)
    second_part = jnp.sum(two * hidden * r2, axis=0)
    branch_grad = links.head_gather(hidden_grad.astype(bf))
    mixed_grad = lax.dot_general(
        branch_grad, out_weight, (((1,), (1,)), ((), ())), preferred_element_type=f32
    ).astype(bf)

    grad_up_block = links.both_blocks(out_grad)
    grad_feed_down = links.grad_columns(links.both(activ), grad_up_block)
    two_block = links.both_blocks(normed_two)
    grad_feed_gate = links.grad_rows(two_block, links.both(gate_pre_grad))
    grad_feed_up = links.grad_rows(two_block, links.both(up_pre_grad))
    output = hidden + links.head_scatter(dot_f32(activ, feed_down))
    output = links.head_gather(output.astype(bf))
    grad_out_weight = links.grad_columns(links.both(mixed), links.both_blocks(branch_grad))

    dq, dk, dv, dg, drate, dw0, db0, dgain, dshift, dpg, dps = mixer_bwd(
        lengths, query, key, value, gate, rate_logit, mixed_grad, zt, rt, wt, mt, inner_gain, inner_shift, pg, ps
    )
    back = (((1,), (1,)), ((), ()))
    part = lax.dot_general(dq, query_weight, back, preferred_element_type=f32)
    part = part + lax.dot_general(dk, key_weight, back, preferred_element_type=f32)
    part = part + lax.dot_general(dv, value_weight, back, preferred_element_type=f32)
    part = part + lax.dot_general(dg, gate_weight, back, preferred_element_type=f32)
    part = part + lax.dot_general(drate.astype(bf), rate_weight, back, preferred_element_type=f32)
    one = links.head_scatter(part)
    r1 = rms_inv(own_source)
    w = one * first_gain
    input_grad = hidden_grad + r1 * w - own_source * (r1 * r1 * r1) * jnp.mean(w * own_source, axis=-1, keepdims=True)
    input_grad = links.head_gather(input_grad.astype(bf))
    first_part = jnp.sum(one * own_source * r1, axis=0)

    one_block = links.both_blocks(normed_one)
    grad_query = links.grad_rows(one_block, links.both(dq))
    grad_key = links.grad_rows(one_block, links.both(dk))
    grad_value = links.grad_rows(one_block, links.both(dv))
    grad_gate = links.grad_rows(one_block, links.both(dg))
    rate_part = lax.dot_general(
        normed_one, drate.astype(bf), (((0,), (0,)), ((), ())), preferred_element_type=f32
    )

    def rows_of(x):
        return x.reshape(nq, -1)

    def heads_of(x):
        return x.reshape((heads, nq, -1)).transpose(1, 0, 2).reshape(nq, -1)

    small = [rows_of(first_part), rows_of(second_part), rows_of(rate_part), heads_of(dw0)]
    small += [heads_of(x) for x in (db0, dgain, dshift)] + [rows_of(dpg), rows_of(dps)]
    sizes = [x.shape[1] for x in small]
    small = jnp.concatenate(small, axis=1).reshape(nz, 2, -1)
    keep = lax.dynamic_index_in_dim(small, links.c, 1, keepdims=False)
    give = lax.dynamic_index_in_dim(small, 1 - links.c, 1, keepdims=False)
    small = links.line_reduce(keep + links.sibling(give), f32)
    ends = [sum(sizes[: i + 1]) for i in range(len(sizes))]
    small = [small[e - n : e] for e, n in zip(ends, sizes)]
    gains = links.head_total(jnp.stack([small[0], small[1]]))
    per = width // nq
    return (
        output,
        input_grad,
        gains[0],
        grad_query,
        grad_key,
        grad_value,
        grad_gate,
        small[2].reshape(-1, heads),
        small[3].reshape(heads, per, width),
        small[4].reshape(heads, per),
        small[5].reshape(heads, per),
        small[6].reshape(heads, per),
        small[7],
        small[8],
        grad_out_weight,
        gains[1],
        grad_feed_gate,
        grad_feed_up,
        grad_feed_down,
    )


def solution(mesh):
    in_specs = (
        P("seq", None),
        P("seq", None),
        P(),
        P(None, "head"),
        P(None, "head"),
        P(None, "head"),
        P(None, "head"),
        P(None, "head"),
        P("head", None, None),
        P("head", None),
        P("head", None),
        P("head", None),
        P("head"),
        P("head"),
        P("head", None),
        P(),
        P(None, "head"),
        P(None, "head"),
        P("head", None),
        P("seq", None),
    )
    out_specs = (
        P("seq", None),
        P("seq", None),
        P("seq"),
        P("seq", "head"),
        P("seq", "head"),
        P("seq", "head"),
        P("seq", "head"),
        P("seq", "head"),
        P("head", "seq", None),
        P("head", "seq"),
        P("head", "seq"),
        P("head", "seq"),
        P(("head", "seq")),
        P(("head", "seq")),
        P("head", "seq"),
        P("seq"),
        P("seq", "head"),
        P("seq", "head"),
        P("head", "seq"),
    )
    return jax.shard_map(
        functools.partial(per_device, Links(mesh)), mesh=mesh, in_specs=in_specs, out_specs=out_specs, check_vma=False
    )
```

```python
import functools

import jax
import jax.numpy as jnp
from jax import lax
from jax.experimental import pallas as pl
from jax.experimental.pallas import tpu as pltpu
from jax.sharding import PartitionSpec as P

MB=16; EPS=1e-6
bf=jnp.bfloat16; f32=jnp.float32

def dot_nn(a,b): return lax.dot_general(a,b,(((1,),(0,)),((),())),preferred_element_type=f32)
def dot_nt(a,b): return lax.dot_general(a,b,(((1,),(1,)),((),())),preferred_element_type=f32)
def dot_tn(a,b): return lax.dot_general(a,b,(((0,),(0,)),((),())),preferred_element_type=f32)

def mean0(x): return jnp.mean(x,axis=0,keepdims=True)

def norm_parts(x):
    c=x-mean0(x)
    inv=lax.rsqrt(mean0(c*c)+EPS)
    return c*inv,inv

def norm_back(dy,n,inv):
    return inv*(dy-mean0(dy)-n*mean0(dy*n))

def split2(x):
    hi=x.astype(bf)
    return jnp.concatenate([hi,(x-hi.astype(f32)).astype(bf)],axis=0)

def two_rows(x):
    h=x.shape[0]//2
    return x[:h]+x[h:]

def stack_heads(rows,F):
    H=rows.shape[1]//F
    r=rows.astype(f32)
    return jnp.concatenate([r[:,h*F:(h+1)*F] for h in range(H)],axis=0).T

GC=0.7978845608028654; GA=0.044715
def gelu_parts(x):
    u=GC*(x+GA*x*x*x)
    t=jnp.tanh(u)
    val=0.5*x*(1.0+t)
    der=0.5*(1.0+t)+0.5*x*(1.0-t*t)*GC*(1.0+3.0*GA*x*x)
    return val,der

def plan_blocks(where):
    n0=(where[1]+MB-1)//MB; n1=(where[2]+MB-1)//MB
    return (n0,n1),(0,n0)

def row_of(where,b,per):
    return pl.multiple_of(((lax.div(b,per)^where[0])*per+lax.rem(b,per))*MB,MB)

def lane_iota(shape,dim): return lax.broadcasted_iota(jnp.int32,shape,dim)

def valid_row(where,offs,blk,L):
    pos=blk*MB+lane_iota((1,L),1)%MB
    a=(pos>=offs[0]*MB)&(pos<offs[0]*MB+where[1])
    b=(pos>=offs[1]*MB)&(pos<offs[1]*MB+where[2])
    return a|b

def fill_bd(dst,blk,rows,row0,F):
    H=rows.shape[1]//F
    for h in range(H):
        dst[blk,row0+h*MB:row0+(h+1)*MB,h*F:(h+1)*F]=rows[:,h*F:(h+1)*F]

def same_head(L):
    return lane_iota((L,L),0)//MB==lane_iota((L,L),1)//MB

def head_lanes(H,L):
    return (lane_iota((H,L),0)==lane_iota((H,L),1)//MB).astype(f32)

HIGH=lax.Precision.HIGHEST
def head_rows(ref,F):
    return jnp.concatenate([ref[:,i:i+F] for i in range(0,ref.shape[1],F)],axis=0)
def spread(per_head,rep):
    return lax.dot_general(per_head,rep,(((0,),(0,)),((),())),precision=HIGH,preferred_element_type=f32)
def gather_heads(x,rep):
    return lax.dot_general(rep,x,(((1,),(1,)),((),())),precision=HIGH,preferred_element_type=f32)

def fwd_kernel(UN,PER,where,q_ref,k_ref,v_ref,g_ref,rlh_ref,w0_ref,b0_ref,gainh_ref,shifth_ref,pgh_ref,psh_ref,
               mixed_ref,slope_ref,zt_ref,rt_ref,wt_ref,mt_ref,
               kq,tt,rate,mtb,wst,bst,rl_ref,gain_ref,shift_ref,pg_ref,ps_ref):
    T,C=q_ref.shape; H,F=b0_ref.shape; L=H*MB; NB=T//MB
    rep=head_lanes(H,L)
    rl_ref[...]=lax.dot_general(rlh_ref[...],rep,(((1,),(0,)),((),())),precision=HIGH,preferred_element_type=f32)
    gain_ref[...]=spread(gainh_ref[...],rep); shift_ref[...]=spread(shifth_ref[...],rep)
    pg_ref[...]=spread(head_rows(pgh_ref,F),rep); ps_ref[...]=spread(head_rows(psh_ref,F),rep)
    counts,offs=plan_blocks(where)
    zero_kq=jnp.zeros((2*L,C),bf)
    onesbd=same_head(L).astype(f32).astype(bf)
    keep=same_head(L)&(lane_iota((L,L),0)<=lane_iota((L,L),1))
    pick=lane_iota((MB,L),0)==lane_iota((MB,L),1)%MB
    def clear(b,_):
        kq[b]=zero_kq
        return 0
    lax.fori_loop(0,NB+1,clear,0)
    tt[NB]=jnp.zeros((F,L),f32); rate[NB]=jnp.zeros((1,L),f32); mtb[NB]=jnp.zeros((L,2*L),bf)
    def pre_one(b):
        r=row_of(where,b,PER)
        kn=k_ref[pl.ds(r,MB),:]; qn=q_ref[pl.ds(r,MB),:]; vn=v_ref[pl.ds(r,MB),:]
        fill_bd(kq,b,kn,0,F); fill_bd(kq,b,qn,L,F)
        tt[b]=stack_heads(vn,F)-stack_heads(kn,F)
        ok=valid_row(where,offs,b,L)
        rl=jnp.sum(jnp.where(pick,rl_ref[pl.ds(r,MB),:],0.0),axis=0,keepdims=True)
        rate[b]=jnp.where(ok,jax.nn.sigmoid(rl)*(1.0/F),0.0)
        st=dot_nt(kq[b,0:L,:],kq[b,L:2*L,:])
        m=jnp.where(keep,st+1.0,0.0).astype(bf)
        mt_ref[b]=m
        mtb[b,:,0:L]=m; mtb[b,:,L:2*L]=onesbd
        rt_ref[b]=jnp.zeros((F,L),f32)
        zt_ref[b]=jnp.zeros((F,L),f32)
        wt_ref[b]=jnp.zeros((F,C),bf)
    def pre(i,_):
        for u in range(UN): pre_one(i*UN+u)
        return 0
    lax.fori_loop(0,NB//UN,pre,0)
    bias0=spread(b0_ref[...],rep)
    for h in range(H):
        wh=w0_ref[h].T
        for s in range(2): wst[s,:,h*F:(h+1)*F]=wh
    for s in range(2): bst[s]=bias0
    def step(i,_):
        for s in range(2):
            b=jnp.where(i<counts[s],offs[s]+i,NB)
            w=wst[s]; bias=bst[s]
            w2=split2(w)
            wt_ref[b]=w2[:F]
            zq=two_rows(dot_nt(w2,kq[b]))
            z=zq[:,:L]+bias; qw=zq[:,L:]+bias
            zt_ref[b]=z
            n,inv=norm_parts(z)
            p=(n*gain_ref[...]+shift_ref[...]-tt[b])*gain_ref[...]
            g=inv*(p-mean0(p)-n*mean0(p*n))
            gr=split2(g*rate[b])
            ob=two_rows(dot_nn(gr,mtb[b]))
            rt_ref[b]=qw-ob[:,:L]
            bst[s]=bias-ob[:,L:]
            wst[s]=w-two_rows(dot_nn(gr,kq[b,0:L,:]))
        return 0
    lax.fori_loop(0,jnp.maximum(counts[0],counts[1]),step,0)
    def post_one(b):
        r=row_of(where,b,PER)
        qt=stack_heads(q_ref[pl.ds(r,MB),:],F); gt=stack_heads(g_ref[pl.ds(r,MB),:],F)
        nr,_=norm_parts(rt_ref[b])
        io=qt+nr*gain_ref[...]+shift_ref[...]
        ni,_=norm_parts(io)
        act,der=gelu_parts(gt)
        ok=valid_row(where,offs,b,L)
        lo=jnp.where(ok,ni*pg_ref[...]+ps_ref[...],0.0)
        m=(act*lo).T; sl=(der*lo).T
        for h in range(H):
            mixed_ref[pl.ds(r,MB),h*F:(h+1)*F]=m[h*MB:(h+1)*MB,:].astype(bf)
            slope_ref[pl.ds(r,MB),h*F:(h+1)*F]=sl[h*MB:(h+1)*MB,:].astype(bf)
    def post(i,_):
        for u in range(UN): post_one(i*UN+u)
        return 0
    lax.fori_loop(0,NB//UN,post,0)

def bwd_kernel(UN,PER,where,q_ref,k_ref,v_ref,g_ref,rlh_ref,dm_ref,zt_ref,rt_ref,wt_ref,mt_ref,gainh_ref,shifth_ref,pgh_ref,psh_ref,
               dqkv_ref,drlh_ref,dw0_ref,db0h_ref,dgainh_ref,dshifth_ref,dpgh_ref,dpsh_ref,
               kq,rate,ns,ps_,gs,xs,rs,ios,rows,zs,es,dws,wst,bst,rl_ref,gain_ref,shift_ref,pg_ref,ps_ref,
               dgain_ref,dshift_ref,dpg_ref,dps_ref,drl_ref):
    T,C=q_ref.shape; H,F=gainh_ref.shape; L=H*MB; NB=T//MB
    rep=head_lanes(H,L)
    rl_ref[...]=lax.dot_general(rlh_ref[...],rep,(((1,),(0,)),((),())),precision=HIGH,preferred_element_type=f32)
    gain_ref[...]=spread(gainh_ref[...],rep); shift_ref[...]=spread(shifth_ref[...],rep)
    pg_ref[...]=spread(head_rows(pgh_ref,F),rep); ps_ref[...]=spread(head_rows(psh_ref,F),rep)
    counts,offs=plan_blocks(where)
    zero_kq=jnp.zeros((2*L,C),bf)
    onesbd=same_head(L).astype(f32).astype(bf)
    keep=same_head(L)&(lane_iota((L,L),0)<=lane_iota((L,L),1))
    keep_t=same_head(L)&(lane_iota((L,L),1)<=lane_iota((L,L),0))
    pick=lane_iota((MB,L),0)==lane_iota((MB,L),1)%MB
    zfl=jnp.zeros((F,L),f32)
    def clear(b,_):
        kq[b]=zero_kq
        return 0
    lax.fori_loop(0,NB+1,clear,0)
    for ref in (ns,ps_,gs,xs,rs): ref[NB]=zfl
    rate[NB]=jnp.zeros((1,L),f32); rows[NB]=jnp.zeros((8,L),f32)
    for ref in (dgain_ref,dshift_ref,dpg_ref,dps_ref): ref[...]=zfl
    def pre_one(b):
        r=row_of(where,b,PER)
        kn=k_ref[pl.ds(r,MB),:]; qn=q_ref[pl.ds(r,MB),:]
        fill_bd(kq,b,kn,0,F); fill_bd(kq,b,qn,L,F)
        t=stack_heads(v_ref[pl.ds(r,MB),:],F)-stack_heads(kn,F)
        qt=stack_heads(qn,F); gt=stack_heads(g_ref[pl.ds(r,MB),:],F)
        dm=stack_heads(dm_ref[pl.ds(r,MB),:],F)
        ok=valid_row(where,offs,b,L)
        rl=jnp.sum(jnp.where(pick,rl_ref[pl.ds(r,MB),:],0.0),axis=0,keepdims=True)
        sg=jax.nn.sigmoid(rl)
        rt=jnp.where(ok,sg*(1.0/F),0.0)
        rate[b]=rt
        gain=gain_ref[...]; shift=shift_ref[...]
        n,inv=norm_parts(zt_ref[b])
        e=n*gain+shift-t
        p=e*gain
        mpn=mean0(p*n)
        g=inv*(p-mean0(p)-n*mpn)
        nr,invr=norm_parts(rt_ref[b])
        io=qt+nr*gain+shift
        ni,invi=norm_parts(io)
        act,_=gelu_parts(gt)
        dl=jnp.where(ok,dm*act,0.0)
        dio=norm_back(dl*pg_ref[...],ni,invi)
        dr=norm_back(dio*gain,nr,invr)
        drb=dr.astype(bf)
        ns[b]=n; ps_[b]=e; gs[b]=g; rs[b]=dr; ios[b]=dio
        xs[b]=dot_nt(drb,mt_ref[b])
        rows[b]=jnp.concatenate([inv,mpn,sg*(1.0-sg)*jnp.where(ok,1.0/F,0.0),jnp.zeros((5,L),f32)],axis=0)
        zs[b]=zfl; es[b]=zfl; dws[b]=jnp.zeros((F,C),bf)
        return dl,dl*ni,dio,dio*nr
    def pre(i,_):
        acc=None
        for u in range(UN):
            x=pre_one(i*UN+u)
            acc=x if acc is None else tuple(a+c for a,c in zip(acc,x))
        dps_ref[...]+=acc[0]; dpg_ref[...]+=acc[1]; dshift_ref[...]+=acc[2]; dgain_ref[...]+=acc[3]
        return 0
    lax.fori_loop(0,NB//UN,pre,0)
    for s in range(2):
        wst[s]=jnp.zeros((F,C),f32); bst[s]=zfl
    steps=jnp.maximum(counts[0],counts[1])
    def step(j,_):
        i=steps-1-j
        for s in range(2):
            b=jnp.where(i<counts[s],offs[s]+i,NB)
            w=wst[s]; bias=bst[s]
            w2=split2(w)
            dws[b]=w2[:F]
            x=two_rows(dot_nt(w2,kq[b,0:L,:]))+bias+xs[b]
            g=gs[b]; n=ns[b]; gain=gain_ref[...]; p=ps_[b]*gain
            row=rows[b]
            inv=row[0:1]; mpn=row[1:2]
            rows[b,3:4,:]=-jnp.sum(g*x,axis=0,keepdims=True)*row[2:3]
            h=-rate[b]*x
            da=inv*h
            m1=mean0(da*n); m2=mean0(da); m3=mean0(h*g)
            dp=da-m2-n*m1
            de=dp*gain
            dn=de*gain-da*mpn-p*m1
            dz=inv*(dn-mean0(dn)-n*(mean0(dn*n)+m3))
            zs[b]=dz; es[b]=dp
            dr=rs[b]
            zr=jnp.concatenate([dz,dr],axis=1)
            wst[s]=w+two_rows(dot_nn(split2(zr),kq[b]))
            bst[s]=bias+two_rows(dot_nn(split2(dz+dr),onesbd))
        return 0
    lax.fori_loop(0,steps,step,0)
    for h in range(H):
        dw0_ref[h]=(wst[0,:,h*F:(h+1)*F]+wst[1,:,h*F:(h+1)*F]).T
    db0h_ref[...]=gather_heads(bst[0]+bst[1],jnp.where(lane_iota((H,L),1)%MB==0,rep,0.0))
    def post_one(b):
        r=row_of(where,b,PER)
        dp=es[b]; row=rows[b]
        de=dp*gain_ref[...]
        dgain=dp*ps_[b]+de*ns[b]
        gr=(gs[b]*rate[b])
        drb=rs[b].astype(bf); grb=gr.astype(bf); dzb=zs[b].astype(bf)
        dst=jnp.where(keep,-dot_tn(grb,drb),0.0).astype(bf)
        dss=jnp.where(keep_t,-dot_tn(drb,grb),0.0).astype(bf)
        wt=wt_ref[b]
        kb=kq[b,0:L,:]; qb=kq[b,L:2*L,:]
        dqf=dot_tn(jnp.concatenate([drb,dst],axis=0),jnp.concatenate([wt,kb],axis=0))
        dkf=dot_tn(jnp.concatenate([dzb,(-gr).astype(bf),dss],axis=0),jnp.concatenate([wt,dws[b],qb],axis=0))
        det=de.T; dit=ios[b].T
        for h in range(H):
            rr=slice(h*MB,(h+1)*MB); cc=slice(h*F,(h+1)*F)
            dqkv_ref[pl.ds(r,MB),h*F:(h+1)*F]=(dqf[rr,cc]+dit[rr,:]).astype(bf)
            dqkv_ref[pl.ds(r,MB),C+h*F:C+(h+1)*F]=(dkf[rr,cc]+det[rr,:]).astype(bf)
            dqkv_ref[pl.ds(r,MB),2*C+h*F:2*C+(h+1)*F]=(-det[rr,:]).astype(bf)
        drl_ref[pl.ds(r,MB),:]=jnp.where(pick,row[3:4],0.0)
        return dgain,de
    def post(i,_):
        acc=None
        for u in range(UN):
            x=post_one(i*UN+u)
            acc=x if acc is None else tuple(a+c for a,c in zip(acc,x))
        dgain_ref[...]+=acc[0]; dshift_ref[...]+=acc[1]
        return 0
    lax.fori_loop(0,NB//UN,post,0)
    dgainh_ref[...]=gather_heads(dgain_ref[...],rep); dshifth_ref[...]=gather_heads(dshift_ref[...],rep)
    dpgh_ref[...]=gather_heads(dpg_ref[...],rep); dpsh_ref[...]=gather_heads(dps_ref[...],rep)
    drlh_ref[...]=lax.dot_general(drl_ref[...],rep,(((1,),(1,)),((),())),precision=HIGH,preferred_element_type=f32)

VM=pl.BlockSpec(memory_space=pltpu.VMEM); SM=pl.BlockSpec(memory_space=pltpu.SMEM)

def mixer_fwd(where,per,q,k,v,g,rl,w0,b0,gain,shift,pg,ps,UN=2):
    T,C=q.shape; H,F=b0.shape; L=H*MB; NB=T//MB
    S=jax.ShapeDtypeStruct
    fl=pltpu.VMEM((F,L),f32)
    return pl.pallas_call(functools.partial(fwd_kernel,UN,per),
        out_shape=[S((T,C),bf),S((T,C),bf),S((NB+1,F,L),f32),S((NB+1,F,L),f32),S((NB+1,F,C),bf),S((NB,L,L),bf)],
        in_specs=[SM]+[VM]*11,out_specs=[VM]*6,
        scratch_shapes=[pltpu.VMEM((NB+1,2*L,C),bf),pltpu.VMEM((NB+1,F,L),f32),pltpu.VMEM((NB+1,1,L),f32),
            pltpu.VMEM((NB+1,L,2*L),bf),pltpu.VMEM((2,F,C),f32),pltpu.VMEM((2,F,L),f32),pltpu.VMEM((T,L),f32),fl,fl,fl,fl],
        cost_estimate=cost(28),
        name='mixer_forward')(where,q,k,v,g,rl,w0,b0,gain,shift,pg,ps)

def mixer_bwd(where,per,q,k,v,g,rl,dm,zt,rt,wt,mt,gain,shift,pg,ps,UN=2):
    T,C=q.shape; H,F=gain.shape; L=H*MB; NB=T//MB
    S=jax.ShapeDtypeStruct
    fls=pltpu.VMEM((NB+1,F,L),f32); fl=pltpu.VMEM((F,L),f32)
    return pl.pallas_call(functools.partial(bwd_kernel,UN,per),
        out_shape=[S((T,3*C),bf),S((T,H),f32),S((H,F,F),f32)]+[S((H,F),f32)]*5,
        in_specs=[SM]+[VM]*14,out_specs=[VM]*8,
        scratch_shapes=[pltpu.VMEM((NB+1,2*L,C),bf),pltpu.VMEM((NB+1,1,L),f32)]+[fls]*6+[
            pltpu.VMEM((NB+1,8,L),f32),fls,fls,pltpu.VMEM((NB+1,F,C),bf),pltpu.VMEM((2,F,C),f32),pltpu.VMEM((2,F,L),f32),
            pltpu.VMEM((T,L),f32)]+[fl]*8+[pltpu.VMEM((T,L),f32)],
        cost_estimate=cost(33),
        name='mixer_backward')(where,q,k,v,g,rl,dm,zt,rt,wt,mt,gain,shift,pg,ps)


def cost(us):
    return pl.CostEstimate(flops=int(us * 1e9), bytes_accessed=int(us * 1e6), transcendentals=0)


def whole(x):
    return pl.BlockSpec(x.shape, lambda *_: (0,) * x.ndim)


SDS = jax.ShapeDtypeStruct


def project_kernel(nh, where, x_ref, gain_ref, wq, wk, wv, wg, wr, xn, q, k, v, g, rl):
    n = x_ref.shape[0] // nh

    @pl.when(pl.program_id(0) == 0)
    def _():
        for r in range(nh):
            x = x_ref[pl.ds(pl.multiple_of((where[0] ^ r) * n, MB), n), :].astype(f32)
            inv = lax.rsqrt(jnp.mean(x * x, axis=-1, keepdims=True) + EPS)
            xn[r * n : (r + 1) * n, :] = (gain_ref[...] * (x * inv)).astype(bf)
        rl[...] = dot_nt(xn[...], wr[...])

    for w, o in ((wq, q), (wk, k), (wv, v), (wg, g)):
        o[...] = dot_nn(xn[...], w[...]).astype(bf)


def project(nh, where, x, gain, weights, wr, tile=256):
    T, D = x.shape
    C, H = weights[0].shape[1], wr.shape[0]
    col = pl.BlockSpec((D, tile), lambda j: (0, j))
    out = pl.BlockSpec((T, tile), lambda j: (0, j))
    return pl.pallas_call(
        functools.partial(project_kernel, nh),
        grid=(C // tile,),
        in_specs=[SM, whole(x), whole(gain)] + [col] * 4 + [whole(wr)],
        out_specs=[pl.BlockSpec((T, D), lambda j: (0, 0))] + [out] * 4 + [pl.BlockSpec((T, H), lambda j: (0, 0))],
        out_shape=[SDS((T, D), bf)] + [SDS((T, C), bf)] * 4 + [SDS((T, H), f32)],
        cost_estimate=cost(8),
        name="project",
    )(where, x, gain, *weights, wr)


def split_kernel(kinds, more, *refs):
    n = len(kinds)
    acc = None
    for turned, a, b in zip(kinds, refs[:n], refs[n : 2 * n]):
        y = (dot_nt if turned else dot_nn)(a[...], b[...])
        acc = y if acc is None else acc + y
    extra, outs = refs[2 * n : 2 * n + more], refs[2 * n + more :]
    rows = outs[0].shape[0]
    for r, o in enumerate(outs):
        o[:rows, :] = acc[r * rows : (r + 1) * rows].astype(o.dtype)
        if r and more:
            o[rows:, :] = extra[r - 1][...]


def split_product(nh, terms, name, us, extra=(), tile=512):
    T = terms[0][0].shape[0]
    D = terms[0][1].shape[0 if terms[0][2] else 1]
    a_specs, b_specs = [], []
    for a, b, turned, col in terms:
        depth = b.shape[1 if turned else 0]
        a_specs.append(pl.BlockSpec((T, depth), lambda j, col=col: (0, col)))
        b_specs.append(
            pl.BlockSpec((tile, depth), lambda j: (j, 0)) if turned else pl.BlockSpec((depth, tile), lambda j: (0, j))
        )
    n = T // nh
    rows = [n] + [2 * n if extra else n] * (nh - 1)
    return pl.pallas_call(
        functools.partial(split_kernel, [t[2] for t in terms], len(extra)),
        grid=(D // tile,),
        in_specs=a_specs + b_specs + [pl.BlockSpec((n, tile), lambda j: (0, j))] * len(extra),
        out_specs=[pl.BlockSpec((m, tile), lambda j: (0, j)) for m in rows],
        out_shape=[SDS((m, D), bf if r else f32) for r, m in enumerate(rows)],
        cost_estimate=cost(us),
        name=name,
    )(*[t[0] for t in terms], *[t[1] for t in terms], *extra)


def feed_kernel(plan, n, chunk, *refs):
    arrays = refs[:n]
    wg, wu, wd, x, og, activ, dgate, dup = refs[n:]

    @pl.when(pl.program_id(0) == 0)
    def _():
        for which, (rows_x, rows_g) in enumerate(plan):
            for target, (a, at) in ((x, rows_x), (og, rows_g)):
                n_rows = x.shape[0] // len(plan)
                target[which * n_rows : (which + 1) * n_rows, :] = arrays[a][at : at + n_rows, :]

    def body(i, _):
        rows = pl.ds(pl.multiple_of(i * chunk, MB), chunk)
        gate = dot_nt(x[rows, :], wg[...])
        up = dot_nt(x[rows, :], wu[...])
        back = dot_nt(og[rows, :], wd[...])
        sig = jax.nn.sigmoid(gate)
        silu = gate * sig
        activ[rows, :] = (silu * up).astype(bf)
        dgate[rows, :] = (back * up * sig * (1.0 + gate * (1.0 - sig))).astype(bf)
        dup[rows, :] = (back * silu).astype(bf)
        return 0

    lax.fori_loop(0, x.shape[0] // chunk, body, 0)


def feed(n_rows, plan, arrays, wg, wu, wd, name, us, tile=256):
    T = n_rows * len(plan)
    N, D = wg.shape
    chunk = max(c for c in range(MB, 385, MB) if T % c == 0)
    row = pl.BlockSpec((tile, D), lambda j: (j, 0))
    flat = pl.BlockSpec((T, D), lambda j: (0, 0))
    return pl.pallas_call(
        functools.partial(feed_kernel, plan, len(arrays), chunk),
        grid=(pl.cdiv(N, tile),),
        in_specs=[whole(x) for x in arrays] + [row] * 3,
        out_specs=[flat, flat] + [pl.BlockSpec((T, tile), lambda j: (0, j))] * 3,
        out_shape=[SDS((T, D), bf)] * 2 + [SDS((T, N), bf)] * 3,
        cost_estimate=cost(us),
        name=name,
    )(*arrays, wg, wu, wd)


def branch_kernel(n, *refs):
    pieces = refs[:n]
    w, slope, flat, mg, dg = refs[n:]

    @pl.when(pl.program_id(0) == 0)
    def _():
        rows = flat.shape[0] // n
        for i, a in enumerate(pieces):
            flat[i * rows : (i + 1) * rows, :] = a[:rows, :]

    y = dot_nt(flat[...], w[...])
    mg[...] = y.astype(bf)
    dg[...] = (y * slope[...].astype(f32)).astype(bf)


def branch_back(pieces, n, w, slope, tile=256):
    T, C = slope.shape
    D = w.shape[1]
    out = pl.BlockSpec((T, tile), lambda j: (0, j))
    return pl.pallas_call(
        functools.partial(branch_kernel, len(pieces)),
        grid=(C // tile,),
        in_specs=[whole(x) for x in pieces] + [pl.BlockSpec((tile, D), lambda j: (j, 0)), out],
        out_specs=[pl.BlockSpec((T, D), lambda j: (0, 0)), out, out],
        out_shape=[SDS((T, D), bf), SDS((T, C), bf), SDS((T, C), bf)],
        cost_estimate=cost(4),
        name="branch_back",
    )(*pieces, w, slope)


def blocks_kernel(groups, turned, *refs):
    refs = refs[1:]
    n = sum(groups)
    xs, ns, outs = refs[:n], refs[n : 2 * n], refs[2 * n :]
    parts, at = [], 0
    for count in groups:
        y = None
        for i in range(at, at + count):
            p = dot_tn(xs[i][...], ns[i][...])
            y = p if y is None else y + p
        parts.append(y)
        at += count
    for k, o in enumerate(outs):
        @pl.when(pl.program_id(0) == k)
        def _(o=o):
            at = 0
            for y in parts:
                if turned:
                    o[at : at + y.shape[1], :] = y.T.astype(o.dtype)
                else:
                    o[:, at : at + y.shape[1]] = y.astype(o.dtype)
                at += y.shape[1]


def block_products(where, stride, groups, kinds, wide, name, us, turned=False):
    xs = [x for group in groups for x, _ in group]
    ns = [n for group in groups for _, n in group]
    N = sum(group[0][1].shape[1] for group in groups)
    x_specs = [pl.BlockSpec((x.shape[0], wide), lambda k, where: (0, where[3 + stride * k])) for x in xs]
    n_specs = [pl.BlockSpec(n.shape, lambda k, where: (0, 0)) for n in ns]
    shape = (N, wide) if turned else (wide, N)
    return pl.pallas_call(
        functools.partial(blocks_kernel, [len(group) for group in groups], turned),
        grid_spec=pltpu.PrefetchScalarGridSpec(
            num_scalar_prefetch=1,
            grid=(len(kinds),),
            in_specs=x_specs + n_specs,
            out_specs=[pl.BlockSpec(shape, lambda k, where: (0, 0))] * len(kinds),
        ),
        out_shape=[SDS(shape, kind) for kind in kinds],
        cost_estimate=cost(us),
        name=name,
    )(where, *xs, *ns)


def natural_kernel(nh, where, *refs):
    pieces, outs = refs[:nh], refs[nh:]
    n = outs[0].shape[0] // nh
    for r in range(nh):
        for i, out in enumerate(outs):
            out[pl.ds(pl.multiple_of((where[0] ^ r) * n, MB), n), :] = pieces[r][i * n : (i + 1) * n, :]


def natural(where, pieces, n, count):
    nh = len(pieces)
    D = pieces[0].shape[1]
    return pl.pallas_call(
        functools.partial(natural_kernel, nh),
        in_specs=[SM] + [VM] * nh,
        out_specs=[VM] * count,
        out_shape=[SDS((n * nh, D), pieces[0].dtype)] * count,
        cost_estimate=cost(4),
        name="natural",
    )(where, *pieces)


def add_rows(x, row):
    high = row.astype(bf)
    low = (row - high.astype(f32)).astype(bf)
    rest = jnp.zeros((MB - 2, row.shape[0]), bf)
    return jnp.concatenate([x, high[None], low[None], rest], axis=0)


def last_rows(x):
    return x[-MB].astype(f32) + x[1 - MB].astype(f32)


def after(x, *others):
    return lax.optimization_barrier((x, others))[0]


def rms_inv(x):
    return lax.rsqrt(jnp.mean(x * x, axis=-1, keepdims=True) + EPS)


class Links:
    def __init__(self, mesh):
        self.nh = mesh.shape["head"]
        self.nq = mesh.shape["seq"]
        self.nz = self.nq // 2
        self.turns = tuple(range(self.nh - 1, 0, -1))

    def place(self):
        self.h = lax.axis_index("head")
        self.s = lax.axis_index("seq")
        self.c = self.s % 2
        self.z = self.s // 2

    def partner(self, x, r):
        return lax.ppermute(x, "head", [(i, i ^ r) for i in range(self.nh)])

    def sibling(self, x):
        return lax.ppermute(x, "seq", [(i, i ^ 1) for i in range(self.nq)])

    def along(self, x, k):
        n = self.nz
        return lax.ppermute(x, "seq", [(2 * p + c, 2 * ((p + k) % n) + c) for p in range(n) for c in range(2)])

    def head_sum(self, parts, hold=()):
        got = [after(self.partner(parts[r], r), *hold) for r in self.turns]
        total = parts[0]
        for x in got:
            total = total + x.astype(f32)
        return total

    def head_pieces(self, x):
        got = {r: self.partner(x, r) for r in self.turns}
        return [x] + [got[r] for r in range(1, self.nh)]

    def line_sum(self, parts):
        got = [self.along(parts[k], k) for k in self.line_order()]
        total = parts[0]
        for x in got:
            total = total + x.astype(f32)
        return total

    def line_order(self):
        half = self.nz // 2
        return sorted(range(1, self.nz), key=lambda k: abs(k - half))

    def ring(self, x):
        out = []
        for _ in range(1, self.nz):
            x = self.along(x, 1)
            out.append(x)
        return out

    def ring_sum(self, parts):
        total = parts[self.nz - 1]
        for k in range(self.nz - 2, -1, -1):
            total = parts[k] + self.along(total, 1).astype(f32)
            total = total if k == 0 else total.astype(bf)
        return total

    def relative(self, x):
        n = x.shape[0] // self.nh
        return jnp.concatenate(
            [lax.dynamic_slice_in_dim(x, (self.h ^ r) * n, n, axis=0) for r in range(self.nh)], axis=0
        )


def per_device(
    links,
    inputs,
    lengths,
    first_gain,
    query_weight,
    key_weight,
    value_weight,
    gate_weight,
    rate_weight,
    inner_weight,
    inner_offset,
    inner_gain,
    inner_shift,
    post_gain,
    post_shift,
    out_weight,
    second_gain,
    feed_gate,
    feed_up,
    feed_down,
    out_grad,
):
    links.place()
    nh, nz, nq = links.nh, links.nz, links.nq
    spot = jnp.arange(4 + nz, dtype=jnp.int32)
    cols = 2 * lax.rem(links.z + spot + (nz - 3), nz) + links.c
    cols = jnp.where(spot == 3 + nz, 2 * links.z + 1 - links.c, cols)
    where = jnp.where(spot == 0, links.h, jnp.where(spot == 1, lengths[0, 0], jnp.where(spot == 2, lengths[0, 1], cols)))
    n = inputs.shape[0] // nh
    per = n // MB
    wide = inputs.shape[1] // nq
    heads, width = inner_offset.shape
    C = heads * width
    pg, ps = post_gain[None], post_shift[None]
    rate_turned = rate_weight.T
    feed_gate, feed_up = feed_gate.T, feed_up.T

    grad_rel = links.relative(out_grad)
    straight = [0] + list(range(3, nh))
    grad_ring = [links.along(jnp.concatenate([grad_rel[:n], grad_rel[3 * n :]], axis=0), 1)]
    normed_one, query, key, value, gate, rate_logit = project(
        nh, where, inputs, first_gain[None], (query_weight, key_weight, value_weight, gate_weight), rate_turned
    )
    mixed, slope, zt, rt, wt, mt = mixer_fwd(
        where, per, query, key, value, gate, rate_logit, inner_weight, inner_offset, inner_gain, inner_shift, pg, ps
    )
    own_source = lax.dynamic_slice_in_dim(inputs, links.h * n, n, axis=0).astype(f32)
    own_upstream = grad_rel[:n].astype(f32)

    mixed = after(mixed, grad_ring[0])
    for k in range(2, nz):
        grad_ring.append(links.along(grad_ring[-1], 1))
    out_parts = split_product(nh, [(mixed, out_weight, False, 0)], "out_product", 4)
    hidden = own_source + links.head_sum(out_parts)
    r2 = rms_inv(hidden)
    two_own = after((second_gain * (hidden * r2)).astype(bf), grad_ring[1])
    twos = links.head_pieces(two_own)
    plan = tuple(((r, 0), (nh, r * n)) for r in range(nh))
    twos[0] = after(twos[0], grad_ring[-1])
    grad_across = after(jnp.concatenate([x[:n] for x in grad_ring], axis=0), *twos[1:])
    grad_across = [links.partner(grad_across, r) for r in (1, 2)]
    normed_two, grad_own, activ, gate_grad, up_grad = feed(
        n, plan, [*twos, grad_rel], feed_gate, feed_up, feed_down, "feed_own", 4
    )
    two_ring = [links.along(jnp.concatenate([twos[r] for r in straight], axis=0), 1)]
    for k in range(2, nz):
        two_ring.append(links.along(two_ring[-1], 1))
    back_parts = split_product(
        nh, [(gate_grad, feed_gate, False, 0), (up_grad, feed_up, False, 0)], "feed_back", 9
    )
    back_parts = [back_parts[0]] + [after(x, two_ring[0], *grad_across) for x in back_parts[1:]]
    down_parts = list(split_product(nh, [(after(activ, back_parts[0]), feed_down, False, 0)], "feed_down", 1))
    two = links.head_sum(back_parts, (down_parts[0], two_ring[1]))
    u = two * second_gain
    hidden_grad = own_upstream + r2 * u - hidden * (r2 * r2 * r2) * jnp.mean(u * hidden, axis=-1, keepdims=True)
    second_part = jnp.sum(two * hidden * r2, axis=0)
    pieces = links.head_pieces(add_rows(hidden_grad.astype(bf), second_part))
    second_part = second_part + sum(last_rows(x) for x in pieces[1:])
    pieces[0] = after(pieces[0], two_ring[-1])
    branch_grad, mixed_grad, dg = branch_back(pieces, n, out_weight, slope)
    across = jnp.concatenate([x[:n] for x in two_ring], axis=0)
    across = [links.partner(across, r) for r in (1, 2)]

    one_sib = links.sibling(normed_one)
    groups = [
        [(normed_one, dg), (one_sib, links.sibling(dg))],
        [(branch_grad, mixed), (links.sibling(branch_grad), links.sibling(mixed))],
    ]
    pair = block_products(where, 1, groups, [f32] + [bf] * (nz - 1), wide, "gate_out_blocks", 8)
    order = links.line_order()
    pair_got = {k: links.along(pair[k], k) for k in order[:2]}

    dqkv, drate, dw0, db0, dgain, dshift, dpg, dps = mixer_bwd(
        where, per, query, key, value, gate, rate_logit, after(mixed_grad, pair[0]),
        zt, rt, wt, mt, inner_gain, inner_shift, pg, ps
    )
    dqkv = after(dqkv, *pair_got.values(), *across)
    drate_low = drate.astype(bf)
    dqkv_sib = links.sibling(dqkv)
    back_parts = split_product(
        nh,
        [
            (dqkv, query_weight, True, 0),
            (dqkv, key_weight, True, 1),
            (dqkv, value_weight, True, 2),
            (dg, gate_weight, True, 0),
            (drate_low, rate_turned, False, 0),
        ],
        "input_back",
        8,
        extra=down_parts[1:],
    )
    groups = [[(normed_one, after(dqkv, back_parts[0])), (one_sib, dqkv_sib)]]
    trio = block_products(where, 1, groups, [f32] + [bf] * (nz - 1), wide, "qkv_blocks", 8)
    trio_step = links.along(trio[-1], 1)

    steps = nz - 1
    plan = tuple(
        ((k, i * n), (steps + k, i * n)) for k in range(steps) for i in range(len(straight))
    )
    two_ring[0] = after(two_ring[0], trio[0])
    first = feed(n, plan, [*two_ring, *grad_ring], feed_gate, feed_up, feed_down, "feed_straight", 20)

    send = (trio[nz - 2].astype(f32) + after(trio_step, first[2]).astype(f32)).astype(bf)
    sums = links.head_sum([jnp.concatenate([back_parts[0], down_parts[0]], axis=0)] + list(back_parts[1:]), (send,))
    one, output = sums[:n], hidden + sums[n:]
    r1 = rms_inv(own_source)
    w = one * first_gain
    input_grad = hidden_grad + r1 * w - own_source * (r1 * r1 * r1) * jnp.mean(w * own_source, axis=-1, keepdims=True)
    input_low = input_grad.astype(bf)
    first_part = jnp.sum(one * own_source * r1, axis=0)
    pieces = links.head_pieces(add_rows(jnp.concatenate([input_low, output.astype(bf)], axis=0), first_part))
    plan = tuple(((i, k * n), (2 + i, k * n)) for k in range(steps) for i in range(2))
    across[0] = after(across[0], pieces[0])
    second = [*feed(n, plan, [*across, *grad_across], feed_gate, feed_up, feed_down, "feed_across", 20)]

    hold = second[2]
    for k in range(nz - 3, -1, -1):
        got = after(links.along(send, 1), hold)
        send = trio[k].astype(f32) + got.astype(f32)
        if k:
            send = send.astype(bf)
            if k == nz - 3:
                hold = send
                for i in (2, 3, 4):
                    second[i] = after(second[i], send)
                pieces[1:] = [after(x, send) for x in pieces[1:]]
    grad_qkv = send
    for k in order[2:]:
        pair_got[k] = links.along(after(pair[k], hold), k)
    pair = pair[0] + sum(x.astype(f32) for x in pair_got.values())
    first_part = first_part + sum(last_rows(x) for x in pieces[1:])
    rate_part = lax.dot_general(
        after(normed_one, hold), drate_low, (((0,), (0,)), ((), ())), preferred_element_type=f32
    )

    input_grad, output = natural(where, pieces, n, 2)
    tokens = ((normed_two, grad_own, activ, gate_grad, up_grad), first, second)
    feed_grads = []
    for x, m, name in ((0, 3, "feed_gate_blocks"), (0, 4, "feed_up_blocks"), (1, 2, "feed_down_blocks")):
        terms = [(t[x], t[m]) for t in tokens]
        if feed_grads:
            terms[0] = (after(terms[0][0], keep, *([pair] if len(feed_grads) == 2 else [])), terms[0][1])
        keep, give = block_products(
            where, nz, [terms], [f32, bf], wide, name, 8, turned=True
        )
        feed_grads.append(keep + links.sibling(give).astype(f32))

    def rows_of(x):
        return x.reshape(nq, -1)

    def heads_of(x):
        return x.reshape((heads, nq, -1)).transpose(1, 0, 2).reshape(nq, -1)

    small = [rows_of(first_part), rows_of(second_part), rows_of(rate_part), heads_of(dw0)]
    small += [heads_of(x) for x in (db0, dgain, dshift)] + [rows_of(dpg), rows_of(dps)]
    sizes = [x.shape[1] for x in small]
    small = jnp.concatenate(small, axis=1).reshape(nz, 2, -1)
    keep = lax.dynamic_index_in_dim(small, links.c, 1, keepdims=False)
    give = lax.dynamic_index_in_dim(small, 1 - links.c, 1, keepdims=False)
    small = keep + links.sibling(give)
    small = links.line_sum([lax.dynamic_index_in_dim(small, lax.rem(links.z + k, nz), 0, keepdims=False) for k in range(nz)])
    ends = [sum(sizes[: i + 1]) for i in range(len(sizes))]
    small = [small[e - n : e] for e, n in zip(ends, sizes)]
    part = width // nq
    return (
        output,
        input_grad,
        small[0],
        grad_qkv[:, :C],
        grad_qkv[:, C : 2 * C],
        grad_qkv[:, 2 * C :],
        pair[:, :C],
        small[2].reshape(-1, heads),
        small[3].reshape(heads, part, width),
        small[4].reshape(heads, part),
        small[5].reshape(heads, part),
        small[6].reshape(heads, part),
        small[7],
        small[8],
        pair[:, C:].T,
        small[1],
        feed_grads[0].T,
        feed_grads[1].T,
        feed_grads[2],
    )


def solution(mesh):
    in_specs = (
        P("seq", None),
        P("seq", None),
        P(),
        P(None, "head"),
        P(None, "head"),
        P(None, "head"),
        P(None, "head"),
        P(None, "head"),
        P("head", None, None),
        P("head", None),
        P("head", None),
        P("head", None),
        P("head"),
        P("head"),
        P("head", None),
        P(),
        P(None, "head"),
        P(None, "head"),
        P("head", None),
        P("seq", None),
    )
    out_specs = (
        P("seq", None),
        P("seq", None),
        P("seq"),
        P("seq", "head"),
        P("seq", "head"),
        P("seq", "head"),
        P("seq", "head"),
        P("seq", "head"),
        P("head", "seq", None),
        P("head", "seq"),
        P("head", "seq"),
        P("head", "seq"),
        P(("head", "seq")),
        P(("head", "seq")),
        P("head", "seq"),
        P("seq"),
        P("seq", "head"),
        P("seq", "head"),
        P("head", "seq"),
    )
    return jax.shard_map(
        functools.partial(per_device, Links(mesh)), mesh=mesh, in_specs=in_specs, out_specs=out_specs, check_vma=False
    )
```

```python
import functools

import jax
import jax.numpy as jnp
from jax import lax
from jax.experimental import pallas as pl
from jax.experimental.pallas import tpu as pltpu
from jax.sharding import PartitionSpec as P

MB=16; EPS=1e-6
bf=jnp.bfloat16; f32=jnp.float32

def dot_nn(a,b): return lax.dot_general(a,b,(((1,),(0,)),((),())),preferred_element_type=f32)
def dot_nt(a,b): return lax.dot_general(a,b,(((1,),(1,)),((),())),preferred_element_type=f32)
def dot_tn(a,b): return lax.dot_general(a,b,(((0,),(0,)),((),())),preferred_element_type=f32)

def mean0(x): return jnp.mean(x,axis=0,keepdims=True)

def norm_parts(x):
    c=x-mean0(x)
    inv=lax.rsqrt(mean0(c*c)+EPS)
    return c*inv,inv

def norm_back(dy,n,inv):
    return inv*(dy-mean0(dy)-n*mean0(dy*n))

def split2(x):
    hi=x.astype(bf)
    return jnp.concatenate([hi,(x-hi.astype(f32)).astype(bf)],axis=0)

def two_rows(x):
    h=x.shape[0]//2
    return x[:h]+x[h:]

def stack_heads(rows,F):
    H=rows.shape[1]//F
    r=rows.astype(f32)
    return jnp.concatenate([r[:,h*F:(h+1)*F] for h in range(H)],axis=0).T

GC=0.7978845608028654; GA=0.044715
def gelu_parts(x):
    u=GC*(x+GA*x*x*x)
    t=jnp.tanh(u)
    val=0.5*x*(1.0+t)
    der=0.5*(1.0+t)+0.5*x*(1.0-t*t)*GC*(1.0+3.0*GA*x*x)
    return val,der

def plan_blocks(where):
    n0=(where[1]+MB-1)//MB; n1=(where[2]+MB-1)//MB
    return (n0,n1),(0,n0)

def row_of(where,b,per):
    return pl.multiple_of(((lax.div(b,per)^where[0])*per+lax.rem(b,per))*MB,MB)

def lane_iota(shape,dim): return lax.broadcasted_iota(jnp.int32,shape,dim)

def valid_row(where,offs,blk,L):
    pos=blk*MB+lane_iota((1,L),1)%MB
    a=(pos>=offs[0]*MB)&(pos<offs[0]*MB+where[1])
    b=(pos>=offs[1]*MB)&(pos<offs[1]*MB+where[2])
    return a|b

def fill_bd(dst,blk,rows,row0,F):
    H=rows.shape[1]//F
    for h in range(H):
        dst[blk,row0+h*MB:row0+(h+1)*MB,h*F:(h+1)*F]=rows[:,h*F:(h+1)*F]

def fill_turned(dst,blk,kt,qt):
    F,L=kt.shape
    both=jnp.concatenate([kt,qt],axis=1).astype(bf)
    lane=lane_iota((F,2*L),1)%L//MB
    for h in range(L//MB):
        dst[blk,h*F:(h+1)*F,:]=jnp.where(lane==h,both,jnp.zeros_like(both))

def same_head(L):
    return lane_iota((L,L),0)//MB==lane_iota((L,L),1)//MB

def head_lanes(H,L):
    return (lane_iota((H,L),0)==lane_iota((H,L),1)//MB).astype(f32)

HIGH=lax.Precision.HIGHEST
def head_rows(ref,F):
    return jnp.concatenate([ref[:,i:i+F] for i in range(0,ref.shape[1],F)],axis=0)
def spread(per_head,rep):
    return lax.dot_general(per_head,rep,(((0,),(0,)),((),())),precision=HIGH,preferred_element_type=f32)
def gather_heads(x,rep):
    return lax.dot_general(rep,x,(((1,),(1,)),((),())),precision=HIGH,preferred_element_type=f32)

def fwd_kernel(UN,PER,where,q_ref,k_ref,v_ref,g_ref,rlh_ref,w0_ref,b0_ref,gainh_ref,shifth_ref,pgh_ref,psh_ref,
               mixed_ref,slope_ref,zt_ref,rt_ref,wt_ref,mt_ref,
               kq,kqt,tt,rate,mtb,wst,bst,rl_ref,gain_ref,shift_ref,pg_ref,ps_ref):
    T,C=q_ref.shape; H,F=b0_ref.shape; L=H*MB; NB=T//MB
    rep=head_lanes(H,L)
    rl_ref[...]=lax.dot_general(rlh_ref[...],rep,(((1,),(0,)),((),())),precision=HIGH,preferred_element_type=f32)
    gain_ref[...]=spread(gainh_ref[...],rep); shift_ref[...]=spread(shifth_ref[...],rep)
    pg_ref[...]=spread(head_rows(pgh_ref,F),rep); ps_ref[...]=spread(head_rows(psh_ref,F),rep)
    counts,offs=plan_blocks(where)
    zero_kq=jnp.zeros((2*L,C),bf)
    onesbd=same_head(L).astype(f32).astype(bf)
    keep=same_head(L)&(lane_iota((L,L),0)<=lane_iota((L,L),1))
    pick=lane_iota((MB,L),0)==lane_iota((MB,L),1)%MB
    def clear(b,_):
        kq[b]=zero_kq
        return 0
    lax.fori_loop(0,NB+1,clear,0)
    kqt[NB]=jnp.zeros((C,2*L),bf)
    tt[NB]=jnp.zeros((F,L),f32); rate[NB]=jnp.zeros((1,L),f32); mtb[NB]=jnp.zeros((L,2*L),bf)
    def pre_one(b):
        r=row_of(where,b,PER)
        kn=k_ref[pl.ds(r,MB),:]; qn=q_ref[pl.ds(r,MB),:]; vn=v_ref[pl.ds(r,MB),:]
        fill_bd(kq,b,kn,0,F); fill_bd(kq,b,qn,L,F)
        kt=stack_heads(kn,F); qt=stack_heads(qn,F)
        tt[b]=stack_heads(vn,F)-kt
        fill_turned(kqt,b,kt,qt)
        ok=valid_row(where,offs,b,L)
        rl=jnp.sum(jnp.where(pick,rl_ref[pl.ds(r,MB),:],0.0),axis=0,keepdims=True)
        rate[b]=jnp.where(ok,jax.nn.sigmoid(rl)*(1.0/F),0.0)
        st=dot_nn(kq[b,0:L,:],kqt[b,:,L:2*L])
        m=jnp.where(keep,st+1.0,0.0).astype(bf)
        mt_ref[b]=m
        mtb[b,:,0:L]=m; mtb[b,:,L:2*L]=onesbd
    def pre(i,_):
        for u in range(UN): pre_one(i*UN+u)
        return 0
    lax.fori_loop(0,NB//UN,pre,0)
    def unused(b,_):
        rt_ref[b]=jnp.zeros((F,L),f32)
        zt_ref[b]=jnp.zeros((F,L),f32)
        wt_ref[b]=jnp.zeros((F,C),bf)
        return 0
    lax.fori_loop(counts[0]+counts[1],NB,unused,0)
    bias0=spread(b0_ref[...],rep)
    for h in range(H):
        wh=w0_ref[h].T
        for s in range(2): wst[s,:,h*F:(h+1)*F]=wh
    for s in range(2): bst[s]=bias0
    gain2=jnp.concatenate([gain_ref[...]]*2,axis=1); shift2=jnp.concatenate([shift_ref[...]]*2,axis=1)
    def step(i,_):
        bs=[jnp.where(i<counts[s],offs[s]+i,NB) for s in range(2)]
        w=[wst[s] for s in range(2)]; bias=[bst[s] for s in range(2)]
        w2=[split2(x) for x in w]
        zq=[two_rows(dot_nn(w2[s],kqt[bs[s]])) for s in range(2)]
        z=[zq[s][:,:L]+bias[s] for s in range(2)]
        for s in range(2):
            wt_ref[bs[s]]=w2[s][:F]; zt_ref[bs[s]]=z[s]
        zz=jnp.concatenate(z,axis=1)
        n,inv=norm_parts(zz)
        t2=jnp.concatenate([tt[b] for b in bs],axis=1)
        p=(n*gain2+shift2-t2)*gain2
        g=inv*(p-mean0(p)-n*mean0(p*n))
        g=g*jnp.concatenate([rate[b] for b in bs],axis=1)
        gr=[g[:,s*L:(s+1)*L].astype(bf) for s in range(2)]
        up=[dot_nn(gr[s],kq[bs[s],0:L,:]) for s in range(2)]
        for s in range(2): wst[s]=w[s]-up[s]
        ob=[dot_nn(gr[s],mtb[bs[s]]) for s in range(2)]
        for s in range(2):
            bst[s]=bias[s]-ob[s][:,L:]
            rt_ref[bs[s]]=zq[s][:,L:]+bias[s]-ob[s][:,:L]
        return 0
    lax.fori_loop(0,jnp.maximum(counts[0],counts[1]),step,0)
    def post_one(b):
        r=row_of(where,b,PER)
        qt=stack_heads(q_ref[pl.ds(r,MB),:],F); gt=stack_heads(g_ref[pl.ds(r,MB),:],F)
        nr,_=norm_parts(rt_ref[b])
        io=qt+nr*gain_ref[...]+shift_ref[...]
        ni,_=norm_parts(io)
        act,der=gelu_parts(gt)
        ok=valid_row(where,offs,b,L)
        lo=jnp.where(ok,ni*pg_ref[...]+ps_ref[...],0.0)
        m=(act*lo).T; sl=(der*lo).T
        for h in range(H):
            mixed_ref[pl.ds(r,MB),h*F:(h+1)*F]=m[h*MB:(h+1)*MB,:].astype(bf)
            slope_ref[pl.ds(r,MB),h*F:(h+1)*F]=sl[h*MB:(h+1)*MB,:].astype(bf)
    def post(i,_):
        for u in range(UN): post_one(i*UN+u)
        return 0
    lax.fori_loop(0,NB//UN,post,0)

def bwd_kernel(UN,PER,where,q_ref,k_ref,v_ref,g_ref,rlh_ref,dm_ref,zt_ref,rt_ref,wt_ref,mt_ref,gainh_ref,shifth_ref,pgh_ref,psh_ref,
               dqkv_ref,drlh_ref,dw0_ref,db0h_ref,dgainh_ref,dshifth_ref,dpgh_ref,dpsh_ref,
               kq,kqt,rate,ns,ps_,gs,xs,rs,ios,rows,zs,es,dws,wst,bst,rl_ref,gain_ref,shift_ref,pg_ref,ps_ref,
               dgain_ref,dshift_ref,dpg_ref,dps_ref,drl_ref):
    T,C=q_ref.shape; H,F=gainh_ref.shape; L=H*MB; NB=T//MB
    rep=head_lanes(H,L)
    rl_ref[...]=lax.dot_general(rlh_ref[...],rep,(((1,),(0,)),((),())),precision=HIGH,preferred_element_type=f32)
    gain_ref[...]=spread(gainh_ref[...],rep); shift_ref[...]=spread(shifth_ref[...],rep)
    pg_ref[...]=spread(head_rows(pgh_ref,F),rep); ps_ref[...]=spread(head_rows(psh_ref,F),rep)
    counts,offs=plan_blocks(where)
    zero_kq=jnp.zeros((2*L,C),bf)
    onesbd=same_head(L).astype(f32).astype(bf)
    keep=same_head(L)&(lane_iota((L,L),0)<=lane_iota((L,L),1))
    keep_t=same_head(L)&(lane_iota((L,L),1)<=lane_iota((L,L),0))
    pick=lane_iota((MB,L),0)==lane_iota((MB,L),1)%MB
    zfl=jnp.zeros((F,L),f32)
    def clear(b,_):
        kq[b]=zero_kq
        return 0
    lax.fori_loop(0,NB+1,clear,0)
    for ref in (ns,ps_,gs,xs,rs): ref[NB]=zfl
    kqt[NB]=jnp.zeros((C,2*L),bf)
    rate[NB]=jnp.zeros((1,L),f32); rows[NB]=jnp.zeros((8,L),f32)
    for ref in (dgain_ref,dshift_ref,dpg_ref,dps_ref): ref[...]=zfl
    def pre_one(b):
        r=row_of(where,b,PER)
        kn=k_ref[pl.ds(r,MB),:]; qn=q_ref[pl.ds(r,MB),:]
        fill_bd(kq,b,kn,0,F); fill_bd(kq,b,qn,L,F)
        kt=stack_heads(kn,F); qt=stack_heads(qn,F)
        t=stack_heads(v_ref[pl.ds(r,MB),:],F)-kt
        fill_turned(kqt,b,kt,kt)
        gt=stack_heads(g_ref[pl.ds(r,MB),:],F)
        dm=stack_heads(dm_ref[pl.ds(r,MB),:],F)
        ok=valid_row(where,offs,b,L)
        rl=jnp.sum(jnp.where(pick,rl_ref[pl.ds(r,MB),:],0.0),axis=0,keepdims=True)
        sg=jax.nn.sigmoid(rl)
        rt=jnp.where(ok,sg*(1.0/F),0.0)
        rate[b]=rt
        gain=gain_ref[...]; shift=shift_ref[...]
        n,inv=norm_parts(zt_ref[b])
        e=n*gain+shift-t
        p=e*gain
        mpn=mean0(p*n)
        g=inv*(p-mean0(p)-n*mpn)
        nr,invr=norm_parts(rt_ref[b])
        io=qt+nr*gain+shift
        ni,invi=norm_parts(io)
        act,_=gelu_parts(gt)
        dl=jnp.where(ok,dm*act,0.0)
        dio=norm_back(dl*pg_ref[...],ni,invi)
        dr=norm_back(dio*gain,nr,invr)
        drb=dr.astype(bf)
        ns[b]=n; ps_[b]=e; gs[b]=g; rs[b]=dr; ios[b]=dio
        xs[b]=dot_nt(drb,mt_ref[b])
        rows[b]=jnp.concatenate([inv,mpn,sg*(1.0-sg)*jnp.where(ok,1.0/F,0.0),jnp.zeros((5,L),f32)],axis=0)
        return dl,dl*ni,dio,dio*nr
    def pre(i,_):
        acc=None
        for u in range(UN):
            x=pre_one(i*UN+u)
            acc=x if acc is None else tuple(a+c for a,c in zip(acc,x))
        dps_ref[...]+=acc[0]; dpg_ref[...]+=acc[1]; dshift_ref[...]+=acc[2]; dgain_ref[...]+=acc[3]
        return 0
    lax.fori_loop(0,NB//UN,pre,0)
    def unused(b,_):
        zs[b]=zfl; es[b]=zfl; dws[b]=jnp.zeros((F,C),bf)
        return 0
    lax.fori_loop(counts[0]+counts[1],NB,unused,0)
    for s in range(2):
        wst[s]=jnp.zeros((F,C),f32); bst[s]=zfl
    steps=jnp.maximum(counts[0],counts[1])
    gain2=jnp.concatenate([gain_ref[...]]*2,axis=1)
    def step(j,_):
        i=steps-1-j
        bs=[jnp.where(i<counts[s],offs[s]+i,NB) for s in range(2)]
        both=lambda ref: jnp.concatenate([ref[b] for b in bs],axis=1)
        w=[wst[s] for s in range(2)]; bias=[bst[s] for s in range(2)]
        w2=[split2(x) for x in w]
        xx=[two_rows(dot_nn(w2[s],kqt[bs[s],:,0:L])) for s in range(2)]
        x=jnp.concatenate(xx,axis=1)+jnp.concatenate(bias,axis=1)+both(xs)
        for s in range(2): dws[bs[s]]=w2[s][:F]
        g=both(gs); n=both(ns); p=both(ps_)*gain2; row=both(rows)
        inv=row[0:1]; mpn=row[1:2]
        h=-both(rate)*x
        da=inv*h
        m1=mean0(da*n); m2=mean0(da); m3=mean0(h*g)
        dp=da-m2-n*m1
        de=dp*gain2
        dn=de*gain2-da*mpn-p*m1
        dz=inv*(dn-mean0(dn)-n*(mean0(dn*n)+m3))
        dr=[rs[b] for b in bs]
        dzs=[dz[:,:L],dz[:,L:]]
        up=[dot_nn(jnp.concatenate([dzs[s],dr[s]],axis=1).astype(bf),kq[bs[s]]) for s in range(2)]
        ub=[dot_nn((dzs[s]+dr[s]).astype(bf),onesbd) for s in range(2)]
        out=-jnp.sum(g*x,axis=0,keepdims=True)*row[2:3]
        for s in range(2):
            wst[s]=w[s]+up[s]; bst[s]=bias[s]+ub[s]
            zs[bs[s]]=dzs[s]; es[bs[s]]=dp[:,s*L:(s+1)*L]
            rows[bs[s],3:4,:]=out[:,s*L:(s+1)*L]
        return 0
    lax.fori_loop(0,steps,step,0)
    for h in range(H):
        dw0_ref[h]=(wst[0,:,h*F:(h+1)*F]+wst[1,:,h*F:(h+1)*F]).T
    db0h_ref[...]=gather_heads(bst[0]+bst[1],jnp.where(lane_iota((H,L),1)%MB==0,rep,0.0))
    def post_one(b):
        r=row_of(where,b,PER)
        dp=es[b]; row=rows[b]
        de=dp*gain_ref[...]
        dgain=dp*ps_[b]+de*ns[b]
        gr=(gs[b]*rate[b])
        drb=rs[b].astype(bf); grb=gr.astype(bf); dzb=zs[b].astype(bf)
        dst=jnp.where(keep,-dot_tn(grb,drb),0.0).astype(bf)
        dss=jnp.where(keep_t,-dot_tn(drb,grb),0.0).astype(bf)
        wt=wt_ref[b]
        kb=kq[b,0:L,:]; qb=kq[b,L:2*L,:]
        dqf=dot_tn(jnp.concatenate([drb,dst],axis=0),jnp.concatenate([wt,kb],axis=0))
        dkf=dot_tn(jnp.concatenate([dzb,(-gr).astype(bf),dss],axis=0),jnp.concatenate([wt,dws[b],qb],axis=0))
        det=de.T; dit=ios[b].T
        for h in range(H):
            rr=slice(h*MB,(h+1)*MB); cc=slice(h*F,(h+1)*F)
            dqkv_ref[pl.ds(r,MB),h*F:(h+1)*F]=(dqf[rr,cc]+dit[rr,:]).astype(bf)
            dqkv_ref[pl.ds(r,MB),C+h*F:C+(h+1)*F]=(dkf[rr,cc]+det[rr,:]).astype(bf)
            dqkv_ref[pl.ds(r,MB),2*C+h*F:2*C+(h+1)*F]=(-det[rr,:]).astype(bf)
        drl_ref[pl.ds(r,MB),:]=jnp.where(pick,row[3:4],0.0)
        return dgain,de
    def post(i,_):
        acc=None
        for u in range(UN):
            x=post_one(i*UN+u)
            acc=x if acc is None else tuple(a+c for a,c in zip(acc,x))
        dgain_ref[...]+=acc[0]; dshift_ref[...]+=acc[1]
        return 0
    lax.fori_loop(0,NB//UN,post,0)
    dgainh_ref[...]=gather_heads(dgain_ref[...],rep); dshifth_ref[...]=gather_heads(dshift_ref[...],rep)
    dpgh_ref[...]=gather_heads(dpg_ref[...],rep); dpsh_ref[...]=gather_heads(dps_ref[...],rep)
    drlh_ref[...]=lax.dot_general(drl_ref[...],rep,(((1,),(1,)),((),())),precision=HIGH,preferred_element_type=f32).astype(bf)

VM=pl.BlockSpec(memory_space=pltpu.VMEM); SM=pl.BlockSpec(memory_space=pltpu.SMEM)

def mixer_fwd(where,per,q,k,v,g,rl,w0,b0,gain,shift,pg,ps,UN=4):
    T,C=q.shape; H,F=b0.shape; L=H*MB; NB=T//MB
    S=jax.ShapeDtypeStruct
    fl=pltpu.VMEM((F,L),f32)
    return pl.pallas_call(functools.partial(fwd_kernel,UN,per),
        out_shape=[S((T,C),bf),S((T,C),bf),S((NB+1,F,L),f32),S((NB+1,F,L),f32),S((NB+1,F,C),bf),S((NB,L,L),bf)],
        in_specs=[SM]+[VM]*11,out_specs=[VM]*6,
        scratch_shapes=[pltpu.VMEM((NB+1,2*L,C),bf),pltpu.VMEM((NB+1,C,2*L),bf),pltpu.VMEM((NB+1,F,L),f32),pltpu.VMEM((NB+1,1,L),f32),
            pltpu.VMEM((NB+1,L,2*L),bf),pltpu.VMEM((2,F,C),f32),pltpu.VMEM((2,F,L),f32),pltpu.VMEM((T,L),f32),fl,fl,fl,fl],
        cost_estimate=cost(28),
        name='mixer_forward')(where,q,k,v,g,rl,w0,b0,gain,shift,pg,ps)

def mixer_bwd(where,per,q,k,v,g,rl,dm,zt,rt,wt,mt,gain,shift,pg,ps,UN=4):
    T,C=q.shape; H,F=gain.shape; L=H*MB; NB=T//MB
    S=jax.ShapeDtypeStruct
    fls=pltpu.VMEM((NB+1,F,L),f32); fl=pltpu.VMEM((F,L),f32)
    return pl.pallas_call(functools.partial(bwd_kernel,UN,per),
        out_shape=[S((T,3*C),bf),S((T,H),bf),S((H,F,F),f32)]+[S((H,F),f32)]*5,
        in_specs=[SM]+[VM]*14,out_specs=[VM]*8,
        scratch_shapes=[pltpu.VMEM((NB+1,2*L,C),bf),pltpu.VMEM((NB+1,C,2*L),bf),pltpu.VMEM((NB+1,1,L),f32)]+[fls]*6+[
            pltpu.VMEM((NB+1,8,L),f32),fls,fls,pltpu.VMEM((NB+1,F,C),bf),pltpu.VMEM((2,F,C),f32),pltpu.VMEM((2,F,L),f32),
            pltpu.VMEM((T,L),f32)]+[fl]*8+[pltpu.VMEM((T,L),f32)],
        cost_estimate=cost(33),
        name='mixer_backward')(where,q,k,v,g,rl,dm,zt,rt,wt,mt,gain,shift,pg,ps)


def cost(us):
    return pl.CostEstimate(flops=int(us * 1e9), bytes_accessed=int(us * 1e6), transcendentals=0)


def whole(x):
    return pl.BlockSpec(x.shape, lambda *_: (0,) * x.ndim)


SDS = jax.ShapeDtypeStruct


def project_kernel(nh, where, x_ref, gain_ref, wq, wk, wv, wg, wr, xn, q, k, v, g, rl):
    n = x_ref.shape[0] // nh

    @pl.when(pl.program_id(0) == 0)
    def _():
        for r in range(nh):
            x = x_ref[pl.ds(pl.multiple_of((where[0] ^ r) * n, MB), n), :].astype(f32)
            inv = lax.rsqrt(jnp.mean(x * x, axis=-1, keepdims=True) + EPS)
            xn[r * n : (r + 1) * n, :] = (gain_ref[...] * (x * inv)).astype(bf)
        rl[...] = dot_nt(xn[...], wr[...])

    for w, o in ((wq, q), (wk, k), (wv, v), (wg, g)):
        o[...] = dot_nn(xn[...], w[...]).astype(bf)


def project(nh, where, x, gain, weights, wr, tile=256):
    T, D = x.shape
    C, H = weights[0].shape[1], wr.shape[0]
    col = pl.BlockSpec((D, tile), lambda j: (0, j))
    out = pl.BlockSpec((T, tile), lambda j: (0, j))
    return pl.pallas_call(
        functools.partial(project_kernel, nh),
        grid=(C // tile,),
        in_specs=[SM, whole(x), whole(gain)] + [col] * 4 + [whole(wr)],
        out_specs=[pl.BlockSpec((T, D), lambda j: (0, 0))] + [out] * 4 + [pl.BlockSpec((T, H), lambda j: (0, 0))],
        out_shape=[SDS((T, D), bf)] + [SDS((T, C), bf)] * 4 + [SDS((T, H), f32)],
        cost_estimate=cost(8),
        name="project",
    )(where, x, gain, *weights, wr)


def split_kernel(kinds, more, *refs):
    n = len(kinds)
    acc = None
    for turned, a, b in zip(kinds, refs[:n], refs[n : 2 * n]):
        y = (dot_nt if turned else dot_nn)(a[...], b[...])
        acc = y if acc is None else acc + y
    extra, outs = refs[2 * n : 2 * n + more], refs[2 * n + more :]
    rows = outs[0].shape[0]
    for r, o in enumerate(outs):
        o[:rows, :] = acc[r * rows : (r + 1) * rows].astype(o.dtype)
        if r and more:
            o[rows:, :] = extra[r - 1][...]


def split_product(nh, terms, name, us, extra=(), tile=512):
    T = terms[0][0].shape[-2]
    D = terms[0][1].shape[0 if terms[0][2] else 1]
    a_specs, b_specs = [], []
    for a, b, turned, col in terms:
        depth = b.shape[1 if turned else 0]
        if a.ndim == 3:
            a_specs.append(pl.BlockSpec((None, T, depth), lambda j, col=col: (col, 0, 0)))
        else:
            a_specs.append(pl.BlockSpec((T, depth), lambda j, col=col: (0, col)))
        b_specs.append(
            pl.BlockSpec((tile, depth), lambda j: (j, 0)) if turned else pl.BlockSpec((depth, tile), lambda j: (0, j))
        )
    n = T // nh
    rows = [n] + [2 * n if extra else n] * (nh - 1)
    return pl.pallas_call(
        functools.partial(split_kernel, [t[2] for t in terms], len(extra)),
        grid=(D // tile,),
        in_specs=a_specs + b_specs + [pl.BlockSpec((n, tile), lambda j: (0, j))] * len(extra),
        out_specs=[pl.BlockSpec((m, tile), lambda j: (0, j)) for m in rows],
        out_shape=[SDS((m, D), bf if r else f32) for r, m in enumerate(rows)],
        cost_estimate=cost(us),
        name=name,
    )(*[t[0] for t in terms], *[t[1] for t in terms], *extra)


def lay(target, arrays, plan):
    rows = target.shape[0] // len(plan)
    for i, (a, at) in enumerate(plan):
        target[i * rows : (i + 1) * rows, :] = arrays[a][at : at + rows, :]


def rows_kernel(plan, *refs):
    lay(refs[-1], refs[:-1], plan)


def pick_rows(arrays, plan, n):
    D = arrays[0].shape[1]
    return pl.pallas_call(
        functools.partial(rows_kernel, plan),
        in_specs=[VM] * len(arrays),
        out_specs=VM,
        out_shape=SDS((n * len(plan), D), arrays[0].dtype),
        cost_estimate=cost(2),
        name="pick_rows",
    )(*arrays)


def chunks_of(T):
    return max(c for c in range(MB, 385, MB) if T % c == 0)


def feed_grad_kernel(plan, n, chunk, *refs):
    w, flat, back = refs[n:]

    @pl.when(pl.program_id(0) == 0)
    def _():
        lay(flat, refs[:n], plan)

    def body(i, _):
        rows = pl.ds(pl.multiple_of(i * chunk, MB), chunk)
        back[rows, :] = dot_nt(flat[rows, :], w[...]).astype(bf)
        return 0

    lax.fori_loop(0, flat.shape[0] // chunk, body, 0)


def feed_grad(n_rows, plan, arrays, w, name, us, tile=256):
    T = n_rows * len(plan)
    N, D = w.shape
    return pl.pallas_call(
        functools.partial(feed_grad_kernel, plan, len(arrays), chunks_of(T)),
        grid=(pl.cdiv(N, tile),),
        in_specs=[whole(x) for x in arrays] + [pl.BlockSpec((tile, D), lambda j: (j, 0))],
        out_specs=[pl.BlockSpec((T, D), lambda j: (0, 0)), pl.BlockSpec((T, tile), lambda j: (0, j))],
        out_shape=[SDS((T, D), bf), SDS((T, N), bf)],
        cost_estimate=cost(us),
        name=name,
    )(*arrays, w)


def feed_kernel(plan, n, chunk, *refs):
    wg, wu, back, flat, out = refs[n:]

    @pl.when(pl.program_id(0) == 0)
    def _():
        lay(flat, refs[:n], plan)

    def body(i, _):
        rows = pl.ds(pl.multiple_of(i * chunk, MB), chunk)
        gate = dot_nt(flat[rows, :], wg[...])
        up = dot_nt(flat[rows, :], wu[...])
        grad = back[rows, :].astype(f32)
        sig = jax.nn.sigmoid(gate)
        silu = gate * sig
        out[0, rows, :] = (grad * up * sig * (1.0 + gate * (1.0 - sig))).astype(bf)
        out[1, rows, :] = (grad * silu).astype(bf)
        out[2, rows, :] = (silu * up).astype(bf)
        return 0

    lax.fori_loop(0, flat.shape[0] // chunk, body, 0)


def feed(n_rows, plan, arrays, wg, wu, back, at, name, us, tile=256):
    T = n_rows * len(plan)
    N, D = wg.shape
    row = pl.BlockSpec((tile, D), lambda j: (j, 0))
    return pl.pallas_call(
        functools.partial(feed_kernel, plan, len(arrays), chunks_of(T)),
        grid=(pl.cdiv(N, tile),),
        in_specs=[whole(x) for x in arrays] + [row, row, pl.BlockSpec((T, tile), lambda j: (at, j))],
        out_specs=[pl.BlockSpec((T, D), lambda j: (0, 0)), pl.BlockSpec((3, T, tile), lambda j: (0, 0, j))],
        out_shape=[SDS((T, D), bf), SDS((3, T, N), bf)],
        cost_estimate=cost(us),
        name=name,
    )(*arrays, wg, wu, back)


def feed_blocks_kernel(n, *refs):
    xs, ns = refs[1 : 1 + n], refs[1 + n : 1 + 2 * n]
    give, keep = refs[1 + 2 * n :]
    y = None
    for x, m in zip(xs, ns):
        p = dot_tn(x[...], m[...])
        y = p if y is None else y + p
    y = y.T

    @pl.when(pl.program_id(1) == 0)
    def _():
        give[...] = y.astype(bf)

    @pl.when(pl.program_id(1) == 1)
    def _():
        keep[...] = y


def feed_blocks(where, nz, xs, ns, first, layers, wide, name, us):
    N = ns[0].shape[2]
    col = lambda b, where: where[3 + nz * (1 - b)]
    x_specs = [
        pl.BlockSpec((n.shape[1], wide), lambda w, b, where, at=at: (at, col(b, where))) for n, (_, at) in zip(ns, xs)
    ]
    n_specs = [pl.BlockSpec((None, n.shape[1], N), lambda w, b, where: (first + w, 0, 0)) for n in ns]
    out = pl.BlockSpec((None, N, wide), lambda w, b, where: (w, 0, 0))
    return pl.pallas_call(
        functools.partial(feed_blocks_kernel, len(ns)),
        grid_spec=pltpu.PrefetchScalarGridSpec(
            num_scalar_prefetch=1, grid=(layers, 2), in_specs=x_specs + n_specs, out_specs=[out, out]
        ),
        out_shape=[SDS((layers, N, wide), bf), SDS((layers, N, wide), f32)],
        cost_estimate=cost(us),
        name=name,
    )(where, *[x for x, _ in xs], *ns)


def branch_kernel(n, *refs):
    pieces = refs[:n]
    w, slope, flat, mg, dg = refs[n:]

    @pl.when(pl.program_id(0) == 0)
    def _():
        rows = flat.shape[0] // n
        for i, a in enumerate(pieces):
            flat[i * rows : (i + 1) * rows, :] = a[:rows, :]

    y = dot_nt(flat[...], w[...])
    mg[...] = y.astype(bf)
    dg[...] = (y * slope[...].astype(f32)).astype(bf)


def branch_back(pieces, n, w, slope, tile=256):
    T, C = slope.shape
    D = w.shape[1]
    out = pl.BlockSpec((T, tile), lambda j: (0, j))
    return pl.pallas_call(
        functools.partial(branch_kernel, len(pieces)),
        grid=(C // tile,),
        in_specs=[whole(x) for x in pieces] + [pl.BlockSpec((tile, D), lambda j: (j, 0)), out],
        out_specs=[pl.BlockSpec((T, D), lambda j: (0, 0)), out, out],
        out_shape=[SDS((T, D), bf), SDS((T, C), bf), SDS((T, C), bf)],
        cost_estimate=cost(4),
        name="branch_back",
    )(*pieces, w, slope)


def blocks_kernel(groups, turned, *refs):
    refs = refs[1:]
    n = sum(groups)
    xs, ns, outs = refs[:n], refs[n : 2 * n], refs[2 * n :]
    parts, at = [], 0
    for count in groups:
        y = None
        for i in range(at, at + count):
            p = dot_tn(xs[i][...], ns[i][...])
            y = p if y is None else y + p
        parts.append(y)
        at += count
    for k, o in enumerate(outs):
        @pl.when(pl.program_id(0) == k)
        def _(o=o):
            at = 0
            for y in parts:
                if turned:
                    o[at : at + y.shape[1], :] = y.T.astype(o.dtype)
                else:
                    o[:, at : at + y.shape[1]] = y.astype(o.dtype)
                at += y.shape[1]


def block_products(where, stride, groups, kinds, wide, name, us, turned=False):
    xs = [x for group in groups for x, _ in group]
    ns = [n for group in groups for _, n in group]
    N = sum(group[0][1].shape[1] for group in groups)
    x_specs = [pl.BlockSpec((x.shape[0], wide), lambda k, where: (0, where[3 + stride * k])) for x in xs]
    n_specs = [pl.BlockSpec(n.shape, lambda k, where: (0, 0)) for n in ns]
    shape = (N, wide) if turned else (wide, N)
    return pl.pallas_call(
        functools.partial(blocks_kernel, [len(group) for group in groups], turned),
        grid_spec=pltpu.PrefetchScalarGridSpec(
            num_scalar_prefetch=1,
            grid=(len(kinds),),
            in_specs=x_specs + n_specs,
            out_specs=[pl.BlockSpec(shape, lambda k, where: (0, 0))] * len(kinds),
        ),
        out_shape=[SDS(shape, kind) for kind in kinds],
        cost_estimate=cost(us),
        name=name,
    )(where, *xs, *ns)


def natural_kernel(nh, where, *refs):
    pieces, outs = refs[:nh], refs[nh:]
    n = outs[0].shape[0] // nh
    for r in range(nh):
        for i, out in enumerate(outs):
            out[pl.ds(pl.multiple_of((where[0] ^ r) * n, MB), n), :] = pieces[r][i * n : (i + 1) * n, :]


def natural(where, pieces, n, count):
    nh = len(pieces)
    D = pieces[0].shape[1]
    return pl.pallas_call(
        functools.partial(natural_kernel, nh),
        in_specs=[SM] + [VM] * nh,
        out_specs=[VM] * count,
        out_shape=[SDS((n * nh, D), pieces[0].dtype)] * count,
        cost_estimate=cost(0.2),
        name="natural",
    )(where, *pieces)


def add_rows(x, row):
    high = row.astype(bf)
    low = (row - high.astype(f32)).astype(bf)
    rest = jnp.zeros((MB - 2, row.shape[0]), bf)
    return jnp.concatenate([x, high[None], low[None], rest], axis=0)


def last_rows(x):
    return x[-MB].astype(f32) + x[1 - MB].astype(f32)


def after(x, *others):
    return lax.optimization_barrier((x, others))[0]


def rms_inv(x):
    return lax.rsqrt(jnp.mean(x * x, axis=-1, keepdims=True) + EPS)


class Links:
    def __init__(self, mesh):
        self.nh = mesh.shape["head"]
        self.nq = mesh.shape["seq"]
        self.nz = self.nq // 2
        self.turns = tuple(range(self.nh - 1, 0, -1))

    def place(self):
        self.h = lax.axis_index("head")
        self.s = lax.axis_index("seq")
        self.c = self.s % 2
        self.z = self.s // 2

    def partner(self, x, r):
        return lax.ppermute(x, "head", [(i, i ^ r) for i in range(self.nh)])

    def sibling(self, x):
        return lax.ppermute(x, "seq", [(i, i ^ 1) for i in range(self.nq)])

    def along(self, x, k):
        n = self.nz
        return lax.ppermute(x, "seq", [(2 * p + c, 2 * ((p + k) % n) + c) for p in range(n) for c in range(2)])

    def head_sum(self, parts, hold=()):
        got = [after(self.partner(parts[r], r), *hold) for r in self.turns]
        total = parts[0]
        for x in got:
            total = total + x.astype(f32)
        return total

    def head_pieces(self, x):
        got = {r: self.partner(x, r) for r in self.turns}
        return [x] + [got[r] for r in range(1, self.nh)]

    def line_sum(self, parts):
        got = [self.along(parts[k], k) for k in self.line_order()]
        total = parts[0]
        for x in got:
            total = total + x.astype(f32)
        return total

    def line_order(self):
        half = self.nz // 2
        return sorted(range(1, self.nz), key=lambda k: abs(k - half))

    def ring(self, x):
        out = []
        for _ in range(1, self.nz):
            x = self.along(x, 1)
            out.append(x)
        return out

    def ring_sum(self, parts):
        total = parts[self.nz - 1]
        for k in range(self.nz - 2, -1, -1):
            total = parts[k] + self.along(total, 1).astype(f32)
            total = total if k == 0 else total.astype(bf)
        return total

    def relative(self, x):
        n = x.shape[0] // self.nh
        return jnp.concatenate(
            [lax.dynamic_slice_in_dim(x, (self.h ^ r) * n, n, axis=0) for r in range(self.nh)], axis=0
        )


def per_device(
    links,
    inputs,
    lengths,
    first_gain,
    query_weight,
    key_weight,
    value_weight,
    gate_weight,
    rate_weight,
    inner_weight,
    inner_offset,
    inner_gain,
    inner_shift,
    post_gain,
    post_shift,
    out_weight,
    second_gain,
    feed_gate,
    feed_up,
    feed_down,
    out_grad,
):
    links.place()
    nh, nz, nq = links.nh, links.nz, links.nq
    spot = jnp.arange(4 + nz, dtype=jnp.int32)
    cols = 2 * lax.rem(links.z + spot + (nz - 3), nz) + links.c
    cols = jnp.where(spot == 3 + nz, 2 * links.z + 1 - links.c, cols)
    where = jnp.where(spot == 0, links.h, jnp.where(spot == 1, lengths[0, 0], jnp.where(spot == 2, lengths[0, 1], cols)))
    n = inputs.shape[0] // nh
    per = n // MB
    wide = inputs.shape[1] // nq
    heads, width = inner_offset.shape
    C = heads * width
    pg, ps = post_gain[None], post_shift[None]
    rate_turned = rate_weight.T
    feed_gate, feed_up = feed_gate.T, feed_up.T

    grad_rel = links.relative(out_grad)
    straight = [0] + list(range(3, nh))
    grad_ring = [links.along(jnp.concatenate([grad_rel[:n], grad_rel[3 * n :]], axis=0), 1)]
    normed_one, query, key, value, gate, rate_logit = project(
        nh, where, inputs, first_gain[None], (query_weight, key_weight, value_weight, gate_weight), rate_turned
    )
    mixed, slope, zt, rt, wt, mt = mixer_fwd(
        where, per, query, key, value, gate, rate_logit, inner_weight, inner_offset, inner_gain, inner_shift, pg, ps
    )
    own_source = lax.dynamic_slice_in_dim(inputs, links.h * n, n, axis=0).astype(f32)
    own_upstream = grad_rel[:n].astype(f32)

    mixed = after(mixed, grad_ring[0])
    for k in range(2, nz):
        grad_ring.append(links.along(grad_ring[-1], 1))
    out_parts = split_product(nh, [(mixed, out_weight, False, 0)], "out_product", 4, tile=1024)
    plan = tuple((0, r * n) for r in range(nh))
    grad_own, back_own = feed_grad(n, plan, [after(grad_rel, out_parts[0])], feed_down, "feed_grad_own", 1)
    hidden = own_source + links.head_sum(out_parts, (back_own,))
    r2 = rms_inv(hidden)
    two_own = after((second_gain * (hidden * r2)).astype(bf), grad_ring[1])
    twos = links.head_pieces(two_own)
    plan = tuple((r, 0) for r in range(nh))
    twos[0] = after(twos[0], grad_ring[-1])
    firsts = tuple((k, 0) for k in range(nz - 1))
    grad_across = pick_rows([after(grad_ring[0], *twos[1:]), *grad_ring[1:]], firsts, n)
    grad_across = [links.partner(grad_across, r) for r in (1, 2)]
    normed_two, feed_own = feed(n, plan, twos, feed_gate, feed_up, back_own, 0, "feed_own", 4)
    two_ring = [links.along(after(jnp.concatenate([twos[r] for r in straight], axis=0), *twos[1:]), 1)]
    back_parts = split_product(
        nh, [(feed_own, feed_gate, False, 0), (feed_own, feed_up, False, 1)], "feed_back", 9
    )
    two_ring[0] = after(two_ring[0], back_parts[0])
    for k in range(2, nz):
        two_ring.append(links.along(two_ring[-1], 1))
    back_parts = [back_parts[0]] + [after(x, two_ring[0], *grad_across) for x in back_parts[1:]]
    down_parts = list(split_product(nh, [(after(feed_own, back_parts[0]), feed_down, False, 2)], "feed_down", 1, tile=1024))
    two = links.head_sum(back_parts, (down_parts[0], two_ring[1]))
    u = two * second_gain
    hidden_grad = own_upstream + r2 * u - hidden * (r2 * r2 * r2) * jnp.mean(u * hidden, axis=-1, keepdims=True)
    second_part = jnp.sum(two * hidden * r2, axis=0)
    pieces = links.head_pieces(add_rows(hidden_grad.astype(bf), second_part))
    steps = nz - 1
    straight_plan = tuple((k, i * n) for k in range(steps) for i in range(len(straight)))
    across_plan = tuple((i, k * n) for k in range(steps) for i in range(2))
    plan = straight_plan + tuple((steps + i, at) for i, at in across_plan)
    held = [after(grad_ring[0], pieces[0]), *grad_ring[1:], *grad_across]
    grad_others, back_others = feed_grad(n, plan, held, feed_down, "feed_grad_others", 1)
    pieces[1:] = [after(x, back_others) for x in pieces[1:]]
    second_part = (second_part, pieces[1:])
    pieces[0] = after(pieces[0], two_ring[-1])
    branch_grad, mixed_grad, dg = branch_back(pieces, n, out_weight, slope)
    across = pick_rows(two_ring, firsts, n)
    across = [links.partner(across, r) for r in (1, 2)]

    one_sib = links.sibling(normed_one)
    groups = [
        [(normed_one, dg), (one_sib, links.sibling(dg))],
        [(branch_grad, mixed), (links.sibling(branch_grad), links.sibling(mixed))],
    ]
    pair = block_products(where, 1, groups, [f32] + [bf] * (nz - 1), wide, "gate_out_blocks", 8)
    order = links.line_order()
    pair_got = {order[0]: links.along(pair[order[0]], order[0])}

    dqkv, drate, dw0, db0, dgain, dshift, dpg, dps = mixer_bwd(
        where, per, query, key, value, gate, rate_logit, after(mixed_grad, pair[0]),
        zt, rt, wt, mt, inner_gain, inner_shift, pg, ps
    )
    dqkv = after(dqkv, *pair_got.values(), *across)
    pair_got[1] = links.along(after(pair[1], dqkv), 1)
    drate_low = drate
    dqkv_sib = links.sibling(dqkv)
    back_parts = split_product(
        nh,
        [
            (dqkv, query_weight, True, 0),
            (dqkv, key_weight, True, 1),
            (dqkv, value_weight, True, 2),
            (dg, gate_weight, True, 0),
            (drate_low, rate_turned, False, 0),
        ],
        "input_back",
        8,
        extra=down_parts[1:],
    )
    groups = [[(normed_one, after(dqkv, back_parts[0], pair_got[1])), (one_sib, dqkv_sib)]]
    trio = block_products(where, 1, groups, [f32] + [bf] * (nz - 1), wide, "qkv_blocks", 8)
    trio_step = links.along(trio[-1], 1)

    two_ring[0] = after(two_ring[0], trio[0])
    rows = len(straight_plan)
    first = feed(n, straight_plan, two_ring, feed_gate, feed_up, back_others, 0, "feed_straight", 15)

    def rows_of(x):
        return x.reshape(nq, -1)

    def heads_of(x):
        return x.reshape((heads, nq, -1)).transpose(1, 0, 2).reshape(nq, -1)

    second_part, held = second_part
    second_part = second_part + sum(last_rows(after(x, first[1])) for x in held)
    rate_part = lax.dot_general(
        after(normed_one, first[1]), drate_low, (((0,), (0,)), ((), ())), preferred_element_type=f32
    )
    dw0, db0, dgain, dshift, dpg, dps = after((dw0, db0, dgain, dshift, dpg, dps), first[1])
    small = [rows_of(second_part), rows_of(rate_part), heads_of(dw0)]
    small += [heads_of(x) for x in (db0, dgain, dshift)] + [rows_of(dpg), rows_of(dps)]
    sizes = [x.shape[1] for x in small]
    small = jnp.concatenate(small, axis=1)
    trio_step = after(trio_step, small)
    send = (trio[nz - 2].astype(f32) + after(trio_step, first[1]).astype(f32)).astype(bf)
    sums = links.head_sum([jnp.concatenate([back_parts[0], down_parts[0]], axis=0)] + list(back_parts[1:]), (send,))
    one, output = sums[:n], hidden + sums[n:]
    r1 = rms_inv(own_source)
    w = one * first_gain
    input_grad = hidden_grad + r1 * w - own_source * (r1 * r1 * r1) * jnp.mean(w * own_source, axis=-1, keepdims=True)
    input_low = input_grad.astype(bf)
    first_part = jnp.sum(one * own_source * r1, axis=0)
    pieces = links.head_pieces(add_rows(jnp.concatenate([input_low, output.astype(bf)], axis=0), first_part))
    across[0] = after(across[0], pieces[0])
    second = feed(n, across_plan, across, feed_gate, feed_up, back_others, 1, "feed_across", 15)

    hold = second[1]
    for k in range(nz - 3, -1, -1):
        got = links.along(send, 1)
        if k:
            send = (trio[k].astype(f32) + after(got, hold).astype(f32)).astype(bf)
            hold = send
    outs = [feed_own, first[1], after(second[1], send)]
    xs = [(normed_two, 0), (first[0], 0), (second[0], 0)]
    give, keep = feed_blocks(where, nz, xs, outs, 0, 2, wide, "feed_in_blocks", 12)
    grad_qkv = trio[0] + after(got, keep).astype(f32)
    got = links.sibling(give).astype(f32)
    grad_feed_gate, grad_feed_up = keep[0] + got[0], keep[1] + got[1]
    pieces[1:] = [after(x, grad_qkv) for x in pieces[1:]]
    first_part = first_part + sum(last_rows(x) for x in pieces[1:])
    sizes = [wide] + sizes
    small = jnp.concatenate([rows_of(first_part), small], axis=1).reshape(nz, 2, -1)
    keep = lax.dynamic_index_in_dim(small, links.c, 1, keepdims=False)
    give = lax.dynamic_index_in_dim(small, 1 - links.c, 1, keepdims=False)
    small = after(keep + links.sibling(give), grad_qkv)
    for k in order[1:]:
        if k != 1:
            pair_got[k] = links.along(after(pair[k], small), k)
    xs = [(after(grad_own, small), 0), (grad_others, 0), (grad_others, 1)]
    small = links.line_sum([lax.dynamic_index_in_dim(small, lax.rem(links.z + k, nz), 0, keepdims=False) for k in range(nz)])
    give, keep = feed_blocks(where, nz, xs, outs, 2, 1, wide, "feed_out_blocks", 0.5)
    grad_feed_down = keep[0] + links.sibling(give[0]).astype(f32)
    pair = pair[0] + sum(after(x, keep).astype(f32) for x in pair_got.values())
    pieces[0] = after(pieces[0], keep)
    input_grad, output = natural(where, pieces, n, 2)
    ends = [sum(sizes[: i + 1]) for i in range(len(sizes))]
    small = [small[e - n : e] for e, n in zip(ends, sizes)]
    part = width // nq
    return (
        output,
        input_grad,
        small[0],
        grad_qkv[:, :C],
        grad_qkv[:, C : 2 * C],
        grad_qkv[:, 2 * C :],
        pair[:, :C],
        small[2].reshape(-1, heads),
        small[3].reshape(heads, part, width),
        small[4].reshape(heads, part),
        small[5].reshape(heads, part),
        small[6].reshape(heads, part),
        small[7],
        small[8],
        pair[:, C:].T,
        small[1],
        grad_feed_gate.T,
        grad_feed_up.T,
        grad_feed_down,
    )


def solution(mesh):
    in_specs = (
        P("seq", None),
        P("seq", None),
        P(),
        P(None, "head"),
        P(None, "head"),
        P(None, "head"),
        P(None, "head"),
        P(None, "head"),
        P("head", None, None),
        P("head", None),
        P("head", None),
        P("head", None),
        P("head"),
        P("head"),
        P("head", None),
        P(),
        P(None, "head"),
        P(None, "head"),
        P("head", None),
        P("seq", None),
    )
    out_specs = (
        P("seq", None),
        P("seq", None),
        P("seq"),
        P("seq", "head"),
        P("seq", "head"),
        P("seq", "head"),
        P("seq", "head"),
        P("seq", "head"),
        P("head", "seq", None),
        P("head", "seq"),
        P("head", "seq"),
        P("head", "seq"),
        P(("head", "seq")),
        P(("head", "seq")),
        P("head", "seq"),
        P("seq"),
        P("seq", "head"),
        P("seq", "head"),
        P("head", "seq"),
    )
    return jax.shard_map(
        functools.partial(per_device, Links(mesh)), mesh=mesh, in_specs=in_specs, out_specs=out_specs, check_vma=False
    )
```

```python
import functools

import jax
import jax.numpy as jnp
from jax import lax
from jax.experimental import pallas as pl
from jax.experimental.pallas import tpu as pltpu
from jax.sharding import PartitionSpec as P

MB=16; EPS=1e-6
bf=jnp.bfloat16; f32=jnp.float32

def dot_nn(a,b): return lax.dot_general(a,b,(((1,),(0,)),((),())),preferred_element_type=f32)
def dot_nt(a,b): return lax.dot_general(a,b,(((1,),(1,)),((),())),preferred_element_type=f32)
def dot_tn(a,b): return lax.dot_general(a,b,(((0,),(0,)),((),())),preferred_element_type=f32)

def mean0(x): return jnp.mean(x,axis=0,keepdims=True)

def norm_parts(x):
    c=x-mean0(x)
    inv=lax.rsqrt(mean0(c*c)+EPS)
    return c*inv,inv

def norm_back(dy,n,inv):
    return inv*(dy-mean0(dy)-n*mean0(dy*n))

def split2(x):
    hi=x.astype(bf)
    return jnp.concatenate([hi,(x-hi.astype(f32)).astype(bf)],axis=0)

def two_rows(x):
    h=x.shape[0]//2
    return x[:h]+x[h:]

def stack_heads(rows,F):
    H=rows.shape[1]//F
    r=rows.astype(f32)
    return jnp.concatenate([r[:,h*F:(h+1)*F] for h in range(H)],axis=0).T

GC=0.7978845608028654; GA=0.044715
def gelu_parts(x):
    u=GC*(x+GA*x*x*x)
    t=jnp.tanh(u)
    val=0.5*x*(1.0+t)
    der=0.5*(1.0+t)+0.5*x*(1.0-t*t)*GC*(1.0+3.0*GA*x*x)
    return val,der

def plan_blocks(where):
    n0=(where[1]+MB-1)//MB; n1=(where[2]+MB-1)//MB
    return (n0,n1),(0,n0)

def row_of(where,b,per):
    return pl.multiple_of(((lax.div(b,per)^where[0])*per+lax.rem(b,per))*MB,MB)

def lane_iota(shape,dim): return lax.broadcasted_iota(jnp.int32,shape,dim)

def valid_row(where,offs,blk,L):
    pos=blk*MB+lane_iota((1,L),1)%MB
    a=(pos>=offs[0]*MB)&(pos<offs[0]*MB+where[1])
    b=(pos>=offs[1]*MB)&(pos<offs[1]*MB+where[2])
    return a|b

def fill_bd(dst,blk,rows,row0,F):
    H=rows.shape[1]//F
    for h in range(H):
        dst[blk,row0+h*MB:row0+(h+1)*MB,h*F:(h+1)*F]=rows[:,h*F:(h+1)*F]

def fill_turned(dst,blk,kt,qt):
    F,L=kt.shape
    both=jnp.concatenate([kt,qt],axis=1).astype(bf)
    lane=lane_iota((F,2*L),1)%L//MB
    for h in range(L//MB):
        dst[blk,h*F:(h+1)*F,:]=jnp.where(lane==h,both,jnp.zeros_like(both))

def same_head(L):
    return lane_iota((L,L),0)//MB==lane_iota((L,L),1)//MB

def head_lanes(H,L):
    return (lane_iota((H,L),0)==lane_iota((H,L),1)//MB).astype(f32)

HIGH=lax.Precision.HIGHEST
def head_rows(ref,F):
    return jnp.concatenate([ref[:,i:i+F] for i in range(0,ref.shape[1],F)],axis=0)
def spread(per_head,rep):
    return lax.dot_general(per_head,rep,(((0,),(0,)),((),())),precision=HIGH,preferred_element_type=f32)
def gather_heads(x,rep):
    return lax.dot_general(rep,x,(((1,),(1,)),((),())),precision=HIGH,preferred_element_type=f32)

def fwd_kernel(UN,PER,where,q_ref,k_ref,v_ref,g_ref,rlh_ref,w0_ref,b0_ref,gainh_ref,shifth_ref,pgh_ref,psh_ref,
               mixed_ref,slope_ref,zt_ref,rt_ref,wt_ref,mt_ref,
               kq,kqt,tt,rate,mtb,wst,bst,rl_ref,gain_ref,shift_ref,pg_ref,ps_ref):
    T,C=q_ref.shape; H,F=b0_ref.shape; L=H*MB; NB=T//MB
    rep=head_lanes(H,L)
    rl_ref[...]=lax.dot_general(rlh_ref[...],rep,(((1,),(0,)),((),())),precision=HIGH,preferred_element_type=f32)
    gain_ref[...]=spread(gainh_ref[...],rep); shift_ref[...]=spread(shifth_ref[...],rep)
    pg_ref[...]=spread(head_rows(pgh_ref,F),rep); ps_ref[...]=spread(head_rows(psh_ref,F),rep)
    counts,offs=plan_blocks(where)
    zero_kq=jnp.zeros((2*L,C),bf)
    onesbd=same_head(L).astype(f32).astype(bf)
    keep=same_head(L)&(lane_iota((L,L),0)<=lane_iota((L,L),1))
    pick=lane_iota((MB,L),0)==lane_iota((MB,L),1)%MB
    def clear(b,_):
        kq[b]=zero_kq
        return 0
    lax.fori_loop(0,NB+1,clear,0)
    kqt[NB]=jnp.zeros((C,2*L),bf)
    tt[NB]=jnp.zeros((F,L),f32); rate[NB]=jnp.zeros((1,L),f32); mtb[NB]=jnp.zeros((L,2*L),bf)
    def pre_one(b):
        r=row_of(where,b,PER)
        kn=k_ref[pl.ds(r,MB),:]; qn=q_ref[pl.ds(r,MB),:]; vn=v_ref[pl.ds(r,MB),:]
        fill_bd(kq,b,kn,0,F); fill_bd(kq,b,qn,L,F)
        kt=stack_heads(kn,F); qt=stack_heads(qn,F)
        tt[b]=stack_heads(vn,F)-kt
        fill_turned(kqt,b,kt,qt)
        ok=valid_row(where,offs,b,L)
        rl=jnp.sum(jnp.where(pick,rl_ref[pl.ds(r,MB),:],0.0),axis=0,keepdims=True)
        rate[b]=jnp.where(ok,jax.nn.sigmoid(rl)*(1.0/F),0.0)
        st=dot_nn(kq[b,0:L,:],kqt[b,:,L:2*L])
        m=jnp.where(keep,st+1.0,0.0).astype(bf)
        mt_ref[b]=m
        mtb[b,:,0:L]=m; mtb[b,:,L:2*L]=onesbd
    def pre(i,_):
        for u in range(UN): pre_one(i*UN+u)
        return 0
    lax.fori_loop(0,NB//UN,pre,0)
    def unused(b,_):
        rt_ref[b]=jnp.zeros((F,L),f32)
        zt_ref[b]=jnp.zeros((F,L),f32)
        wt_ref[b]=jnp.zeros((F,C),bf)
        return 0
    lax.fori_loop(counts[0]+counts[1],NB,unused,0)
    bias0=spread(b0_ref[...],rep)
    for h in range(H):
        wh=w0_ref[h].T
        for s in range(2): wst[s,:,h*F:(h+1)*F]=wh
    for s in range(2): bst[s]=bias0
    gain2=jnp.concatenate([gain_ref[...]]*2,axis=1); shift2=jnp.concatenate([shift_ref[...]]*2,axis=1)
    def step(i,_):
        bs=[jnp.where(i<counts[s],offs[s]+i,NB) for s in range(2)]
        w=[wst[s] for s in range(2)]; bias=[bst[s] for s in range(2)]
        w2=[split2(x) for x in w]
        zq=[two_rows(dot_nn(w2[s],kqt[bs[s]])) for s in range(2)]
        z=[zq[s][:,:L]+bias[s] for s in range(2)]
        for s in range(2):
            wt_ref[bs[s]]=w2[s][:F]; zt_ref[bs[s]]=z[s]
        zz=jnp.concatenate(z,axis=1)
        n,inv=norm_parts(zz)
        t2=jnp.concatenate([tt[b] for b in bs],axis=1)
        p=(n*gain2+shift2-t2)*gain2
        g=inv*(p-mean0(p)-n*mean0(p*n))
        g=g*jnp.concatenate([rate[b] for b in bs],axis=1)
        gr=[g[:,s*L:(s+1)*L].astype(bf) for s in range(2)]
        up=[dot_nn(gr[s],kq[bs[s],0:L,:]) for s in range(2)]
        for s in range(2): wst[s]=w[s]-up[s]
        ob=[dot_nn(gr[s],mtb[bs[s]]) for s in range(2)]
        for s in range(2):
            bst[s]=bias[s]-ob[s][:,L:]
            rt_ref[bs[s]]=zq[s][:,L:]+bias[s]-ob[s][:,:L]
        return 0
    lax.fori_loop(0,jnp.maximum(counts[0],counts[1]),step,0)
    def post_one(b):
        r=row_of(where,b,PER)
        qt=stack_heads(q_ref[pl.ds(r,MB),:],F); gt=stack_heads(g_ref[pl.ds(r,MB),:],F)
        nr,_=norm_parts(rt_ref[b])
        io=qt+nr*gain_ref[...]+shift_ref[...]
        ni,_=norm_parts(io)
        act,der=gelu_parts(gt)
        ok=valid_row(where,offs,b,L)
        lo=jnp.where(ok,ni*pg_ref[...]+ps_ref[...],0.0)
        m=(act*lo).T; sl=(der*lo).T
        for h in range(H):
            mixed_ref[pl.ds(r,MB),h*F:(h+1)*F]=m[h*MB:(h+1)*MB,:].astype(bf)
            slope_ref[pl.ds(r,MB),h*F:(h+1)*F]=sl[h*MB:(h+1)*MB,:].astype(bf)
    def post(i,_):
        for u in range(UN): post_one(i*UN+u)
        return 0
    lax.fori_loop(0,NB//UN,post,0)

def bwd_kernel(UN,PER,where,q_ref,k_ref,v_ref,g_ref,rlh_ref,dm_ref,zt_ref,rt_ref,wt_ref,mt_ref,gainh_ref,shifth_ref,pgh_ref,psh_ref,
               dqkv_ref,drlh_ref,dw0_ref,db0h_ref,dgainh_ref,dshifth_ref,dpgh_ref,dpsh_ref,
               kq,kqt,rate,ns,ps_,gs,xs,rs,ios,rows,zs,es,dws,wst,bst,rl_ref,gain_ref,shift_ref,pg_ref,ps_ref,
               dgain_ref,dshift_ref,dpg_ref,dps_ref,drl_ref):
    T,C=q_ref.shape; H,F=gainh_ref.shape; L=H*MB; NB=T//MB
    rep=head_lanes(H,L)
    rl_ref[...]=lax.dot_general(rlh_ref[...],rep,(((1,),(0,)),((),())),precision=HIGH,preferred_element_type=f32)
    gain_ref[...]=spread(gainh_ref[...],rep); shift_ref[...]=spread(shifth_ref[...],rep)
    pg_ref[...]=spread(head_rows(pgh_ref,F),rep); ps_ref[...]=spread(head_rows(psh_ref,F),rep)
    counts,offs=plan_blocks(where)
    zero_kq=jnp.zeros((2*L,C),bf)
    onesbd=same_head(L).astype(f32).astype(bf)
    keep=same_head(L)&(lane_iota((L,L),0)<=lane_iota((L,L),1))
    keep_t=same_head(L)&(lane_iota((L,L),1)<=lane_iota((L,L),0))
    pick=lane_iota((MB,L),0)==lane_iota((MB,L),1)%MB
    zfl=jnp.zeros((F,L),f32)
    def clear(b,_):
        kq[b]=zero_kq
        return 0
    lax.fori_loop(0,NB+1,clear,0)
    for ref in (ns,ps_,gs,xs,rs): ref[NB]=zfl
    kqt[NB]=jnp.zeros((C,2*L),bf)
    rate[NB]=jnp.zeros((1,L),f32); rows[NB]=jnp.zeros((8,L),f32)
    for ref in (dgain_ref,dshift_ref,dpg_ref,dps_ref): ref[...]=zfl
    def pre_one(b):
        r=row_of(where,b,PER)
        kn=k_ref[pl.ds(r,MB),:]; qn=q_ref[pl.ds(r,MB),:]
        fill_bd(kq,b,kn,0,F); fill_bd(kq,b,qn,L,F)
        kt=stack_heads(kn,F); qt=stack_heads(qn,F)
        t=stack_heads(v_ref[pl.ds(r,MB),:],F)-kt
        fill_turned(kqt,b,kt,kt)
        gt=stack_heads(g_ref[pl.ds(r,MB),:],F)
        dm=stack_heads(dm_ref[pl.ds(r,MB),:],F)
        ok=valid_row(where,offs,b,L)
        rl=jnp.sum(jnp.where(pick,rl_ref[pl.ds(r,MB),:],0.0),axis=0,keepdims=True)
        sg=jax.nn.sigmoid(rl)
        rt=jnp.where(ok,sg*(1.0/F),0.0)
        rate[b]=rt
        gain=gain_ref[...]; shift=shift_ref[...]
        n,inv=norm_parts(zt_ref[b])
        e=n*gain+shift-t
        p=e*gain
        mpn=mean0(p*n)
        g=inv*(p-mean0(p)-n*mpn)
        nr,invr=norm_parts(rt_ref[b])
        io=qt+nr*gain+shift
        ni,invi=norm_parts(io)
        act,_=gelu_parts(gt)
        dl=jnp.where(ok,dm*act,0.0)
        dio=norm_back(dl*pg_ref[...],ni,invi)
        dr=norm_back(dio*gain,nr,invr)
        drb=dr.astype(bf)
        ns[b]=n; ps_[b]=e; gs[b]=g; rs[b]=dr; ios[b]=dio
        xs[b]=dot_nt(drb,mt_ref[b])
        rows[b]=jnp.concatenate([inv,mpn,sg*(1.0-sg)*jnp.where(ok,1.0/F,0.0),jnp.zeros((5,L),f32)],axis=0)
        return dl,dl*ni,dio,dio*nr
    def pre(i,_):
        acc=None
        for u in range(UN):
            x=pre_one(i*UN+u)
            acc=x if acc is None else tuple(a+c for a,c in zip(acc,x))
        dps_ref[...]+=acc[0]; dpg_ref[...]+=acc[1]; dshift_ref[...]+=acc[2]; dgain_ref[...]+=acc[3]
        return 0
    lax.fori_loop(0,NB//UN,pre,0)
    def unused(b,_):
        zs[b]=zfl; es[b]=zfl; dws[b]=jnp.zeros((F,C),bf)
        return 0
    lax.fori_loop(counts[0]+counts[1],NB,unused,0)
    for s in range(2):
        wst[s]=jnp.zeros((F,C),f32); bst[s]=zfl
    steps=jnp.maximum(counts[0],counts[1])
    gain2=jnp.concatenate([gain_ref[...]]*2,axis=1)
    def step(j,_):
        i=steps-1-j
        bs=[jnp.where(i<counts[s],offs[s]+i,NB) for s in range(2)]
        both=lambda ref: jnp.concatenate([ref[b] for b in bs],axis=1)
        w=[wst[s] for s in range(2)]; bias=[bst[s] for s in range(2)]
        w2=[split2(x) for x in w]
        xx=[two_rows(dot_nn(w2[s],kqt[bs[s],:,0:L])) for s in range(2)]
        x=jnp.concatenate(xx,axis=1)+jnp.concatenate(bias,axis=1)+both(xs)
        for s in range(2): dws[bs[s]]=w2[s][:F]
        g=both(gs); n=both(ns); p=both(ps_)*gain2; row=both(rows)
        inv=row[0:1]; mpn=row[1:2]
        h=-both(rate)*x
        da=inv*h
        m1=mean0(da*n); m2=mean0(da); m3=mean0(h*g)
        dp=da-m2-n*m1
        de=dp*gain2
        dn=de*gain2-da*mpn-p*m1
        dz=inv*(dn-mean0(dn)-n*(mean0(dn*n)+m3))
        dr=[rs[b] for b in bs]
        dzs=[dz[:,:L],dz[:,L:]]
        up=[dot_nn(jnp.concatenate([dzs[s],dr[s]],axis=1).astype(bf),kq[bs[s]]) for s in range(2)]
        ub=[dot_nn((dzs[s]+dr[s]).astype(bf),onesbd) for s in range(2)]
        out=-jnp.sum(g*x,axis=0,keepdims=True)*row[2:3]
        for s in range(2):
            wst[s]=w[s]+up[s]; bst[s]=bias[s]+ub[s]
            zs[bs[s]]=dzs[s]; es[bs[s]]=dp[:,s*L:(s+1)*L]
            rows[bs[s],3:4,:]=out[:,s*L:(s+1)*L]
        return 0
    lax.fori_loop(0,steps,step,0)
    for h in range(H):
        dw0_ref[h]=(wst[0,:,h*F:(h+1)*F]+wst[1,:,h*F:(h+1)*F]).T
    db0h_ref[...]=gather_heads(bst[0]+bst[1],jnp.where(lane_iota((H,L),1)%MB==0,rep,0.0))
    def post_one(b):
        r=row_of(where,b,PER)
        dp=es[b]; row=rows[b]
        de=dp*gain_ref[...]
        dgain=dp*ps_[b]+de*ns[b]
        gr=(gs[b]*rate[b])
        drb=rs[b].astype(bf); grb=gr.astype(bf); dzb=zs[b].astype(bf)
        dst=jnp.where(keep,-dot_tn(grb,drb),0.0).astype(bf)
        dss=jnp.where(keep_t,-dot_tn(drb,grb),0.0).astype(bf)
        wt=wt_ref[b]
        kb=kq[b,0:L,:]; qb=kq[b,L:2*L,:]
        dqf=dot_tn(jnp.concatenate([drb,dst],axis=0),jnp.concatenate([wt,kb],axis=0))
        dkf=dot_tn(jnp.concatenate([dzb,(-gr).astype(bf),dss],axis=0),jnp.concatenate([wt,dws[b],qb],axis=0))
        det=de.T; dit=ios[b].T
        for h in range(H):
            rr=slice(h*MB,(h+1)*MB); cc=slice(h*F,(h+1)*F)
            dqkv_ref[pl.ds(r,MB),h*F:(h+1)*F]=(dqf[rr,cc]+dit[rr,:]).astype(bf)
            dqkv_ref[pl.ds(r,MB),C+h*F:C+(h+1)*F]=(dkf[rr,cc]+det[rr,:]).astype(bf)
            dqkv_ref[pl.ds(r,MB),2*C+h*F:2*C+(h+1)*F]=(-det[rr,:]).astype(bf)
        drl_ref[pl.ds(r,MB),:]=jnp.where(pick,row[3:4],0.0)
        return dgain,de
    def post(i,_):
        acc=None
        for u in range(UN):
            x=post_one(i*UN+u)
            acc=x if acc is None else tuple(a+c for a,c in zip(acc,x))
        dgain_ref[...]+=acc[0]; dshift_ref[...]+=acc[1]
        return 0
    lax.fori_loop(0,NB//UN,post,0)
    dgainh_ref[...]=gather_heads(dgain_ref[...],rep); dshifth_ref[...]=gather_heads(dshift_ref[...],rep)
    dpgh_ref[...]=gather_heads(dpg_ref[...],rep); dpsh_ref[...]=gather_heads(dps_ref[...],rep)
    drlh_ref[...]=lax.dot_general(drl_ref[...],rep,(((1,),(1,)),((),())),precision=HIGH,preferred_element_type=f32).astype(bf)

VM=pl.BlockSpec(memory_space=pltpu.VMEM); SM=pl.BlockSpec(memory_space=pltpu.SMEM)

def mixer_fwd(where,per,q,k,v,g,rl,w0,b0,gain,shift,pg,ps,UN=3):
    T,C=q.shape; H,F=b0.shape; L=H*MB; NB=T//MB
    S=jax.ShapeDtypeStruct
    fl=pltpu.VMEM((F,L),f32)
    return pl.pallas_call(functools.partial(fwd_kernel,UN,per),
        out_shape=[S((T,C),bf),S((T,C),bf),S((NB+1,F,L),f32),S((NB+1,F,L),f32),S((NB+1,F,C),bf),S((NB,L,L),bf)],
        in_specs=[SM]+[VM]*11,out_specs=[VM]*6,
        scratch_shapes=[pltpu.VMEM((NB+1,2*L,C),bf),pltpu.VMEM((NB+1,C,2*L),bf),pltpu.VMEM((NB+1,F,L),f32),pltpu.VMEM((NB+1,1,L),f32),
            pltpu.VMEM((NB+1,L,2*L),bf),pltpu.VMEM((2,F,C),f32),pltpu.VMEM((2,F,L),f32),pltpu.VMEM((T,L),f32),fl,fl,fl,fl],
        cost_estimate=cost(28),
        name='mixer_forward')(where,q,k,v,g,rl,w0,b0,gain,shift,pg,ps)

def mixer_bwd(where,per,q,k,v,g,rl,dm,zt,rt,wt,mt,gain,shift,pg,ps,UN=3):
    T,C=q.shape; H,F=gain.shape; L=H*MB; NB=T//MB
    S=jax.ShapeDtypeStruct
    fls=pltpu.VMEM((NB+1,F,L),f32); fl=pltpu.VMEM((F,L),f32)
    return pl.pallas_call(functools.partial(bwd_kernel,UN,per),
        out_shape=[S((T,3*C),bf),S((T,H),bf),S((H,F,F),f32)]+[S((H,F),f32)]*5,
        in_specs=[SM]+[VM]*14,out_specs=[VM]*8,
        scratch_shapes=[pltpu.VMEM((NB+1,2*L,C),bf),pltpu.VMEM((NB+1,C,2*L),bf),pltpu.VMEM((NB+1,1,L),f32)]+[fls]*6+[
            pltpu.VMEM((NB+1,8,L),f32),fls,fls,pltpu.VMEM((NB+1,F,C),bf),pltpu.VMEM((2,F,C),f32),pltpu.VMEM((2,F,L),f32),
            pltpu.VMEM((T,L),f32)]+[fl]*8+[pltpu.VMEM((T,L),f32)],
        cost_estimate=cost(33),
        name='mixer_backward')(where,q,k,v,g,rl,dm,zt,rt,wt,mt,gain,shift,pg,ps)


def cost(us):
    return pl.CostEstimate(flops=int(us * 1e9), bytes_accessed=int(us * 1e6), transcendentals=0)


def whole(x):
    return pl.BlockSpec(x.shape, lambda *_: (0,) * x.ndim)


SDS = jax.ShapeDtypeStruct


def project_kernel(nh, where, x_ref, gain_ref, wq, wk, wv, wg, wr, xn, q, k, v, g, rl):
    n = x_ref.shape[0] // nh

    @pl.when(pl.program_id(0) == 0)
    def _():
        for r in range(nh):
            x = x_ref[pl.ds(pl.multiple_of((where[0] ^ r) * n, MB), n), :].astype(f32)
            inv = lax.rsqrt(jnp.mean(x * x, axis=-1, keepdims=True) + EPS)
            xn[r * n : (r + 1) * n, :] = (gain_ref[...] * (x * inv)).astype(bf)
        rl[...] = dot_nt(xn[...], wr[...])

    for w, o in ((wq, q), (wk, k), (wv, v), (wg, g)):
        o[...] = dot_nn(xn[...], w[...]).astype(bf)


def project(nh, where, x, gain, weights, wr, tile=256):
    T, D = x.shape
    C, H = weights[0].shape[1], wr.shape[0]
    col = pl.BlockSpec((D, tile), lambda j: (0, j))
    out = pl.BlockSpec((T, tile), lambda j: (0, j))
    return pl.pallas_call(
        functools.partial(project_kernel, nh),
        grid=(C // tile,),
        in_specs=[SM, whole(x), whole(gain)] + [col] * 4 + [whole(wr)],
        out_specs=[pl.BlockSpec((T, D), lambda j: (0, 0))] + [out] * 4 + [pl.BlockSpec((T, H), lambda j: (0, 0))],
        out_shape=[SDS((T, D), bf)] + [SDS((T, C), bf)] * 4 + [SDS((T, H), f32)],
        cost_estimate=cost(8),
        name="project",
    )(where, x, gain, *weights, wr)


def split_kernel(kinds, more, *refs):
    n = len(kinds)
    acc = None
    for turned, a, b in zip(kinds, refs[:n], refs[n : 2 * n]):
        y = (dot_nt if turned else dot_nn)(a[...], b[...])
        acc = y if acc is None else acc + y
    extra, outs = refs[2 * n : 2 * n + more], refs[2 * n + more :]
    rows = outs[0].shape[0]
    for r, o in enumerate(outs):
        o[:rows, :] = acc[r * rows : (r + 1) * rows].astype(o.dtype)
        if 0 < r <= more:
            o[rows:, :] = extra[r - 1][...]


def split_product(nh, terms, name, us, extra=(), tile=512):
    T = terms[0][0].shape[-2]
    D = terms[0][1].shape[0 if terms[0][2] else 1]
    a_specs, b_specs = [], []
    for a, b, turned, col in terms:
        depth = b.shape[1 if turned else 0]
        if a.ndim == 3:
            a_specs.append(pl.BlockSpec((None, T, depth), lambda j, col=col: (col, 0, 0)))
        else:
            a_specs.append(pl.BlockSpec((T, depth), lambda j, col=col: (0, col)))
        b_specs.append(
            pl.BlockSpec((tile, depth), lambda j: (j, 0)) if turned else pl.BlockSpec((depth, tile), lambda j: (0, j))
        )
    n = T // nh
    rows = [2 * n if 0 < r <= len(extra) else n for r in range(nh)]
    return pl.pallas_call(
        functools.partial(split_kernel, [t[2] for t in terms], len(extra)),
        grid=(D // tile,),
        in_specs=a_specs + b_specs + [pl.BlockSpec((n, tile), lambda j: (0, j))] * len(extra),
        out_specs=[pl.BlockSpec((m, tile), lambda j: (0, j)) for m in rows],
        out_shape=[SDS((m, D), bf if r else f32) for r, m in enumerate(rows)],
        cost_estimate=cost(us),
        name=name,
    )(*[t[0] for t in terms], *[t[1] for t in terms], *extra)


def lay(target, arrays, plan):
    rows = target.shape[0] // len(plan)
    for i, (a, at) in enumerate(plan):
        target[i * rows : (i + 1) * rows, :] = arrays[a][at : at + rows, :]


def rows_kernel(*refs):
    out = refs[-1]
    n = refs[0].shape[0]
    for i, x in enumerate(refs[:-1]):
        out[i * n : (i + 1) * n, :] = x[...]


def top_rows(arrays, n):
    D = arrays[0].shape[1]
    return pl.pallas_call(
        rows_kernel,
        grid=(1,),
        in_specs=[pl.BlockSpec((n, D), lambda i: (0, 0))] * len(arrays),
        out_specs=pl.BlockSpec((n * len(arrays), D), lambda i: (0, 0)),
        out_shape=SDS((n * len(arrays), D), arrays[0].dtype),
        cost_estimate=cost(2),
        name="top_rows",
    )(*arrays)


def chunk_of(T):
    return T if T <= 576 else max(c for c in range(MB, 577, MB) if T % c == 0)


def feed_grad_kernel(many, chunk, *refs):
    w, back, flat = refs[many:]

    @pl.when(pl.program_id(0) == 0)
    def _():
        at = 0
        for a in refs[:many]:
            flat[at : at + a.shape[0], :] = a[...]
            at += a.shape[0]

    def body(i, _):
        rows = pl.ds(pl.multiple_of(i * chunk, MB), chunk)
        back[rows, :] = dot_nt(flat[rows, :], w[...]).astype(bf)
        return 0

    lax.fori_loop(0, back.shape[0] // chunk, body, 0)


def feed_grad(arrays, w, name, us, tile=512):
    T = sum(x.shape[0] for x in arrays)
    N, D = w.shape
    return pl.pallas_call(
        functools.partial(feed_grad_kernel, len(arrays), chunk_of(T)),
        grid=(pl.cdiv(N, tile),),
        in_specs=[whole(x) for x in arrays] + [pl.BlockSpec((tile, D), lambda j: (j, 0))],
        out_specs=pl.BlockSpec((T, tile), lambda j: (0, j)),
        out_shape=SDS((T, N), bf),
        scratch_shapes=[pltpu.VMEM((T, D), bf)],
        cost_estimate=cost(us),
        name=name,
    )(*arrays, w)


def feed_kernel(plan, many, chunk, *refs):
    arrays, backs = refs[:many], refs[many:-5]
    wg, wu, flat, out, grads = refs[-5:]

    @pl.when(pl.program_id(0) == 0)
    def _():
        lay(flat, arrays, plan)

    at = 0
    for b in backs:
        grads[at : at + b.shape[0], :] = b[...]
        at += b.shape[0]

    def body(i, _):
        rows = pl.ds(pl.multiple_of(i * chunk, MB), chunk)
        gate = dot_nt(flat[rows, :], wg[...])
        up = dot_nt(flat[rows, :], wu[...])
        grad = grads[rows, :].astype(f32)
        sig = jax.nn.sigmoid(gate)
        silu = gate * sig
        out[0, rows, :] = (grad * up * sig * (1.0 + gate * (1.0 - sig))).astype(bf)
        out[1, rows, :] = (grad * silu).astype(bf)
        out[2, rows, :] = (silu * up).astype(bf)
        return 0

    lax.fori_loop(0, flat.shape[0] // chunk, body, 0)


def feed(n, plan, arrays, backs, wg, wu, name, us, tile=512):
    T = n * len(plan)
    N, D = wg.shape
    row = pl.BlockSpec((tile, D), lambda j: (j, 0))
    return pl.pallas_call(
        functools.partial(feed_kernel, plan, len(arrays), chunk_of(T)),
        grid=(pl.cdiv(N, tile),),
        in_specs=[whole(x) for x in arrays]
        + [pl.BlockSpec((x.shape[0], tile), lambda j: (0, j)) for x in backs]
        + [row, row],
        out_specs=[pl.BlockSpec((T, D), lambda j: (0, 0)), pl.BlockSpec((3, T, tile), lambda j: (0, 0, j))],
        out_shape=[SDS((T, D), bf), SDS((3, T, N), bf)],
        scratch_shapes=[pltpu.VMEM((T, tile), bf)],
        cost_estimate=cost(us),
        name=name,
    )(*arrays, *backs, wg, wu)


def feed_blocks_kernel(plans, many, *refs):
    xs, ns = refs[1 : 1 + many], refs[1 + many : -2]
    give, keep = refs[-2:]
    y = None
    for plan, m in zip(plans, ns):
        x = jnp.concatenate([xs[i][...] for i in plan], axis=0)
        p = dot_tn(x, m[...])
        y = p if y is None else y + p
    y = y.T

    @pl.when(pl.program_id(1) == 0)
    def _():
        give[...] = y.astype(bf)

    @pl.when(pl.program_id(1) == 1)
    def _():
        keep[...] = y


def feed_blocks(where, nz, xs, plans, ns, first, layers, wide, name, us):
    N = ns[0].shape[2]
    x_specs = [
        pl.BlockSpec((x.shape[0], wide), lambda w, b, where: (0, where[3 + nz * (1 - b)])) for x in xs
    ]
    n_specs = [pl.BlockSpec((None, m.shape[1], N), lambda w, b, where: (first + w, 0, 0)) for m in ns]
    out = pl.BlockSpec((None, N, wide), lambda w, b, where: (w, 0, 0))
    return pl.pallas_call(
        functools.partial(feed_blocks_kernel, plans, len(xs)),
        grid_spec=pltpu.PrefetchScalarGridSpec(
            num_scalar_prefetch=1, grid=(layers, 2), in_specs=x_specs + n_specs, out_specs=[out, out]
        ),
        out_shape=[SDS((layers, N, wide), bf), SDS((layers, N, wide), f32)],
        cost_estimate=cost(us),
        name=name,
    )(where, *xs, *ns)


def branch_kernel(n, *refs):
    pieces = refs[:n]
    w, slope, flat, mg, dg = refs[n:]

    @pl.when(pl.program_id(0) == 0)
    def _():
        rows = flat.shape[0] // n
        for i, a in enumerate(pieces):
            flat[i * rows : (i + 1) * rows, :] = a[:rows, :]

    y = dot_nt(flat[...], w[...])
    mg[...] = y.astype(bf)
    dg[...] = (y * slope[...].astype(f32)).astype(bf)


def branch_back(pieces, n, w, slope, tile=256):
    T, C = slope.shape
    D = w.shape[1]
    out = pl.BlockSpec((T, tile), lambda j: (0, j))
    return pl.pallas_call(
        functools.partial(branch_kernel, len(pieces)),
        grid=(C // tile,),
        in_specs=[whole(x) for x in pieces] + [pl.BlockSpec((tile, D), lambda j: (j, 0)), out],
        out_specs=[pl.BlockSpec((T, D), lambda j: (0, 0)), out, out],
        out_shape=[SDS((T, D), bf), SDS((T, C), bf), SDS((T, C), bf)],
        cost_estimate=cost(4),
        name="branch_back",
    )(*pieces, w, slope)


def blocks_kernel(groups, turned, *refs):
    refs = refs[1:]
    n = sum(groups)
    xs, ns, outs = refs[:n], refs[n : 2 * n], refs[2 * n :]
    parts, at = [], 0
    for count in groups:
        y = None
        for i in range(at, at + count):
            p = dot_tn(xs[i][...], ns[i][...])
            y = p if y is None else y + p
        parts.append(y)
        at += count
    for k, o in enumerate(outs):
        @pl.when(pl.program_id(0) == k)
        def _(o=o):
            at = 0
            for y in parts:
                if turned:
                    o[at : at + y.shape[1], :] = y.T.astype(o.dtype)
                else:
                    o[:, at : at + y.shape[1]] = y.astype(o.dtype)
                at += y.shape[1]


def block_products(where, stride, groups, kinds, wide, name, us, turned=False):
    xs = [x for group in groups for x, _ in group]
    ns = [n for group in groups for _, n in group]
    N = sum(group[0][1].shape[1] for group in groups)
    x_specs = [pl.BlockSpec((x.shape[0], wide), lambda k, where: (0, where[3 + stride * k])) for x in xs]
    n_specs = [pl.BlockSpec(n.shape, lambda k, where: (0, 0)) for n in ns]
    shape = (N, wide) if turned else (wide, N)
    return pl.pallas_call(
        functools.partial(blocks_kernel, [len(group) for group in groups], turned),
        grid_spec=pltpu.PrefetchScalarGridSpec(
            num_scalar_prefetch=1,
            grid=(len(kinds),),
            in_specs=x_specs + n_specs,
            out_specs=[pl.BlockSpec(shape, lambda k, where: (0, 0))] * len(kinds),
        ),
        out_shape=[SDS(shape, kind) for kind in kinds],
        cost_estimate=cost(us),
        name=name,
    )(where, *xs, *ns)


def natural_kernel(n, plans, many, where, *refs):
    for plan, out in zip(plans, refs[many:]):
        for r, (i, at) in enumerate(plan):
            out[pl.ds(pl.multiple_of((where[0] ^ r) * n, MB), n), :] = refs[i][at : at + n, :]


def natural(where, arrays, n, plans):
    D = arrays[0].shape[1]
    return pl.pallas_call(
        functools.partial(natural_kernel, n, plans, len(arrays)),
        in_specs=[SM] + [VM] * len(arrays),
        out_specs=[VM] * len(plans),
        out_shape=[SDS((n * len(plan), D), arrays[0].dtype) for plan in plans],
        cost_estimate=cost(0.2),
        name="natural",
    )(where, *arrays)


def join_kernel(one, by_two, two, by_one, for_one, for_two):
    n = by_two.shape[0]
    for_one[:n, :] = (one[:n, :].astype(f32) + by_two[...].astype(f32)).astype(bf)
    for_one[n:, :] = one[n:, :]
    for_two[:n, :] = two[:n, :]
    for_two[n:, :] = (two[n:, :].astype(f32) + by_one[...].astype(f32)).astype(bf)


def join(one, by_two, two, by_one):
    return pl.pallas_call(
        join_kernel,
        in_specs=[VM] * 4,
        out_specs=[VM] * 2,
        out_shape=[SDS(one.shape, bf), SDS(two.shape, bf)],
        cost_estimate=cost(1),
        name="join",
    )(one, by_two, two, by_one)


def add_rows(x, row):
    high = row.astype(bf)
    low = (row - high.astype(f32)).astype(bf)
    rest = jnp.zeros((MB - 2, row.shape[0]), bf)
    return jnp.concatenate([x, high[None], low[None], rest], axis=0)


def last_rows(x):
    return x[-MB].astype(f32) + x[1 - MB].astype(f32)


def after(x, *others):
    return lax.optimization_barrier((x, others))[0]


def rms_inv(x):
    return lax.rsqrt(jnp.mean(x * x, axis=-1, keepdims=True) + EPS)


class Links:
    def __init__(self, mesh):
        self.nh = mesh.shape["head"]
        self.nq = mesh.shape["seq"]
        self.nz = self.nq // 2
        self.turns = tuple(range(self.nh - 1, 0, -1))

    def place(self):
        self.h = lax.axis_index("head")
        self.s = lax.axis_index("seq")
        self.c = self.s % 2
        self.z = self.s // 2

    def partner(self, x, r):
        return lax.ppermute(x, "head", [(i, i ^ r) for i in range(self.nh)])

    def sibling(self, x):
        return lax.ppermute(x, "seq", [(i, i ^ 1) for i in range(self.nq)])

    def along(self, x, k):
        n = self.nz
        return lax.ppermute(x, "seq", [(2 * p + c, 2 * ((p + k) % n) + c) for p in range(n) for c in range(2)])

    def head_sum(self, parts, hold=()):
        got = [after(self.partner(parts[r], r), *hold) for r in self.turns]
        total = parts[0]
        for x in got:
            total = total + x.astype(f32)
        return total

    def head_pieces(self, x):
        got = {r: self.partner(x, r) for r in self.turns}
        return [x] + [got[r] for r in range(1, self.nh)]

    def paired_start(self, parts, across, hold):
        if self.nh != 4:
            return parts[1:]
        by_two = after(self.partner(parts[3], 2), hold)
        by_one = after(self.partner(across, 1), hold)
        return join(parts[1], by_two, parts[2], by_one)

    def paired_pieces(self, x, n, hold):
        if self.nh != 4:
            pieces = self.head_pieces(x)
            return pieces, tuple((r, 0) for r in range(self.nh)), tuple((r, n) for r in range(self.nh))
        one, two = self.partner(x, 1), self.partner(x, 2)
        one, two = lax.optimization_barrier((after(one, hold), after(two, hold)))
        upper, lower = self.partner(one[:n], 2), self.partner(two[n:], 1)
        return [x, one, two, upper, lower], ((0, 0), (1, 0), (2, 0), (3, 0)), ((0, n), (1, n), (2, n), (4, 0))

    def line_sum(self, parts):
        got = [self.along(parts[k], k) for k in self.line_order()]
        total = parts[0]
        for x in got:
            total = total + x.astype(f32)
        return total

    def line_order(self):
        half = self.nz // 2
        return sorted(range(1, self.nz), key=lambda k: abs(k - half))

    def ring(self, x):
        out = []
        for _ in range(1, self.nz):
            x = self.along(x, 1)
            out.append(x)
        return out

    def ring_sum(self, parts):
        total = parts[self.nz - 1]
        for k in range(self.nz - 2, -1, -1):
            total = parts[k] + self.along(total, 1).astype(f32)
            total = total if k == 0 else total.astype(bf)
        return total

    def relative(self, x):
        n = x.shape[0] // self.nh
        return jnp.concatenate(
            [lax.dynamic_slice_in_dim(x, (self.h ^ r) * n, n, axis=0) for r in range(self.nh)], axis=0
        )


def per_device(
    links,
    inputs,
    lengths,
    first_gain,
    query_weight,
    key_weight,
    value_weight,
    gate_weight,
    rate_weight,
    inner_weight,
    inner_offset,
    inner_gain,
    inner_shift,
    post_gain,
    post_shift,
    out_weight,
    second_gain,
    feed_gate,
    feed_up,
    feed_down,
    out_grad,
):
    links.place()
    nh, nz, nq = links.nh, links.nz, links.nq
    spot = jnp.arange(4 + nz, dtype=jnp.int32)
    cols = 2 * lax.rem(links.z + spot + (nz - 3), nz) + links.c
    cols = jnp.where(spot == 3 + nz, 2 * links.z + 1 - links.c, cols)
    where = jnp.where(spot == 0, links.h, jnp.where(spot == 1, lengths[0, 0], jnp.where(spot == 2, lengths[0, 1], cols)))
    n = inputs.shape[0] // nh
    per = n // MB
    wide = inputs.shape[1] // nq
    heads, width = inner_offset.shape
    C = heads * width
    pg, ps = post_gain[None], post_shift[None]
    rate_turned = rate_weight.T
    feed_gate, feed_up = feed_gate.T, feed_up.T

    grad_rel = links.relative(out_grad)
    straight = [0] + list(range(3, nh))
    steps = nz - 1
    normed_one, query, key, value, gate, rate_logit = project(
        nh, where, inputs, first_gain[None], (query_weight, key_weight, value_weight, gate_weight), rate_turned
    )
    lead = after(grad_rel, rate_logit)
    grad_ring = [links.along(jnp.concatenate([lead[:n], lead[3 * n :]], axis=0), 1)]
    mixed, slope, zt, rt, wt, mt = mixer_fwd(
        where, per, query, key, value, gate, rate_logit, inner_weight, inner_offset, inner_gain, inner_shift, pg, ps
    )
    own_source = lax.dynamic_slice_in_dim(inputs, links.h * n, n, axis=0).astype(f32)
    own_upstream = grad_rel[:n].astype(f32)

    mixed = after(mixed, grad_ring[0])
    for k in range(2, nz):
        grad_ring.append(links.along(grad_ring[-1], 1))
    out_parts = split_product(nh, [(mixed, out_weight, False, 0)], "out_product", 4, tile=1024)
    backs = [feed_grad([after(grad_ring[0], out_parts[0])], feed_down, "feed_grad_first", 1)]
    back_own = feed_grad([after(grad_rel, backs[0])], feed_down, "feed_grad_own", 1)
    hidden = own_source + links.head_sum(out_parts, (back_own,))
    r2 = rms_inv(hidden)
    two_own = (second_gain * (hidden * r2)).astype(bf)
    twos = links.head_pieces(two_own)
    for k in range(1, steps - 1):
        backs.append(feed_grad([after(grad_ring[k], two_own)], feed_down, "feed_grad_next", 1))
    twos[1:] = [after(x, backs[-1], grad_ring[-1]) for x in twos[1:]]
    grad_across = top_rows([after(grad_ring[0], *twos[1:]), *grad_ring[1:]], n)
    grad_across = [links.partner(grad_across, r) for r in (1, 2)]
    own_plan = tuple((r, 0) for r in range(nh))
    normed_two, feed_own = feed(n, own_plan, twos, [back_own], feed_gate, feed_up, "feed_own", 4)
    two_ring = [links.along(after(jnp.concatenate([twos[r] for r in straight], axis=0), *twos[1:]), 1)]
    back_parts = split_product(
        nh, [(feed_own, feed_gate, False, 0), (feed_own, feed_up, False, 1)], "feed_back", 3
    )
    two_ring[0] = after(two_ring[0], back_parts[0])
    for k in range(2, nz):
        two_ring.append(links.along(two_ring[-1], 1))
    back_parts = [back_parts[0]] + [after(x, two_ring[0], *grad_across) for x in back_parts[1:]]
    down_parts = list(split_product(nh, [(after(feed_own, back_parts[0]), feed_down, False, 2)], "feed_down", 1, tile=1024))
    last_grads = [grad_ring[-1], *grad_across]
    backs.append(feed_grad([after(last_grads[0], down_parts[0]), *last_grads[1:]], feed_down, "feed_grad_last", 1))
    two = links.head_sum(back_parts, (backs[-1], two_ring[1]))
    u = two * second_gain
    hidden_grad = own_upstream + r2 * u - hidden * (r2 * r2 * r2) * jnp.mean(u * hidden, axis=-1, keepdims=True)
    second_part = jnp.sum(two * hidden * r2, axis=0)
    pieces = links.head_pieces(add_rows(hidden_grad.astype(bf), second_part))
    parts = range(len(straight))
    plan = tuple((k, i * n) for k in range(steps - 1) for i in parts)
    held = [after(two_ring[0], pieces[0]), *two_ring[1:-1]]
    first = feed(n, plan, held, backs[:-1], feed_gate, feed_up, "feed_first", 1)
    pieces[1:] = [after(x, first[1]) for x in pieces[1:]]
    second_part = (second_part, pieces[1:])
    pieces[0] = after(pieces[0], two_ring[-1])
    branch_grad, mixed_grad, dg = branch_back(pieces, n, out_weight, slope)
    across = top_rows(two_ring, n)
    across = [links.partner(across, r) for r in (1, 2)]

    one_sib = links.sibling(normed_one)
    groups = [
        [(normed_one, dg), (one_sib, links.sibling(dg))],
        [(branch_grad, mixed), (links.sibling(branch_grad), links.sibling(mixed))],
    ]
    pair = block_products(where, 1, groups, [f32] + [bf] * (nz - 1), wide, "gate_out_blocks", 8)
    pair_got = {2: links.along(pair[2], 2)}

    dqkv, drate, dw0, db0, dgain, dshift, dpg, dps = mixer_bwd(
        where, per, query, key, value, gate, rate_logit, after(mixed_grad, pair[0]),
        zt, rt, wt, mt, inner_gain, inner_shift, pg, ps
    )
    dqkv = after(dqkv, *pair_got.values(), *across)
    pair_got[1] = links.along(after(pair[1], dqkv), 1)
    drate_low = drate
    dqkv_sib = links.sibling(dqkv)
    back_parts = split_product(
        nh,
        [
            (dqkv, query_weight, True, 0),
            (dqkv, key_weight, True, 1),
            (dqkv, value_weight, True, 2),
            (dg, gate_weight, True, 0),
            (drate_low, rate_turned, False, 0),
        ],
        "input_back",
        8,
        extra=down_parts[1 : 3 if nh == 4 else nh],
    )
    groups = [[(normed_one, after(dqkv, back_parts[0], *pair_got.values())), (one_sib, dqkv_sib)]]
    trio = block_products(where, 1, groups, [f32] + [bf] * (nz - 1), wide, "qkv_blocks", 8)
    parts_two = links.paired_start(back_parts, down_parts[3], trio[0])
    trio_step = links.along(trio[-1], 1)

    plan = tuple((0, i * n) for i in parts) + tuple((1 + i, k * n) for i in range(2) for k in range(steps))
    held = [after(two_ring[-1], trio[0], parts_two[0]), *across]
    second = feed(n, plan, held, backs[-1:], feed_gate, feed_up, "feed_second", 15, tile=256)

    def rows_of(x):
        return x.reshape(nq, -1)

    def heads_of(x):
        return x.reshape((heads, nq, -1)).transpose(1, 0, 2).reshape(nq, -1)

    received = [links.partner(x, r + 1) for r, x in enumerate(parts_two)]
    second, trio_step, received = lax.optimization_barrier((second, trio_step, received))
    send = (trio[nz - 2].astype(f32) + trio_step.astype(f32)).astype(bf)
    sums = jnp.concatenate([back_parts[0], down_parts[0]], axis=0)
    for x in received:
        sums = sums + x.astype(f32)
    one, output = sums[:n], hidden + sums[n:]
    r1 = rms_inv(own_source)
    w = one * first_gain
    input_grad = hidden_grad + r1 * w - own_source * (r1 * r1 * r1) * jnp.mean(w * own_source, axis=-1, keepdims=True)
    input_low = input_grad.astype(bf)
    first_part = jnp.sum(one * own_source * r1, axis=0)
    packed = add_rows(jnp.concatenate([input_low, output.astype(bf)], axis=0), first_part)
    got = links.along(send, 1)
    outs = [feed_own, first[1], second[1]]
    xs = [normed_two, first[0], after(second[0], packed)]
    give, keep = feed_blocks(where, nz, xs, ((0,), (1,), (2,)), outs, 0, 2, wide, "feed_in_blocks", 6)
    for k in range(nz - 3, 0, -1):
        send = (trio[k].astype(f32) + after(got, keep).astype(f32)).astype(bf)
        got = links.along(send, 1)
    arrays, upper, lower = links.paired_pieces(packed, n, send)
    xs = [after(grad_rel, keep, send), *grad_ring, *grad_across]
    plans = ((0,), tuple(range(1, steps)), tuple(range(steps, len(xs))))
    first_give = give
    give, keep_out = feed_blocks(where, nz, xs, plans, outs, 2, 1, wide, "feed_out_blocks", 4)
    for k in range(3, nz):
        pair_got[k] = links.along(after(pair[k], keep_out), k)
    other = links.sibling(after(first_give, keep_out)).astype(f32)
    feed_grads = [keep[0] + other[0], keep[1] + other[1]]
    second_part, held = second_part
    second_part = second_part + sum(last_rows(after(x, keep_out)) for x in held)
    rate_part = lax.dot_general(
        after(normed_one, keep_out), drate_low, (((0,), (0,)), ((), ())), preferred_element_type=f32
    )
    dw0, db0, dgain, dshift, dpg, dps = after((dw0, db0, dgain, dshift, dpg, dps), keep_out)
    small = [rows_of(second_part), rows_of(rate_part), heads_of(dw0)]
    small += [heads_of(x) for x in (db0, dgain, dshift)] + [rows_of(dpg), rows_of(dps)]
    sizes = [x.shape[1] for x in small]
    small = jnp.concatenate(small, axis=1)
    got, small = lax.optimization_barrier((after(got, keep_out), small))
    grad_qkv = trio[0] + got.astype(f32)
    arrays[1:] = [after(x, grad_qkv, *feed_grads) for x in arrays[1:]]
    feed_grads.append(keep_out[0] + links.sibling(after(give[0], grad_qkv)).astype(f32))
    first_part = first_part + sum(last_rows(arrays[i]) for i, _ in lower[1:])
    sizes = [wide] + sizes
    small = jnp.concatenate([rows_of(first_part), small], axis=1).reshape(nz, 2, -1)
    keep = lax.dynamic_index_in_dim(small, links.c, 1, keepdims=False)
    give = lax.dynamic_index_in_dim(small, 1 - links.c, 1, keepdims=False)
    small = keep + links.sibling(give)
    input_grad, output = natural(where, arrays, n, (upper, lower))
    small = links.line_sum([lax.dynamic_index_in_dim(small, lax.rem(links.z + k, nz), 0, keepdims=False) for k in range(nz)])
    pair = pair[0] + sum(after(x, input_grad).astype(f32) for x in pair_got.values())
    ends = [sum(sizes[: i + 1]) for i in range(len(sizes))]
    small = [small[e - n : e] for e, n in zip(ends, sizes)]
    part = width // nq
    return (
        output,
        input_grad,
        small[0],
        grad_qkv[:, :C],
        grad_qkv[:, C : 2 * C],
        grad_qkv[:, 2 * C :],
        pair[:, :C],
        small[2].reshape(-1, heads),
        small[3].reshape(heads, part, width),
        small[4].reshape(heads, part),
        small[5].reshape(heads, part),
        small[6].reshape(heads, part),
        small[7],
        small[8],
        pair[:, C:].T,
        small[1],
        feed_grads[0].T,
        feed_grads[1].T,
        feed_grads[2],
    )


def solution(mesh):
    in_specs = (
        P("seq", None),
        P("seq", None),
        P(),
        P(None, "head"),
        P(None, "head"),
        P(None, "head"),
        P(None, "head"),
        P(None, "head"),
        P("head", None, None),
        P("head", None),
        P("head", None),
        P("head", None),
        P("head"),
        P("head"),
        P("head", None),
        P(),
        P(None, "head"),
        P(None, "head"),
        P("head", None),
        P("seq", None),
    )
    out_specs = (
        P("seq", None),
        P("seq", None),
        P("seq"),
        P("seq", "head"),
        P("seq", "head"),
        P("seq", "head"),
        P("seq", "head"),
        P("seq", "head"),
        P("head", "seq", None),
        P("head", "seq"),
        P("head", "seq"),
        P("head", "seq"),
        P(("head", "seq")),
        P(("head", "seq")),
        P("head", "seq"),
        P("seq"),
        P("seq", "head"),
        P("seq", "head"),
        P("head", "seq"),
    )
    return jax.shard_map(
        functools.partial(per_device, Links(mesh)), mesh=mesh, in_specs=in_specs, out_specs=out_specs, check_vma=False
    )
```

```python
import functools

import jax
import jax.numpy as jnp
from jax import lax
from jax.experimental import pallas as pl
from jax.experimental.pallas import tpu as pltpu
from jax.sharding import PartitionSpec as P

MB=16; EPS=1e-6
bf=jnp.bfloat16; f32=jnp.float32

def dot_nn(a,b): return lax.dot_general(a,b,(((1,),(0,)),((),())),preferred_element_type=f32)
def dot_nt(a,b): return lax.dot_general(a,b,(((1,),(1,)),((),())),preferred_element_type=f32)
def dot_tn(a,b): return lax.dot_general(a,b,(((0,),(0,)),((),())),preferred_element_type=f32)

def mean0(x): return jnp.mean(x,axis=0,keepdims=True)

def norm_parts(x):
    c=x-mean0(x)
    inv=lax.rsqrt(mean0(c*c)+EPS)
    return c*inv,inv

def norm_back(dy,n,inv):
    return inv*(dy-mean0(dy)-n*mean0(dy*n))

def split2(x):
    hi=x.astype(bf)
    return jnp.concatenate([hi,(x-hi.astype(f32)).astype(bf)],axis=0)

def two_rows(x):
    h=x.shape[0]//2
    return x[:h]+x[h:]

def stack_heads(rows,F):
    H=rows.shape[1]//F
    r=rows.astype(f32)
    return jnp.concatenate([r[:,h*F:(h+1)*F] for h in range(H)],axis=0).T

GC=0.7978845608028654; GA=0.044715
def gelu_parts(x):
    u=GC*(x+GA*x*x*x)
    t=jnp.tanh(u)
    val=0.5*x*(1.0+t)
    der=0.5*(1.0+t)+0.5*x*(1.0-t*t)*GC*(1.0+3.0*GA*x*x)
    return val,der

def plan_blocks(where):
    n0=(where[1]+MB-1)//MB; n1=(where[2]+MB-1)//MB
    return (n0,n1),(0,n0)

def row_of(where,b,per):
    return pl.multiple_of(((lax.div(b,per)^where[0])*per+lax.rem(b,per))*MB,MB)

def lane_iota(shape,dim): return lax.broadcasted_iota(jnp.int32,shape,dim)

def valid_row(where,offs,blk,L):
    pos=blk*MB+lane_iota((1,L),1)%MB
    a=(pos>=offs[0]*MB)&(pos<offs[0]*MB+where[1])
    b=(pos>=offs[1]*MB)&(pos<offs[1]*MB+where[2])
    return a|b

def fill_bd(dst,blk,rows,row0,F):
    H=rows.shape[1]//F
    for h in range(H):
        dst[blk,row0+h*MB:row0+(h+1)*MB,h*F:(h+1)*F]=rows[:,h*F:(h+1)*F]

def fill_turned(dst,blk,kt,qt):
    F,L=kt.shape
    both=jnp.concatenate([kt,qt],axis=1).astype(bf)
    lane=lane_iota((F,2*L),1)%L//MB
    for h in range(L//MB):
        dst[blk,h*F:(h+1)*F,:]=jnp.where(lane==h,both,jnp.zeros_like(both))

def same_head(L):
    return lane_iota((L,L),0)//MB==lane_iota((L,L),1)//MB

def head_lanes(H,L):
    return (lane_iota((H,L),0)==lane_iota((H,L),1)//MB).astype(f32)

HIGH=lax.Precision.HIGHEST
def head_rows(ref,F):
    return jnp.concatenate([ref[:,i:i+F] for i in range(0,ref.shape[1],F)],axis=0)
def spread(per_head,rep):
    return lax.dot_general(per_head,rep,(((0,),(0,)),((),())),precision=HIGH,preferred_element_type=f32)
def gather_heads(x,rep):
    return lax.dot_general(rep,x,(((1,),(1,)),((),())),precision=HIGH,preferred_element_type=f32)

def fwd_kernel(UN,PER,where,q_ref,k_ref,v_ref,g_ref,rlh_ref,w0_ref,b0_ref,gainh_ref,shifth_ref,pgh_ref,psh_ref,
               mixed_ref,slope_ref,zt_ref,rt_ref,wt_ref,mt_ref,
               kq,kqt,tt,rate,mtb,wst,bst,rl_ref,gain_ref,shift_ref,pg_ref,ps_ref):
    T,C=q_ref.shape; H,F=b0_ref.shape; L=H*MB; NB=T//MB
    rep=head_lanes(H,L)
    rl_ref[...]=lax.dot_general(rlh_ref[...],rep,(((1,),(0,)),((),())),precision=HIGH,preferred_element_type=f32)
    gain_ref[...]=spread(gainh_ref[...],rep); shift_ref[...]=spread(shifth_ref[...],rep)
    pg_ref[...]=spread(head_rows(pgh_ref,F),rep); ps_ref[...]=spread(head_rows(psh_ref,F),rep)
    counts,offs=plan_blocks(where)
    zero_kq=jnp.zeros((2*L,C),bf)
    onesbd=same_head(L).astype(f32).astype(bf)
    keep=same_head(L)&(lane_iota((L,L),0)<=lane_iota((L,L),1))
    pick=lane_iota((MB,L),0)==lane_iota((MB,L),1)%MB
    def clear(b,_):
        kq[b]=zero_kq
        return 0
    lax.fori_loop(0,NB+1,clear,0)
    kqt[NB]=jnp.zeros((C,2*L),bf)
    tt[NB]=jnp.zeros((F,L),f32); rate[NB]=jnp.zeros((1,L),f32); mtb[NB]=jnp.zeros((L,2*L),bf)
    def pre_one(b):
        r=row_of(where,b,PER)
        kn=k_ref[pl.ds(r,MB),:]; qn=q_ref[pl.ds(r,MB),:]; vn=v_ref[pl.ds(r,MB),:]
        fill_bd(kq,b,kn,0,F); fill_bd(kq,b,qn,L,F)
        kt=stack_heads(kn,F); qt=stack_heads(qn,F)
        tt[b]=stack_heads(vn,F)-kt
        fill_turned(kqt,b,kt,qt)
        ok=valid_row(where,offs,b,L)
        rl=jnp.sum(jnp.where(pick,rl_ref[pl.ds(r,MB),:],0.0),axis=0,keepdims=True)
        rate[b]=jnp.where(ok,jax.nn.sigmoid(rl)*(1.0/F),0.0)
        st=dot_nn(kq[b,0:L,:],kqt[b,:,L:2*L])
        m=jnp.where(keep,st+1.0,0.0).astype(bf)
        mt_ref[b]=m
        mtb[b,:,0:L]=m; mtb[b,:,L:2*L]=onesbd
    def pre(i,_):
        for u in range(UN): pre_one(i*UN+u)
        return 0
    lax.fori_loop(0,NB//UN,pre,0)
    def unused(b,_):
        rt_ref[b]=jnp.zeros((F,L),f32)
        zt_ref[b]=jnp.zeros((F,L),f32)
        wt_ref[b]=jnp.zeros((F,C),bf)
        return 0
    lax.fori_loop(counts[0]+counts[1],NB,unused,0)
    bias0=spread(b0_ref[...],rep)
    for h in range(H):
        wh=w0_ref[h].T
        for s in range(2): wst[s,:,h*F:(h+1)*F]=wh
    for s in range(2): bst[s]=bias0
    gain2=jnp.concatenate([gain_ref[...]]*2,axis=1); shift2=jnp.concatenate([shift_ref[...]]*2,axis=1)
    def step(i,_):
        bs=[jnp.where(i<counts[s],offs[s]+i,NB) for s in range(2)]
        w=[wst[s] for s in range(2)]; bias=[bst[s] for s in range(2)]
        w2=[split2(x) for x in w]
        zq=[two_rows(dot_nn(w2[s],kqt[bs[s]])) for s in range(2)]
        z=[zq[s][:,:L]+bias[s] for s in range(2)]
        for s in range(2):
            wt_ref[bs[s]]=w2[s][:F]; zt_ref[bs[s]]=z[s]
        zz=jnp.concatenate(z,axis=1)
        n,inv=norm_parts(zz)
        t2=jnp.concatenate([tt[b] for b in bs],axis=1)
        p=(n*gain2+shift2-t2)*gain2
        g=inv*(p-mean0(p)-n*mean0(p*n))
        g=g*jnp.concatenate([rate[b] for b in bs],axis=1)
        gr=[g[:,s*L:(s+1)*L].astype(bf) for s in range(2)]
        up=[dot_nn(gr[s],kq[bs[s],0:L,:]) for s in range(2)]
        for s in range(2): wst[s]=w[s]-up[s]
        ob=[dot_nn(gr[s],mtb[bs[s]]) for s in range(2)]
        for s in range(2):
            bst[s]=bias[s]-ob[s][:,L:]
            rt_ref[bs[s]]=zq[s][:,L:]+bias[s]-ob[s][:,:L]
        return 0
    lax.fori_loop(0,jnp.maximum(counts[0],counts[1]),step,0)
    def post_one(b):
        r=row_of(where,b,PER)
        qt=stack_heads(q_ref[pl.ds(r,MB),:],F); gt=stack_heads(g_ref[pl.ds(r,MB),:],F)
        nr,_=norm_parts(rt_ref[b])
        io=qt+nr*gain_ref[...]+shift_ref[...]
        ni,_=norm_parts(io)
        act,der=gelu_parts(gt)
        ok=valid_row(where,offs,b,L)
        lo=jnp.where(ok,ni*pg_ref[...]+ps_ref[...],0.0)
        m=(act*lo).T; sl=(der*lo).T
        for h in range(H):
            mixed_ref[pl.ds(r,MB),h*F:(h+1)*F]=m[h*MB:(h+1)*MB,:].astype(bf)
            slope_ref[pl.ds(r,MB),h*F:(h+1)*F]=sl[h*MB:(h+1)*MB,:].astype(bf)
    def post(i,_):
        for u in range(UN): post_one(i*UN+u)
        return 0
    lax.fori_loop(0,NB//UN,post,0)

def bwd_kernel(UN,PER,where,q_ref,k_ref,v_ref,g_ref,rlh_ref,dm_ref,zt_ref,rt_ref,wt_ref,mt_ref,gainh_ref,shifth_ref,pgh_ref,psh_ref,
               dqkv_ref,drlh_ref,dw0_ref,db0h_ref,dgainh_ref,dshifth_ref,dpgh_ref,dpsh_ref,
               kq,kqt,rate,ns,ps_,gs,xs,rs,ios,rows,zs,es,dws,wst,bst,rl_ref,gain_ref,shift_ref,pg_ref,ps_ref,
               dgain_ref,dshift_ref,dpg_ref,dps_ref,drl_ref):
    T,C=q_ref.shape; H,F=gainh_ref.shape; L=H*MB; NB=T//MB
    rep=head_lanes(H,L)
    rl_ref[...]=lax.dot_general(rlh_ref[...],rep,(((1,),(0,)),((),())),precision=HIGH,preferred_element_type=f32)
    gain_ref[...]=spread(gainh_ref[...],rep); shift_ref[...]=spread(shifth_ref[...],rep)
    pg_ref[...]=spread(head_rows(pgh_ref,F),rep); ps_ref[...]=spread(head_rows(psh_ref,F),rep)
    counts,offs=plan_blocks(where)
    zero_kq=jnp.zeros((2*L,C),bf)
    onesbd=same_head(L).astype(f32).astype(bf)
    keep=same_head(L)&(lane_iota((L,L),0)<=lane_iota((L,L),1))
    keep_t=same_head(L)&(lane_iota((L,L),1)<=lane_iota((L,L),0))
    pick=lane_iota((MB,L),0)==lane_iota((MB,L),1)%MB
    zfl=jnp.zeros((F,L),f32)
    def clear(b,_):
        kq[b]=zero_kq
        return 0
    lax.fori_loop(0,NB+1,clear,0)
    for ref in (ns,ps_,gs,xs,rs): ref[NB]=zfl
    kqt[NB]=jnp.zeros((C,2*L),bf)
    rate[NB]=jnp.zeros((1,L),f32); rows[NB]=jnp.zeros((8,L),f32)
    for ref in (dgain_ref,dshift_ref,dpg_ref,dps_ref): ref[...]=zfl
    def pre_one(b):
        r=row_of(where,b,PER)
        kn=k_ref[pl.ds(r,MB),:]; qn=q_ref[pl.ds(r,MB),:]
        fill_bd(kq,b,kn,0,F); fill_bd(kq,b,qn,L,F)
        kt=stack_heads(kn,F); qt=stack_heads(qn,F)
        t=stack_heads(v_ref[pl.ds(r,MB),:],F)-kt
        fill_turned(kqt,b,kt,kt)
        gt=stack_heads(g_ref[pl.ds(r,MB),:],F)
        dm=stack_heads(dm_ref[pl.ds(r,MB),:],F)
        ok=valid_row(where,offs,b,L)
        rl=jnp.sum(jnp.where(pick,rl_ref[pl.ds(r,MB),:],0.0),axis=0,keepdims=True)
        sg=jax.nn.sigmoid(rl)
        rt=jnp.where(ok,sg*(1.0/F),0.0)
        rate[b]=rt
        gain=gain_ref[...]; shift=shift_ref[...]
        n,inv=norm_parts(zt_ref[b])
        e=n*gain+shift-t
        p=e*gain
        mpn=mean0(p*n)
        g=inv*(p-mean0(p)-n*mpn)
        nr,invr=norm_parts(rt_ref[b])
        io=qt+nr*gain+shift
        ni,invi=norm_parts(io)
        act,_=gelu_parts(gt)
        dl=jnp.where(ok,dm*act,0.0)
        dio=norm_back(dl*pg_ref[...],ni,invi)
        dr=norm_back(dio*gain,nr,invr)
        drb=dr.astype(bf)
        ns[b]=n; ps_[b]=e; gs[b]=g; rs[b]=dr; ios[b]=dio
        xs[b]=dot_nt(drb,mt_ref[b])
        rows[b]=jnp.concatenate([inv,mpn,sg*(1.0-sg)*jnp.where(ok,1.0/F,0.0),jnp.zeros((5,L),f32)],axis=0)
        return dl,dl*ni,dio,dio*nr
    def pre(i,_):
        acc=None
        for u in range(UN):
            x=pre_one(i*UN+u)
            acc=x if acc is None else tuple(a+c for a,c in zip(acc,x))
        dps_ref[...]+=acc[0]; dpg_ref[...]+=acc[1]; dshift_ref[...]+=acc[2]; dgain_ref[...]+=acc[3]
        return 0
    lax.fori_loop(0,NB//UN,pre,0)
    def unused(b,_):
        zs[b]=zfl; es[b]=zfl; dws[b]=jnp.zeros((F,C),bf)
        return 0
    lax.fori_loop(counts[0]+counts[1],NB,unused,0)
    for s in range(2):
        wst[s]=jnp.zeros((F,C),f32); bst[s]=zfl
    steps=jnp.maximum(counts[0],counts[1])
    gain2=jnp.concatenate([gain_ref[...]]*2,axis=1)
    def step(j,_):
        i=steps-1-j
        bs=[jnp.where(i<counts[s],offs[s]+i,NB) for s in range(2)]
        both=lambda ref: jnp.concatenate([ref[b] for b in bs],axis=1)
        w=[wst[s] for s in range(2)]; bias=[bst[s] for s in range(2)]
        w2=[split2(x) for x in w]
        xx=[two_rows(dot_nn(w2[s],kqt[bs[s],:,0:L])) for s in range(2)]
        x=jnp.concatenate(xx,axis=1)+jnp.concatenate(bias,axis=1)+both(xs)
        for s in range(2): dws[bs[s]]=w2[s][:F]
        g=both(gs); n=both(ns); p=both(ps_)*gain2; row=both(rows)
        inv=row[0:1]; mpn=row[1:2]
        h=-both(rate)*x
        da=inv*h
        m1=mean0(da*n); m2=mean0(da); m3=mean0(h*g)
        dp=da-m2-n*m1
        de=dp*gain2
        dn=de*gain2-da*mpn-p*m1
        dz=inv*(dn-mean0(dn)-n*(mean0(dn*n)+m3))
        dr=[rs[b] for b in bs]
        dzs=[dz[:,:L],dz[:,L:]]
        up=[dot_nn(jnp.concatenate([dzs[s],dr[s]],axis=1).astype(bf),kq[bs[s]]) for s in range(2)]
        ub=[dot_nn((dzs[s]+dr[s]).astype(bf),onesbd) for s in range(2)]
        out=-jnp.sum(g*x,axis=0,keepdims=True)*row[2:3]
        for s in range(2):
            wst[s]=w[s]+up[s]; bst[s]=bias[s]+ub[s]
            zs[bs[s]]=dzs[s]; es[bs[s]]=dp[:,s*L:(s+1)*L]
            rows[bs[s],3:4,:]=out[:,s*L:(s+1)*L]
        return 0
    lax.fori_loop(0,steps,step,0)
    for h in range(H):
        dw0_ref[h]=(wst[0,:,h*F:(h+1)*F]+wst[1,:,h*F:(h+1)*F]).T
    db0h_ref[...]=gather_heads(bst[0]+bst[1],jnp.where(lane_iota((H,L),1)%MB==0,rep,0.0))
    def post_one(b):
        r=row_of(where,b,PER)
        dp=es[b]; row=rows[b]
        de=dp*gain_ref[...]
        dgain=dp*ps_[b]+de*ns[b]
        gr=(gs[b]*rate[b])
        drb=rs[b].astype(bf); grb=gr.astype(bf); dzb=zs[b].astype(bf)
        dst=jnp.where(keep,-dot_tn(grb,drb),0.0).astype(bf)
        dss=jnp.where(keep_t,-dot_tn(drb,grb),0.0).astype(bf)
        wt=wt_ref[b]
        kb=kq[b,0:L,:]; qb=kq[b,L:2*L,:]
        dqf=dot_tn(jnp.concatenate([drb,dst],axis=0),jnp.concatenate([wt,kb],axis=0))
        dkf=dot_tn(jnp.concatenate([dzb,(-gr).astype(bf),dss],axis=0),jnp.concatenate([wt,dws[b],qb],axis=0))
        det=de.T; dit=ios[b].T
        for h in range(H):
            rr=slice(h*MB,(h+1)*MB); cc=slice(h*F,(h+1)*F)
            dqkv_ref[pl.ds(r,MB),h*F:(h+1)*F]=(dqf[rr,cc]+dit[rr,:]).astype(bf)
            dqkv_ref[pl.ds(r,MB),C+h*F:C+(h+1)*F]=(dkf[rr,cc]+det[rr,:]).astype(bf)
            dqkv_ref[pl.ds(r,MB),2*C+h*F:2*C+(h+1)*F]=(-det[rr,:]).astype(bf)
        drl_ref[pl.ds(r,MB),:]=jnp.where(pick,row[3:4],0.0)
        return dgain,de
    def post(i,_):
        acc=None
        for u in range(UN):
            x=post_one(i*UN+u)
            acc=x if acc is None else tuple(a+c for a,c in zip(acc,x))
        dgain_ref[...]+=acc[0]; dshift_ref[...]+=acc[1]
        return 0
    lax.fori_loop(0,NB//UN,post,0)
    dgainh_ref[...]=gather_heads(dgain_ref[...],rep); dshifth_ref[...]=gather_heads(dshift_ref[...],rep)
    dpgh_ref[...]=gather_heads(dpg_ref[...],rep); dpsh_ref[...]=gather_heads(dps_ref[...],rep)
    drlh_ref[...]=lax.dot_general(drl_ref[...],rep,(((1,),(1,)),((),())),precision=HIGH,preferred_element_type=f32).astype(bf)

VM=pl.BlockSpec(memory_space=pltpu.VMEM); SM=pl.BlockSpec(memory_space=pltpu.SMEM)

def mixer_fwd(where,per,q,k,v,g,rl,w0,b0,gain,shift,pg,ps,UN=3):
    T,C=q.shape; H,F=b0.shape; L=H*MB; NB=T//MB
    S=jax.ShapeDtypeStruct
    fl=pltpu.VMEM((F,L),f32)
    return pl.pallas_call(functools.partial(fwd_kernel,UN,per),
        out_shape=[S((T,C),bf),S((T,C),bf),S((NB+1,F,L),f32),S((NB+1,F,L),f32),S((NB+1,F,C),bf),S((NB,L,L),bf)],
        in_specs=[SM]+[VM]*11,out_specs=[VM]*6,
        scratch_shapes=[pltpu.VMEM((NB+1,2*L,C),bf),pltpu.VMEM((NB+1,C,2*L),bf),pltpu.VMEM((NB+1,F,L),f32),pltpu.VMEM((NB+1,1,L),f32),
            pltpu.VMEM((NB+1,L,2*L),bf),pltpu.VMEM((2,F,C),f32),pltpu.VMEM((2,F,L),f32),pltpu.VMEM((T,L),f32),fl,fl,fl,fl],
        cost_estimate=cost(28),
        name='mixer_forward')(where,q,k,v,g,rl,w0,b0,gain,shift,pg,ps)

def mixer_bwd(where,per,q,k,v,g,rl,dm,zt,rt,wt,mt,gain,shift,pg,ps,UN=3):
    T,C=q.shape; H,F=gain.shape; L=H*MB; NB=T//MB
    S=jax.ShapeDtypeStruct
    fls=pltpu.VMEM((NB+1,F,L),f32); fl=pltpu.VMEM((F,L),f32)
    return pl.pallas_call(functools.partial(bwd_kernel,UN,per),
        out_shape=[S((T,3*C),bf),S((T,H),bf),S((H,F,F),f32)]+[S((H,F),f32)]*5,
        in_specs=[SM]+[VM]*14,out_specs=[VM]*8,
        scratch_shapes=[pltpu.VMEM((NB+1,2*L,C),bf),pltpu.VMEM((NB+1,C,2*L),bf),pltpu.VMEM((NB+1,1,L),f32)]+[fls]*6+[
            pltpu.VMEM((NB+1,8,L),f32),fls,fls,pltpu.VMEM((NB+1,F,C),bf),pltpu.VMEM((2,F,C),f32),pltpu.VMEM((2,F,L),f32),
            pltpu.VMEM((T,L),f32)]+[fl]*8+[pltpu.VMEM((T,L),f32)],
        cost_estimate=cost(33),
        name='mixer_backward')(where,q,k,v,g,rl,dm,zt,rt,wt,mt,gain,shift,pg,ps)


def cost(us):
    return pl.CostEstimate(flops=int(us * 1e9), bytes_accessed=int(us * 1e6), transcendentals=0)


def whole(x):
    return pl.BlockSpec(x.shape, lambda *_: (0,) * x.ndim)


SDS = jax.ShapeDtypeStruct


def project_kernel(nh, where, x_ref, gain_ref, wq, wk, wv, wg, wr, xn, q, k, v, g, rl):
    n = x_ref.shape[0] // nh

    @pl.when(pl.program_id(0) == 0)
    def _():
        for r in range(nh):
            x = x_ref[pl.ds(pl.multiple_of((where[0] ^ r) * n, MB), n), :].astype(f32)
            inv = lax.rsqrt(jnp.mean(x * x, axis=-1, keepdims=True) + EPS)
            xn[r * n : (r + 1) * n, :] = (gain_ref[...] * (x * inv)).astype(bf)
        rl[...] = dot_nt(xn[...], wr[...])

    for w, o in ((wq, q), (wk, k), (wv, v), (wg, g)):
        o[...] = dot_nn(xn[...], w[...]).astype(bf)


def project(nh, where, x, gain, weights, wr, tile=256):
    T, D = x.shape
    C, H = weights[0].shape[1], wr.shape[0]
    col = pl.BlockSpec((D, tile), lambda j: (0, j))
    out = pl.BlockSpec((T, tile), lambda j: (0, j))
    return pl.pallas_call(
        functools.partial(project_kernel, nh),
        grid=(C // tile,),
        in_specs=[SM, whole(x), whole(gain)] + [col] * 4 + [whole(wr)],
        out_specs=[pl.BlockSpec((T, D), lambda j: (0, 0))] + [out] * 4 + [pl.BlockSpec((T, H), lambda j: (0, 0))],
        out_shape=[SDS((T, D), bf)] + [SDS((T, C), bf)] * 4 + [SDS((T, H), f32)],
        cost_estimate=cost(8),
        name="project",
    )(where, x, gain, *weights, wr)


def split_kernel(kinds, more, *refs):
    n = len(kinds)
    acc = None
    for turned, a, b in zip(kinds, refs[:n], refs[n : 2 * n]):
        y = (dot_nt if turned else dot_nn)(a[...], b[...])
        acc = y if acc is None else acc + y
    extra, outs = refs[2 * n : 2 * n + more], refs[2 * n + more :]
    rows = outs[0].shape[0]
    for r, o in enumerate(outs):
        o[:rows, :] = acc[r * rows : (r + 1) * rows].astype(o.dtype)
        if 0 < r <= more:
            o[rows:, :] = extra[r - 1][...]


def split_product(nh, terms, name, us, extra=(), tile=512):
    T = terms[0][0].shape[-2]
    D = terms[0][1].shape[0 if terms[0][2] else 1]
    a_specs, b_specs = [], []
    for a, b, turned, col in terms:
        depth = b.shape[1 if turned else 0]
        if a.ndim == 3:
            a_specs.append(pl.BlockSpec((None, T, depth), lambda j, col=col: (col, 0, 0)))
        else:
            a_specs.append(pl.BlockSpec((T, depth), lambda j, col=col: (0, col)))
        b_specs.append(
            pl.BlockSpec((tile, depth), lambda j: (j, 0)) if turned else pl.BlockSpec((depth, tile), lambda j: (0, j))
        )
    n = T // nh
    rows = [2 * n if 0 < r <= len(extra) else n for r in range(nh)]
    return pl.pallas_call(
        functools.partial(split_kernel, [t[2] for t in terms], len(extra)),
        grid=(D // tile,),
        in_specs=a_specs + b_specs + [pl.BlockSpec((n, tile), lambda j: (0, j))] * len(extra),
        out_specs=[pl.BlockSpec((m, tile), lambda j: (0, j)) for m in rows],
        out_shape=[SDS((m, D), bf if r else f32) for r, m in enumerate(rows)],
        cost_estimate=cost(us),
        name=name,
    )(*[t[0] for t in terms], *[t[1] for t in terms], *extra)


def lay(target, arrays, plan):
    rows = target.shape[0] // len(plan)
    for i, (a, at) in enumerate(plan):
        target[i * rows : (i + 1) * rows, :] = arrays[a][at : at + rows, :]


def rows_kernel(*refs):
    out = refs[-1]
    n = refs[0].shape[0]
    for i, x in enumerate(refs[:-1]):
        out[i * n : (i + 1) * n, :] = x[...]


def top_rows(arrays, n):
    D = arrays[0].shape[1]
    return pl.pallas_call(
        rows_kernel,
        grid=(1,),
        in_specs=[pl.BlockSpec((n, D), lambda i: (0, 0))] * len(arrays),
        out_specs=pl.BlockSpec((n * len(arrays), D), lambda i: (0, 0)),
        out_shape=SDS((n * len(arrays), D), arrays[0].dtype),
        cost_estimate=cost(2),
        name="top_rows",
    )(*arrays)


def chunk_of(T):
    return T if T <= 576 else max(c for c in range(MB, 577, MB) if T % c == 0)


def feed_grad_kernel(many, chunk, *refs):
    w, back, flat = refs[many:]

    @pl.when(pl.program_id(0) == 0)
    def _():
        at = 0
        for a in refs[:many]:
            flat[at : at + a.shape[0], :] = a[...]
            at += a.shape[0]

    def body(i, _):
        rows = pl.ds(pl.multiple_of(i * chunk, MB), chunk)
        back[rows, :] = dot_nt(flat[rows, :], w[...]).astype(bf)
        return 0

    lax.fori_loop(0, back.shape[0] // chunk, body, 0)


def feed_grad(arrays, w, name, us, tile=512):
    T = sum(x.shape[0] for x in arrays)
    N, D = w.shape
    return pl.pallas_call(
        functools.partial(feed_grad_kernel, len(arrays), chunk_of(T)),
        grid=(pl.cdiv(N, tile),),
        in_specs=[whole(x) for x in arrays] + [pl.BlockSpec((tile, D), lambda j: (j, 0))],
        out_specs=pl.BlockSpec((T, tile), lambda j: (0, j)),
        out_shape=SDS((T, N), bf),
        scratch_shapes=[pltpu.VMEM((T, D), bf)],
        cost_estimate=cost(us),
        name=name,
    )(*arrays, w)


def feed_kernel(plan, many, chunk, *refs):
    arrays, backs = refs[:many], refs[many:-5]
    wg, wu, flat, out, grads = refs[-5:]

    @pl.when(pl.program_id(0) == 0)
    def _():
        lay(flat, arrays, plan)

    at = 0
    for b in backs:
        grads[at : at + b.shape[0], :] = b[...]
        at += b.shape[0]

    def body(i, _):
        rows = pl.ds(pl.multiple_of(i * chunk, MB), chunk)
        gate = dot_nt(flat[rows, :], wg[...])
        up = dot_nt(flat[rows, :], wu[...])
        grad = grads[rows, :].astype(f32)
        sig = jax.nn.sigmoid(gate)
        silu = gate * sig
        out[0, rows, :] = (grad * up * sig * (1.0 + gate * (1.0 - sig))).astype(bf)
        out[1, rows, :] = (grad * silu).astype(bf)
        out[2, rows, :] = (silu * up).astype(bf)
        return 0

    lax.fori_loop(0, flat.shape[0] // chunk, body, 0)


def feed(n, plan, arrays, backs, wg, wu, name, us, tile=512):
    T = n * len(plan)
    N, D = wg.shape
    row = pl.BlockSpec((tile, D), lambda j: (j, 0))
    return pl.pallas_call(
        functools.partial(feed_kernel, plan, len(arrays), chunk_of(T)),
        grid=(pl.cdiv(N, tile),),
        in_specs=[whole(x) for x in arrays]
        + [pl.BlockSpec((x.shape[0], tile), lambda j: (0, j)) for x in backs]
        + [row, row],
        out_specs=[pl.BlockSpec((T, D), lambda j: (0, 0)), pl.BlockSpec((3, T, tile), lambda j: (0, 0, j))],
        out_shape=[SDS((T, D), bf), SDS((3, T, N), bf)],
        scratch_shapes=[pltpu.VMEM((T, tile), bf)],
        cost_estimate=cost(us),
        name=name,
    )(*arrays, *backs, wg, wu)


def feed_blocks_kernel(plans, many, begun, *refs):
    xs, ns = refs[1 : 1 + many], refs[1 + many : 1 + many + len(plans)]
    give, keep = refs[-2:]
    y = None
    for plan, m in zip(plans, ns):
        x = jnp.concatenate([xs[i][...] for i in plan], axis=0)
        p = dot_tn(x, m[...])
        y = p if y is None else y + p
    y = y.T

    @pl.when(pl.program_id(1) == 0)
    def _():
        give[...] = (y + refs[-4][...] if begun else y).astype(give.dtype)

    @pl.when(pl.program_id(1) == 1)
    def _():
        keep[...] = y + refs[-3][...] if begun else y


def feed_blocks(where, nz, xs, plans, ns, first, layers, wide, name, us, begun=(), kind=bf):
    N = ns[0].shape[2]
    x_specs = [
        pl.BlockSpec((x.shape[0], wide), lambda w, b, where: (0, where[3 + nz * (1 - b)])) for x in xs
    ]
    n_specs = [pl.BlockSpec((None, m.shape[1], N), lambda w, b, where: (first + w, 0, 0)) for m in ns]
    out = pl.BlockSpec((None, N, wide), lambda w, b, where: (w, 0, 0))
    return pl.pallas_call(
        functools.partial(feed_blocks_kernel, plans, len(xs), len(begun)),
        grid_spec=pltpu.PrefetchScalarGridSpec(
            num_scalar_prefetch=1,
            grid=(layers, 2),
            in_specs=x_specs + n_specs + [out] * len(begun),
            out_specs=[out, out],
        ),
        out_shape=[SDS((layers, N, wide), kind), SDS((layers, N, wide), f32)],
        cost_estimate=cost(us),
        name=name,
    )(where, *xs, *ns, *begun)


def branch_kernel(n, *refs):
    pieces = refs[:n]
    w, slope, flat, mg, dg = refs[n:]

    @pl.when(pl.program_id(0) == 0)
    def _():
        rows = flat.shape[0] // n
        for i, a in enumerate(pieces):
            flat[i * rows : (i + 1) * rows, :] = a[:rows, :]

    y = dot_nt(flat[...], w[...])
    mg[...] = y.astype(bf)
    dg[...] = (y * slope[...].astype(f32)).astype(bf)


def branch_back(pieces, n, w, slope, tile=256):
    T, C = slope.shape
    D = w.shape[1]
    out = pl.BlockSpec((T, tile), lambda j: (0, j))
    return pl.pallas_call(
        functools.partial(branch_kernel, len(pieces)),
        grid=(C // tile,),
        in_specs=[whole(x) for x in pieces] + [pl.BlockSpec((tile, D), lambda j: (j, 0)), out],
        out_specs=[pl.BlockSpec((T, D), lambda j: (0, 0)), out, out],
        out_shape=[SDS((T, D), bf), SDS((T, C), bf), SDS((T, C), bf)],
        cost_estimate=cost(4),
        name="branch_back",
    )(*pieces, w, slope)


def blocks_kernel(groups, turned, *refs):
    refs = refs[1:]
    n = sum(groups)
    xs, ns, outs = refs[:n], refs[n : 2 * n], refs[2 * n :]
    parts, at = [], 0
    for count in groups:
        y = None
        for i in range(at, at + count):
            p = dot_tn(xs[i][...], ns[i][...])
            y = p if y is None else y + p
        parts.append(y)
        at += count
    for k, o in enumerate(outs):
        @pl.when(pl.program_id(0) == k)
        def _(o=o):
            at = 0
            for y in parts:
                if turned:
                    o[at : at + y.shape[1], :] = y.T.astype(o.dtype)
                else:
                    o[:, at : at + y.shape[1]] = y.astype(o.dtype)
                at += y.shape[1]


def block_products(where, stride, groups, kinds, wide, name, us, turned=False):
    xs = [x for group in groups for x, _ in group]
    ns = [n for group in groups for _, n in group]
    N = sum(group[0][1].shape[1] for group in groups)
    x_specs = [pl.BlockSpec((x.shape[0], wide), lambda k, where: (0, where[3 + stride * k])) for x in xs]
    n_specs = [pl.BlockSpec(n.shape, lambda k, where: (0, 0)) for n in ns]
    shape = (N, wide) if turned else (wide, N)
    return pl.pallas_call(
        functools.partial(blocks_kernel, [len(group) for group in groups], turned),
        grid_spec=pltpu.PrefetchScalarGridSpec(
            num_scalar_prefetch=1,
            grid=(len(kinds),),
            in_specs=x_specs + n_specs,
            out_specs=[pl.BlockSpec(shape, lambda k, where: (0, 0))] * len(kinds),
        ),
        out_shape=[SDS(shape, kind) for kind in kinds],
        cost_estimate=cost(us),
        name=name,
    )(where, *xs, *ns)


def natural_kernel(n, plans, many, where, *refs):
    for plan, out in zip(plans, refs[many:]):
        for r, (i, at) in enumerate(plan):
            out[pl.ds(pl.multiple_of((where[0] ^ r) * n, MB), n), :] = refs[i][at : at + n, :]


def natural(where, arrays, n, plans):
    D = arrays[0].shape[1]
    return pl.pallas_call(
        functools.partial(natural_kernel, n, plans, len(arrays)),
        in_specs=[SM] + [VM] * len(arrays),
        out_specs=[VM] * len(plans),
        out_shape=[SDS((n * len(plan), D), arrays[0].dtype) for plan in plans],
        cost_estimate=cost(0.2),
        name="natural",
    )(where, *arrays)


def join_kernel(one, by_two, two, by_one, for_one, for_two):
    n = by_two.shape[0]
    for_one[:n, :] = (one[:n, :].astype(f32) + by_two[...].astype(f32)).astype(bf)
    for_one[n:, :] = one[n:, :]
    for_two[:n, :] = two[:n, :]
    for_two[n:, :] = (two[n:, :].astype(f32) + by_one[...].astype(f32)).astype(bf)


def join(one, by_two, two, by_one):
    return pl.pallas_call(
        join_kernel,
        in_specs=[VM] * 4,
        out_specs=[VM] * 2,
        out_shape=[SDS(one.shape, bf), SDS(two.shape, bf)],
        cost_estimate=cost(1),
        name="join",
    )(one, by_two, two, by_one)


def add_rows(x, row):
    high = row.astype(bf)
    low = (row - high.astype(f32)).astype(bf)
    rest = jnp.zeros((MB - 2, row.shape[0]), bf)
    return jnp.concatenate([x, high[None], low[None], rest], axis=0)


def last_rows(x):
    return x[-MB].astype(f32) + x[1 - MB].astype(f32)


def after(x, *others):
    return lax.optimization_barrier((x, others))[0]


def rms_inv(x):
    return lax.rsqrt(jnp.mean(x * x, axis=-1, keepdims=True) + EPS)


class Links:
    def __init__(self, mesh):
        self.nh = mesh.shape["head"]
        self.nq = mesh.shape["seq"]
        self.nz = self.nq // 2
        self.turns = tuple(range(self.nh - 1, 0, -1))

    def place(self):
        self.h = lax.axis_index("head")
        self.s = lax.axis_index("seq")
        self.c = self.s % 2
        self.z = self.s // 2

    def partner(self, x, r):
        return lax.ppermute(x, "head", [(i, i ^ r) for i in range(self.nh)])

    def sibling(self, x):
        return lax.ppermute(x, "seq", [(i, i ^ 1) for i in range(self.nq)])

    def along(self, x, k):
        n = self.nz
        return lax.ppermute(x, "seq", [(2 * p + c, 2 * ((p + k) % n) + c) for p in range(n) for c in range(2)])

    def head_sum(self, parts, hold=()):
        got = [after(self.partner(parts[r], r), *hold) for r in self.turns]
        total = parts[0]
        for x in got:
            total = total + x.astype(f32)
        return total

    def head_pieces(self, x):
        got = {r: self.partner(x, r) for r in self.turns}
        return [x] + [got[r] for r in range(1, self.nh)]

    def paired_start(self, parts, across, hold):
        if self.nh != 4:
            return parts[1:]
        by_two = after(self.partner(parts[3], 2), hold)
        by_one = after(self.partner(across, 1), hold)
        return join(parts[1], by_two, parts[2], by_one)

    def paired_pieces(self, x):
        if self.nh != 4:
            return self.head_pieces(x)
        return [x, self.partner(x, 1), self.partner(x, 2)]

    def paired_rest(self, pieces, n):
        if self.nh != 4:
            return pieces, tuple((r, 0) for r in range(self.nh)), tuple((r, n) for r in range(self.nh))
        upper, lower = self.partner(pieces[1][:n], 2), self.partner(pieces[2][n:], 1)
        return pieces + [upper, lower], ((0, 0), (1, 0), (2, 0), (3, 0)), ((0, n), (1, n), (2, n), (4, 0))

    def line_sum(self, parts):
        got = [self.along(parts[k], k) for k in self.line_order()]
        total = parts[0]
        for x in got:
            total = total + x.astype(f32)
        return total

    def line_order(self):
        half = self.nz // 2
        return sorted(range(1, self.nz), key=lambda k: abs(k - half))

    def ring(self, x):
        out = []
        for _ in range(1, self.nz):
            x = self.along(x, 1)
            out.append(x)
        return out

    def ring_sum(self, parts):
        total = parts[self.nz - 1]
        for k in range(self.nz - 2, -1, -1):
            total = parts[k] + self.along(total, 1).astype(f32)
            total = total if k == 0 else total.astype(bf)
        return total

    def relative(self, x):
        n = x.shape[0] // self.nh
        return jnp.concatenate(
            [lax.dynamic_slice_in_dim(x, (self.h ^ r) * n, n, axis=0) for r in range(self.nh)], axis=0
        )


def per_device(
    links,
    inputs,
    lengths,
    first_gain,
    query_weight,
    key_weight,
    value_weight,
    gate_weight,
    rate_weight,
    inner_weight,
    inner_offset,
    inner_gain,
    inner_shift,
    post_gain,
    post_shift,
    out_weight,
    second_gain,
    feed_gate,
    feed_up,
    feed_down,
    out_grad,
):
    links.place()
    nh, nz, nq = links.nh, links.nz, links.nq
    spot = jnp.arange(4 + nz, dtype=jnp.int32)
    cols = 2 * lax.rem(links.z + spot + (nz - 3), nz) + links.c
    cols = jnp.where(spot == 3 + nz, 2 * links.z + 1 - links.c, cols)
    spread = lax.pad(lengths.reshape(-1), jnp.int32(0), [(1, nz + 1, 0)])
    where = jnp.where(spot == 0, links.h, jnp.where(spot < 3, spread, cols))
    n = inputs.shape[0] // nh
    per = n // MB
    wide = inputs.shape[1] // nq
    heads, width = inner_offset.shape
    C = heads * width
    pg, ps = post_gain[None], post_shift[None]
    rate_turned = rate_weight.T
    feed_gate, feed_up = feed_gate.T, feed_up.T

    grad_rel = links.relative(out_grad)
    straight = [0] + list(range(3, nh))
    steps = nz - 1
    grad_ring = [links.along(jnp.concatenate([grad_rel[:n], grad_rel[3 * n :]], axis=0), 1)]
    normed_one, query, key, value, gate, rate_logit = project(
        nh, where, inputs, first_gain[None], (query_weight, key_weight, value_weight, gate_weight), rate_turned
    )
    mixed, slope, zt, rt, wt, mt = mixer_fwd(
        where, per, query, key, value, gate, rate_logit, inner_weight, inner_offset, inner_gain, inner_shift, pg, ps
    )
    own_source = lax.dynamic_slice_in_dim(inputs, links.h * n, n, axis=0).astype(f32)
    own_upstream = grad_rel[:n].astype(f32)

    mixed = after(mixed, grad_ring[0])
    for k in range(2, nz):
        grad_ring.append(links.along(grad_ring[-1], 1))
    out_parts = split_product(nh, [(mixed, out_weight, False, 0)], "out_product", 4, tile=1024)
    backs = [feed_grad([after(grad_ring[0], out_parts[0])], feed_down, "feed_grad_first", 1)]
    back_own = feed_grad([after(grad_rel, backs[0])], feed_down, "feed_grad_own", 1)
    hidden = own_source + links.head_sum(out_parts, (back_own,))
    r2 = rms_inv(hidden)
    two_own = (second_gain * (hidden * r2)).astype(bf)
    twos = links.head_pieces(two_own)
    for k in range(1, steps - 1):
        backs.append(feed_grad([after(grad_ring[k], two_own)], feed_down, "feed_grad_next", 1))
    twos[1:] = [after(x, backs[-1], grad_ring[-1]) for x in twos[1:]]
    grad_across = top_rows([after(grad_ring[0], *twos[1:]), *grad_ring[1:]], n)
    grad_across = [links.partner(grad_across, r) for r in (1, 2)]
    own_plan = tuple((r, 0) for r in range(nh))
    normed_two, feed_own = feed(n, own_plan, twos, [back_own], feed_gate, feed_up, "feed_own", 4)
    two_ring = [links.along(after(jnp.concatenate([twos[r] for r in straight], axis=0), *twos[1:]), 1)]
    back_parts = split_product(
        nh, [(feed_own, feed_gate, False, 0), (feed_own, feed_up, False, 1)], "feed_back", 3
    )
    two_ring[0] = after(two_ring[0], back_parts[0])
    for k in range(2, nz):
        two_ring.append(links.along(two_ring[-1], 1))
    back_parts = [back_parts[0]] + [after(x, two_ring[0], *grad_across) for x in back_parts[1:]]
    down_parts = list(split_product(nh, [(after(feed_own, back_parts[0]), feed_down, False, 2)], "feed_down", 1, tile=1024))
    last_grads = [grad_ring[-1], *grad_across]
    backs.append(feed_grad([after(last_grads[0], down_parts[0]), *last_grads[1:]], feed_down, "feed_grad_last", 1, tile=256))
    two = links.head_sum(back_parts, (backs[-1], two_ring[1]))
    u = two * second_gain
    hidden_grad = own_upstream + r2 * u - hidden * (r2 * r2 * r2) * jnp.mean(u * hidden, axis=-1, keepdims=True)
    second_part = jnp.sum(two * hidden * r2, axis=0)
    pieces = links.head_pieces(add_rows(hidden_grad.astype(bf), second_part))
    parts = range(len(straight))
    plan = tuple((k, i * n) for k in range(steps - 1) for i in parts)
    held = [after(two_ring[0], pieces[0]), *two_ring[1:-1]]
    first = feed(n, plan, held, backs[:-1], feed_gate, feed_up, "feed_first", 1)
    begun = feed_blocks(
        where, nz, [normed_two, first[0]], ((0,), (1,)), [feed_own, first[1]], 0, 2, wide, "feed_in_begin", 0.5, kind=f32
    )
    pieces[1:] = [after(x, begun[1]) for x in pieces[1:]]
    second_part = (second_part, pieces[1:])
    pieces[0] = after(pieces[0], two_ring[-1])
    branch_grad, mixed_grad, dg = branch_back(pieces, n, out_weight, slope)
    across = top_rows(two_ring, n)
    across = [links.partner(across, r) for r in (1, 2)]

    one_sib = links.sibling(normed_one)
    groups = [
        [(normed_one, dg), (one_sib, links.sibling(dg))],
        [(branch_grad, mixed), (links.sibling(branch_grad), links.sibling(mixed))],
    ]
    pair = block_products(where, 1, groups, [f32] + [bf] * (nz - 1), wide, "gate_out_blocks", 8)
    pair_got = {k: links.along(pair[k], k) for k in (2, 1)}

    dqkv, drate, dw0, db0, dgain, dshift, dpg, dps = mixer_bwd(
        where, per, query, key, value, gate, rate_logit, after(mixed_grad, pair[0]),
        zt, rt, wt, mt, inner_gain, inner_shift, pg, ps
    )
    dqkv = after(dqkv, pair_got[2], *across)
    for k in range(3, nz):
        pair_got[k] = links.along(after(pair[k], dqkv), k)
    drate_low = drate
    dqkv_sib = links.sibling(dqkv)
    back_parts = split_product(
        nh,
        [
            (dqkv, query_weight, True, 0),
            (dqkv, key_weight, True, 1),
            (dqkv, value_weight, True, 2),
            (dg, gate_weight, True, 0),
            (drate_low, rate_turned, False, 0),
        ],
        "input_back",
        8,
        extra=down_parts[1 : 3 if nh == 4 else nh],
    )
    groups = [[(normed_one, after(dqkv, back_parts[0])), (one_sib, dqkv_sib)]]
    trio = block_products(where, 1, groups, [f32] + [bf] * (nz - 1), wide, "qkv_blocks", 8)
    parts_two = links.paired_start(back_parts, down_parts[3], (trio[0], pair_got[1]))
    trio_step = links.along(trio[-1], 1)

    plan = tuple((0, i * n) for i in parts) + tuple((1 + i, k * n) for i in range(2) for k in range(steps))
    held = [after(two_ring[-1], trio[0], parts_two[0]), *across]
    second = feed(n, plan, held, backs[-1:], feed_gate, feed_up, "feed_second", 15, tile=256)

    def rows_of(x):
        return x.reshape(nq, -1)

    def heads_of(x):
        return x.reshape((heads, nq, -1)).transpose(1, 0, 2).reshape(nq, -1)

    received = [links.partner(x, r + 1) for r, x in enumerate(parts_two)]
    second, trio_step, received, pair_got = lax.optimization_barrier((second, trio_step, received, pair_got))
    send = (trio[nz - 2].astype(f32) + trio_step.astype(f32)).astype(bf)
    sums = jnp.concatenate([back_parts[0], down_parts[0]], axis=0)
    for x in received:
        sums = sums + x.astype(f32)
    one, output = sums[:n], hidden + sums[n:]
    r1 = rms_inv(own_source)
    w = one * first_gain
    input_grad = hidden_grad + r1 * w - own_source * (r1 * r1 * r1) * jnp.mean(w * own_source, axis=-1, keepdims=True)
    input_low = input_grad.astype(bf)
    first_part = jnp.sum(one * own_source * r1, axis=0)
    packed = add_rows(jnp.concatenate([input_low, output.astype(bf)], axis=0), first_part)
    got = links.along(send, 1)
    outs = [feed_own, first[1], second[1]]
    give, keep = feed_blocks(
        where, nz, [after(second[0], packed)], ((0,),), outs[2:], 0, 2, wide, "feed_in_blocks", 6, begun=begun
    )
    for k in range(nz - 3, 0, -1):
        send = (trio[k].astype(f32) + after(got, keep).astype(f32)).astype(bf)
        got = links.along(send, 1)
    pieces, send = lax.optimization_barrier((links.paired_pieces(packed), send))
    arrays, upper, lower = links.paired_rest(pieces, n)
    xs = [after(grad_rel, keep, send, pieces), *grad_ring, *grad_across]
    plans = ((0,), tuple(range(1, steps)), tuple(range(steps, len(xs))))
    first_give = give
    give, keep_out = feed_blocks(where, nz, xs, plans, outs, 2, 1, wide, "feed_out_blocks", 4)
    arrays[1:] = [after(x, keep_out) for x in arrays[1:]]
    input_grad, output = natural(where, arrays, n, (upper, lower))
    other = links.sibling(after(first_give, keep_out)).astype(f32)
    feed_grads = [keep[0] + other[0], keep[1] + other[1]]
    second_part, held = second_part
    second_part = second_part + sum(last_rows(after(x, keep_out)) for x in held)
    rate_part = lax.dot_general(
        after(normed_one, output), drate_low, (((0,), (0,)), ((), ())), preferred_element_type=f32
    )
    dw0, db0, dgain, dshift, dpg, dps = after((dw0, db0, dgain, dshift, dpg, dps), output)
    small = [rows_of(second_part), rows_of(rate_part), heads_of(dw0)]
    small += [heads_of(x) for x in (db0, dgain, dshift)] + [rows_of(dpg), rows_of(dps)]
    sizes = [x.shape[1] for x in small]
    small = jnp.concatenate(small, axis=1)
    got, small = lax.optimization_barrier((after(got, keep_out), small))
    grad_qkv = trio[0] + got.astype(f32)
    feed_grads.append(keep_out[0] + links.sibling(after(give[0], grad_qkv)).astype(f32))
    first_part = first_part + sum(last_rows(arrays[i]) for i, _ in lower[1:])
    sizes = [wide] + sizes
    small = jnp.concatenate([rows_of(first_part), small], axis=1).reshape(nz, 2, -1)
    keep = lax.dynamic_index_in_dim(small, links.c, 1, keepdims=False)
    give = lax.dynamic_index_in_dim(small, 1 - links.c, 1, keepdims=False)
    small = keep + links.sibling(give)
    small = links.line_sum([lax.dynamic_index_in_dim(small, lax.rem(links.z + k, nz), 0, keepdims=False) for k in range(nz)])
    pair = pair[0] + sum(x.astype(f32) for x in pair_got.values())
    ends = [sum(sizes[: i + 1]) for i in range(len(sizes))]
    small = [small[e - n : e] for e, n in zip(ends, sizes)]
    part = width // nq
    return (
        output,
        input_grad,
        small[0],
        grad_qkv[:, :C],
        grad_qkv[:, C : 2 * C],
        grad_qkv[:, 2 * C :],
        pair[:, :C],
        small[2].reshape(-1, heads),
        small[3].reshape(heads, part, width),
        small[4].reshape(heads, part),
        small[5].reshape(heads, part),
        small[6].reshape(heads, part),
        small[7],
        small[8],
        pair[:, C:].T,
        small[1],
        feed_grads[0].T,
        feed_grads[1].T,
        feed_grads[2],
    )


def solution(mesh):
    in_specs = (
        P("seq", None),
        P("seq", None),
        P(),
        P(None, "head"),
        P(None, "head"),
        P(None, "head"),
        P(None, "head"),
        P(None, "head"),
        P("head", None, None),
        P("head", None),
        P("head", None),
        P("head", None),
        P("head"),
        P("head"),
        P("head", None),
        P(),
        P(None, "head"),
        P(None, "head"),
        P("head", None),
        P("seq", None),
    )
    out_specs = (
        P("seq", None),
        P("seq", None),
        P("seq"),
        P("seq", "head"),
        P("seq", "head"),
        P("seq", "head"),
        P("seq", "head"),
        P("seq", "head"),
        P("head", "seq", None),
        P("head", "seq"),
        P("head", "seq"),
        P("head", "seq"),
        P(("head", "seq")),
        P(("head", "seq")),
        P("head", "seq"),
        P("seq"),
        P("seq", "head"),
        P("seq", "head"),
        P("head", "seq"),
    )
    return jax.shard_map(
        functools.partial(per_device, Links(mesh)), mesh=mesh, in_specs=in_specs, out_specs=out_specs, check_vma=False
    )
```

```python
import functools

import jax
import jax.numpy as jnp
from jax import lax
from jax.experimental import pallas as pl
from jax.experimental.pallas import tpu as pltpu
from jax.sharding import PartitionSpec as P

MB=16; EPS=1e-6
bf=jnp.bfloat16; f32=jnp.float32

def dot_nn(a,b): return lax.dot_general(a,b,(((1,),(0,)),((),())),preferred_element_type=f32)
def dot_nt(a,b): return lax.dot_general(a,b,(((1,),(1,)),((),())),preferred_element_type=f32)
def dot_tn(a,b): return lax.dot_general(a,b,(((0,),(0,)),((),())),preferred_element_type=f32)

def mean0(x): return jnp.mean(x,axis=0,keepdims=True)

def norm_parts(x):
    c=x-mean0(x)
    inv=lax.rsqrt(mean0(c*c)+EPS)
    return c*inv,inv

def norm_back(dy,n,inv):
    return inv*(dy-mean0(dy)-n*mean0(dy*n))

def split2(x):
    hi=x.astype(bf)
    return jnp.concatenate([hi,(x-hi.astype(f32)).astype(bf)],axis=0)

def two_rows(x):
    h=x.shape[0]//2
    return x[:h]+x[h:]

def stack_heads(rows,F):
    H=rows.shape[1]//F
    r=rows.astype(f32)
    return jnp.concatenate([r[:,h*F:(h+1)*F] for h in range(H)],axis=0).T

GC=0.7978845608028654; GA=0.044715
def gelu_parts(x):
    u=GC*(x+GA*x*x*x)
    t=jnp.tanh(u)
    val=0.5*x*(1.0+t)
    der=0.5*(1.0+t)+0.5*x*(1.0-t*t)*GC*(1.0+3.0*GA*x*x)
    return val,der

def plan_blocks(where):
    n0=(where[1]+MB-1)//MB; n1=(where[2]+MB-1)//MB
    return (n0,n1),(0,n0)

def row_of(where,b,per):
    return pl.multiple_of(((lax.div(b,per)^where[0])*per+lax.rem(b,per))*MB,MB)

def lane_iota(shape,dim): return lax.broadcasted_iota(jnp.int32,shape,dim)

def valid_row(where,offs,blk,L):
    pos=blk*MB+lane_iota((1,L),1)%MB
    a=(pos>=offs[0]*MB)&(pos<offs[0]*MB+where[1])
    b=(pos>=offs[1]*MB)&(pos<offs[1]*MB+where[2])
    return a|b

def fill_bd(dst,blk,rows,row0,F):
    H=rows.shape[1]//F
    for h in range(H):
        dst[blk,row0+h*MB:row0+(h+1)*MB,h*F:(h+1)*F]=rows[:,h*F:(h+1)*F]

def fill_turned(dst,blk,kt,qt):
    F,L=kt.shape
    both=jnp.concatenate([kt,qt],axis=1).astype(bf)
    lane=lane_iota((F,2*L),1)%L//MB
    for h in range(L//MB):
        dst[blk,h*F:(h+1)*F,:]=jnp.where(lane==h,both,jnp.zeros_like(both))

def same_head(L):
    return lane_iota((L,L),0)//MB==lane_iota((L,L),1)//MB

def head_lanes(H,L):
    return (lane_iota((H,L),0)==lane_iota((H,L),1)//MB).astype(f32)

HIGH=lax.Precision.HIGHEST
def head_rows(ref,F):
    return jnp.concatenate([ref[:,i:i+F] for i in range(0,ref.shape[1],F)],axis=0)
def spread(per_head,rep):
    return lax.dot_general(per_head,rep,(((0,),(0,)),((),())),precision=HIGH,preferred_element_type=f32)
def gather_heads(x,rep):
    return lax.dot_general(rep,x,(((1,),(1,)),((),())),precision=HIGH,preferred_element_type=f32)

def fwd_kernel(UN,PER,where,q_ref,k_ref,v_ref,g_ref,rlh_ref,w0_ref,b0_ref,gainh_ref,shifth_ref,pgh_ref,psh_ref,
               mixed_ref,slope_ref,zt_ref,rt_ref,wt_ref,mt_ref,
               kq,kqt,tt,rate,mtb,wst,bst,rl_ref,gain_ref,shift_ref,pg_ref,ps_ref):
    T,C=q_ref.shape; H,F=b0_ref.shape; L=H*MB; NB=T//MB
    rep=head_lanes(H,L)
    rl_ref[...]=lax.dot_general(rlh_ref[...],rep,(((1,),(0,)),((),())),precision=HIGH,preferred_element_type=f32)
    gain_ref[...]=spread(gainh_ref[...],rep); shift_ref[...]=spread(shifth_ref[...],rep)
    pg_ref[...]=spread(head_rows(pgh_ref,F),rep); ps_ref[...]=spread(head_rows(psh_ref,F),rep)
    counts,offs=plan_blocks(where)
    zero_kq=jnp.zeros((2*L,C),bf)
    onesbd=same_head(L).astype(f32).astype(bf)
    keep=same_head(L)&(lane_iota((L,L),0)<=lane_iota((L,L),1))
    pick=lane_iota((MB,L),0)==lane_iota((MB,L),1)%MB
    def clear(b,_):
        kq[b]=zero_kq
        return 0
    lax.fori_loop(0,NB+1,clear,0)
    kqt[NB]=jnp.zeros((C,2*L),bf)
    tt[NB]=jnp.zeros((F,L),f32); rate[NB]=jnp.zeros((1,L),f32); mtb[NB]=jnp.zeros((L,2*L),bf)
    def pre_one(b):
        r=row_of(where,b,PER)
        kn=k_ref[pl.ds(r,MB),:]; qn=q_ref[pl.ds(r,MB),:]; vn=v_ref[pl.ds(r,MB),:]
        fill_bd(kq,b,kn,0,F); fill_bd(kq,b,qn,L,F)
        kt=stack_heads(kn,F); qt=stack_heads(qn,F)
        tt[b]=stack_heads(vn,F)-kt
        fill_turned(kqt,b,kt,qt)
        ok=valid_row(where,offs,b,L)
        rl=jnp.sum(jnp.where(pick,rl_ref[pl.ds(r,MB),:],0.0),axis=0,keepdims=True)
        rate[b]=jnp.where(ok,jax.nn.sigmoid(rl)*(1.0/F),0.0)
        st=dot_nn(kq[b,0:L,:],kqt[b,:,L:2*L])
        m=jnp.where(keep,st+1.0,0.0).astype(bf)
        mt_ref[b]=m
        mtb[b,:,0:L]=m; mtb[b,:,L:2*L]=onesbd
    def pre(i,_):
        for u in range(UN): pre_one(i*UN+u)
        return 0
    lax.fori_loop(0,NB//UN,pre,0)
    def unused(b,_):
        rt_ref[b]=jnp.zeros((F,L),f32)
        zt_ref[b]=jnp.zeros((F,L),f32)
        wt_ref[b]=jnp.zeros((F,C),bf)
        return 0
    lax.fori_loop(counts[0]+counts[1],NB,unused,0)
    bias0=spread(b0_ref[...],rep)
    for h in range(H):
        wh=w0_ref[h].T
        for s in range(2): wst[s,:,h*F:(h+1)*F]=wh
    for s in range(2): bst[s]=bias0
    gain2=jnp.concatenate([gain_ref[...]]*2,axis=1); shift2=jnp.concatenate([shift_ref[...]]*2,axis=1)
    def step(i,_):
        bs=[jnp.where(i<counts[s],offs[s]+i,NB) for s in range(2)]
        w=[wst[s] for s in range(2)]; bias=[bst[s] for s in range(2)]
        w2=[split2(x) for x in w]
        zq=[two_rows(dot_nn(w2[s],kqt[bs[s]])) for s in range(2)]
        z=[zq[s][:,:L]+bias[s] for s in range(2)]
        for s in range(2):
            wt_ref[bs[s]]=w2[s][:F]; zt_ref[bs[s]]=z[s]
        zz=jnp.concatenate(z,axis=1)
        n,inv=norm_parts(zz)
        t2=jnp.concatenate([tt[b] for b in bs],axis=1)
        p=(n*gain2+shift2-t2)*gain2
        g=inv*(p-mean0(p)-n*mean0(p*n))
        g=g*jnp.concatenate([rate[b] for b in bs],axis=1)
        gr=[g[:,s*L:(s+1)*L].astype(bf) for s in range(2)]
        up=[dot_nn(gr[s],kq[bs[s],0:L,:]) for s in range(2)]
        for s in range(2): wst[s]=w[s]-up[s]
        ob=[dot_nn(gr[s],mtb[bs[s]]) for s in range(2)]
        for s in range(2):
            bst[s]=bias[s]-ob[s][:,L:]
            rt_ref[bs[s]]=zq[s][:,L:]+bias[s]-ob[s][:,:L]
        return 0
    lax.fori_loop(0,jnp.maximum(counts[0],counts[1]),step,0)
    def post_one(b):
        r=row_of(where,b,PER)
        qt=stack_heads(q_ref[pl.ds(r,MB),:],F); gt=stack_heads(g_ref[pl.ds(r,MB),:],F)
        nr,_=norm_parts(rt_ref[b])
        io=qt+nr*gain_ref[...]+shift_ref[...]
        ni,_=norm_parts(io)
        act,der=gelu_parts(gt)
        ok=valid_row(where,offs,b,L)
        lo=jnp.where(ok,ni*pg_ref[...]+ps_ref[...],0.0)
        m=(act*lo).T; sl=(der*lo).T
        for h in range(H):
            mixed_ref[pl.ds(r,MB),h*F:(h+1)*F]=m[h*MB:(h+1)*MB,:].astype(bf)
            slope_ref[pl.ds(r,MB),h*F:(h+1)*F]=sl[h*MB:(h+1)*MB,:].astype(bf)
    def post(i,_):
        for u in range(UN): post_one(i*UN+u)
        return 0
    lax.fori_loop(0,NB//UN,post,0)

def bwd_kernel(UN,PER,where,q_ref,k_ref,v_ref,g_ref,rlh_ref,dm_ref,zt_ref,rt_ref,wt_ref,mt_ref,gainh_ref,shifth_ref,pgh_ref,psh_ref,
               dqkv_ref,drlh_ref,dw0_ref,db0h_ref,dgainh_ref,dshifth_ref,dpgh_ref,dpsh_ref,
               kq,kqt,rate,ns,ps_,gs,xs,rs,ios,rows,zs,es,dws,wst,bst,rl_ref,gain_ref,shift_ref,pg_ref,ps_ref,
               dgain_ref,dshift_ref,dpg_ref,dps_ref,drl_ref):
    T,C=q_ref.shape; H,F=gainh_ref.shape; L=H*MB; NB=T//MB
    rep=head_lanes(H,L)
    rl_ref[...]=lax.dot_general(rlh_ref[...],rep,(((1,),(0,)),((),())),precision=HIGH,preferred_element_type=f32)
    gain_ref[...]=spread(gainh_ref[...],rep); shift_ref[...]=spread(shifth_ref[...],rep)
    pg_ref[...]=spread(head_rows(pgh_ref,F),rep); ps_ref[...]=spread(head_rows(psh_ref,F),rep)
    counts,offs=plan_blocks(where)
    zero_kq=jnp.zeros((2*L,C),bf)
    onesbd=same_head(L).astype(f32).astype(bf)
    keep=same_head(L)&(lane_iota((L,L),0)<=lane_iota((L,L),1))
    keep_t=same_head(L)&(lane_iota((L,L),1)<=lane_iota((L,L),0))
    pick=lane_iota((MB,L),0)==lane_iota((MB,L),1)%MB
    zfl=jnp.zeros((F,L),f32)
    def clear(b,_):
        kq[b]=zero_kq
        return 0
    lax.fori_loop(0,NB+1,clear,0)
    for ref in (ns,ps_,gs,xs,rs): ref[NB]=zfl
    kqt[NB]=jnp.zeros((C,2*L),bf)
    rate[NB]=jnp.zeros((1,L),f32); rows[NB]=jnp.zeros((8,L),f32)
    for ref in (dgain_ref,dshift_ref,dpg_ref,dps_ref): ref[...]=zfl
    def pre_one(b):
        r=row_of(where,b,PER)
        kn=k_ref[pl.ds(r,MB),:]; qn=q_ref[pl.ds(r,MB),:]
        fill_bd(kq,b,kn,0,F); fill_bd(kq,b,qn,L,F)
        kt=stack_heads(kn,F); qt=stack_heads(qn,F)
        t=stack_heads(v_ref[pl.ds(r,MB),:],F)-kt
        fill_turned(kqt,b,kt,kt)
        gt=stack_heads(g_ref[pl.ds(r,MB),:],F)
        dm=stack_heads(dm_ref[pl.ds(r,MB),:],F)
        ok=valid_row(where,offs,b,L)
        rl=jnp.sum(jnp.where(pick,rl_ref[pl.ds(r,MB),:],0.0),axis=0,keepdims=True)
        sg=jax.nn.sigmoid(rl)
        rt=jnp.where(ok,sg*(1.0/F),0.0)
        rate[b]=rt
        gain=gain_ref[...]; shift=shift_ref[...]
        n,inv=norm_parts(zt_ref[b])
        e=n*gain+shift-t
        p=e*gain
        mpn=mean0(p*n)
        g=inv*(p-mean0(p)-n*mpn)
        nr,invr=norm_parts(rt_ref[b])
        io=qt+nr*gain+shift
        ni,invi=norm_parts(io)
        act,_=gelu_parts(gt)
        dl=jnp.where(ok,dm*act,0.0)
        dio=norm_back(dl*pg_ref[...],ni,invi)
        dr=norm_back(dio*gain,nr,invr)
        drb=dr.astype(bf)
        ns[b]=n; ps_[b]=e; gs[b]=g; rs[b]=dr; ios[b]=dio
        xs[b]=dot_nt(drb,mt_ref[b])
        rows[b]=jnp.concatenate([inv,mpn,sg*(1.0-sg)*jnp.where(ok,1.0/F,0.0),jnp.zeros((5,L),f32)],axis=0)
        return dl,dl*ni,dio,dio*nr
    def pre(i,_):
        acc=None
        for u in range(UN):
            x=pre_one(i*UN+u)
            acc=x if acc is None else tuple(a+c for a,c in zip(acc,x))
        dps_ref[...]+=acc[0]; dpg_ref[...]+=acc[1]; dshift_ref[...]+=acc[2]; dgain_ref[...]+=acc[3]
        return 0
    lax.fori_loop(0,NB//UN,pre,0)
    def unused(b,_):
        zs[b]=zfl; es[b]=zfl; dws[b]=jnp.zeros((F,C),bf)
        return 0
    lax.fori_loop(counts[0]+counts[1],NB,unused,0)
    for s in range(2):
        wst[s]=jnp.zeros((F,C),f32); bst[s]=zfl
    steps=jnp.maximum(counts[0],counts[1])
    gain2=jnp.concatenate([gain_ref[...]]*2,axis=1)
    def step(j,_):
        i=steps-1-j
        bs=[jnp.where(i<counts[s],offs[s]+i,NB) for s in range(2)]
        both=lambda ref: jnp.concatenate([ref[b] for b in bs],axis=1)
        w=[wst[s] for s in range(2)]; bias=[bst[s] for s in range(2)]
        w2=[split2(x) for x in w]
        xx=[two_rows(dot_nn(w2[s],kqt[bs[s],:,0:L])) for s in range(2)]
        x=jnp.concatenate(xx,axis=1)+jnp.concatenate(bias,axis=1)+both(xs)
        for s in range(2): dws[bs[s]]=w2[s][:F]
        g=both(gs); n=both(ns); p=both(ps_)*gain2; row=both(rows)
        inv=row[0:1]; mpn=row[1:2]
        h=-both(rate)*x
        da=inv*h
        m1=mean0(da*n); m2=mean0(da); m3=mean0(h*g)
        dp=da-m2-n*m1
        de=dp*gain2
        dn=de*gain2-da*mpn-p*m1
        dz=inv*(dn-mean0(dn)-n*(mean0(dn*n)+m3))
        dr=[rs[b] for b in bs]
        dzs=[dz[:,:L],dz[:,L:]]
        up=[dot_nn(jnp.concatenate([dzs[s],dr[s]],axis=1).astype(bf),kq[bs[s]]) for s in range(2)]
        ub=[dot_nn((dzs[s]+dr[s]).astype(bf),onesbd) for s in range(2)]
        out=-jnp.sum(g*x,axis=0,keepdims=True)*row[2:3]
        for s in range(2):
            wst[s]=w[s]+up[s]; bst[s]=bias[s]+ub[s]
            zs[bs[s]]=dzs[s]; es[bs[s]]=dp[:,s*L:(s+1)*L]
            rows[bs[s],3:4,:]=out[:,s*L:(s+1)*L]
        return 0
    lax.fori_loop(0,steps,step,0)
    for h in range(H):
        dw0_ref[h]=(wst[0,:,h*F:(h+1)*F]+wst[1,:,h*F:(h+1)*F]).T
    db0h_ref[...]=gather_heads(bst[0]+bst[1],jnp.where(lane_iota((H,L),1)%MB==0,rep,0.0))
    def post_one(b):
        r=row_of(where,b,PER)
        dp=es[b]; row=rows[b]
        de=dp*gain_ref[...]
        dgain=dp*ps_[b]+de*ns[b]
        gr=(gs[b]*rate[b])
        drb=rs[b].astype(bf); grb=gr.astype(bf); dzb=zs[b].astype(bf)
        dst=jnp.where(keep,-dot_tn(grb,drb),0.0).astype(bf)
        dss=jnp.where(keep_t,-dot_tn(drb,grb),0.0).astype(bf)
        wt=wt_ref[b]
        kb=kq[b,0:L,:]; qb=kq[b,L:2*L,:]
        dqf=dot_tn(jnp.concatenate([drb,dst],axis=0),jnp.concatenate([wt,kb],axis=0))
        dkf=dot_tn(jnp.concatenate([dzb,(-gr).astype(bf),dss],axis=0),jnp.concatenate([wt,dws[b],qb],axis=0))
        det=de.T; dit=ios[b].T
        for h in range(H):
            rr=slice(h*MB,(h+1)*MB); cc=slice(h*F,(h+1)*F)
            dqkv_ref[pl.ds(r,MB),h*F:(h+1)*F]=(dqf[rr,cc]+dit[rr,:]).astype(bf)
            dqkv_ref[pl.ds(r,MB),C+h*F:C+(h+1)*F]=(dkf[rr,cc]+det[rr,:]).astype(bf)
            dqkv_ref[pl.ds(r,MB),2*C+h*F:2*C+(h+1)*F]=(-det[rr,:]).astype(bf)
        drl_ref[pl.ds(r,MB),:]=jnp.where(pick,row[3:4],0.0)
        return dgain,de
    def post(i,_):
        acc=None
        for u in range(UN):
            x=post_one(i*UN+u)
            acc=x if acc is None else tuple(a+c for a,c in zip(acc,x))
        dgain_ref[...]+=acc[0]; dshift_ref[...]+=acc[1]
        return 0
    lax.fori_loop(0,NB//UN,post,0)
    dgainh_ref[...]=gather_heads(dgain_ref[...],rep); dshifth_ref[...]=gather_heads(dshift_ref[...],rep)
    dpgh_ref[...]=gather_heads(dpg_ref[...],rep); dpsh_ref[...]=gather_heads(dps_ref[...],rep)
    drlh_ref[...]=lax.dot_general(drl_ref[...],rep,(((1,),(1,)),((),())),precision=HIGH,preferred_element_type=f32).astype(bf)

VM=pl.BlockSpec(memory_space=pltpu.VMEM); SM=pl.BlockSpec(memory_space=pltpu.SMEM)

def mixer_fwd(where,per,q,k,v,g,rl,w0,b0,gain,shift,pg,ps,UN=3):
    T,C=q.shape; H,F=b0.shape; L=H*MB; NB=T//MB
    S=jax.ShapeDtypeStruct
    fl=pltpu.VMEM((F,L),f32)
    return pl.pallas_call(functools.partial(fwd_kernel,UN,per),
        out_shape=[S((T,C),bf),S((T,C),bf),S((NB+1,F,L),f32),S((NB+1,F,L),f32),S((NB+1,F,C),bf),S((NB,L,L),bf)],
        in_specs=[SM]+[VM]*11,out_specs=[VM]*6,
        scratch_shapes=[pltpu.VMEM((NB+1,2*L,C),bf),pltpu.VMEM((NB+1,C,2*L),bf),pltpu.VMEM((NB+1,F,L),f32),pltpu.VMEM((NB+1,1,L),f32),
            pltpu.VMEM((NB+1,L,2*L),bf),pltpu.VMEM((2,F,C),f32),pltpu.VMEM((2,F,L),f32),pltpu.VMEM((T,L),f32),fl,fl,fl,fl],
        cost_estimate=cost(28),
        name='mixer_forward')(where,q,k,v,g,rl,w0,b0,gain,shift,pg,ps)

def mixer_bwd(where,per,q,k,v,g,rl,dm,zt,rt,wt,mt,gain,shift,pg,ps,UN=3):
    T,C=q.shape; H,F=gain.shape; L=H*MB; NB=T//MB
    S=jax.ShapeDtypeStruct
    fls=pltpu.VMEM((NB+1,F,L),f32); fl=pltpu.VMEM((F,L),f32)
    return pl.pallas_call(functools.partial(bwd_kernel,UN,per),
        out_shape=[S((T,3*C),bf),S((T,H),bf),S((H,F,F),f32)]+[S((H,F),f32)]*5,
        in_specs=[SM]+[VM]*14,out_specs=[VM]*8,
        scratch_shapes=[pltpu.VMEM((NB+1,2*L,C),bf),pltpu.VMEM((NB+1,C,2*L),bf),pltpu.VMEM((NB+1,1,L),f32)]+[fls]*6+[
            pltpu.VMEM((NB+1,8,L),f32),fls,fls,pltpu.VMEM((NB+1,F,C),bf),pltpu.VMEM((2,F,C),f32),pltpu.VMEM((2,F,L),f32),
            pltpu.VMEM((T,L),f32)]+[fl]*8+[pltpu.VMEM((T,L),f32)],
        cost_estimate=cost(33),
        name='mixer_backward')(where,q,k,v,g,rl,dm,zt,rt,wt,mt,gain,shift,pg,ps)


def cost(us):
    return pl.CostEstimate(flops=int(us * 1e9), bytes_accessed=int(us * 1e6), transcendentals=0)


def whole(x):
    return pl.BlockSpec(x.shape, lambda *_: (0,) * x.ndim)


SDS = jax.ShapeDtypeStruct


def project_kernel(nh, where, x_ref, gain_ref, wq, wk, wv, wg, wr, xn, q, k, v, g, rl):
    n = x_ref.shape[0] // nh

    @pl.when(pl.program_id(0) == 0)
    def _():
        for r in range(nh):
            x = x_ref[pl.ds(pl.multiple_of((where[0] ^ r) * n, MB), n), :].astype(f32)
            inv = lax.rsqrt(jnp.mean(x * x, axis=-1, keepdims=True) + EPS)
            xn[r * n : (r + 1) * n, :] = (gain_ref[...] * (x * inv)).astype(bf)
        rl[...] = dot_nt(xn[...], wr[...])

    for w, o in ((wq, q), (wk, k), (wv, v), (wg, g)):
        o[...] = dot_nn(xn[...], w[...]).astype(bf)


def project(nh, where, x, gain, weights, wr, tile=256):
    T, D = x.shape
    C, H = weights[0].shape[1], wr.shape[0]
    col = pl.BlockSpec((D, tile), lambda j: (0, j))
    out = pl.BlockSpec((T, tile), lambda j: (0, j))
    return pl.pallas_call(
        functools.partial(project_kernel, nh),
        grid=(C // tile,),
        in_specs=[SM, whole(x), whole(gain)] + [col] * 4 + [whole(wr)],
        out_specs=[pl.BlockSpec((T, D), lambda j: (0, 0))] + [out] * 4 + [pl.BlockSpec((T, H), lambda j: (0, 0))],
        out_shape=[SDS((T, D), bf)] + [SDS((T, C), bf)] * 4 + [SDS((T, H), f32)],
        cost_estimate=cost(8),
        name="project",
    )(where, x, gain, *weights, wr)


def split_kernel(kinds, more, *refs):
    n = len(kinds)
    acc = None
    for turned, a, b in zip(kinds, refs[:n], refs[n : 2 * n]):
        y = (dot_nt if turned else dot_nn)(a[...], b[...])
        acc = y if acc is None else acc + y
    extra, outs = refs[2 * n : 2 * n + more], refs[2 * n + more :]
    rows = outs[0].shape[0]
    for r, o in enumerate(outs):
        o[:rows, :] = acc[r * rows : (r + 1) * rows].astype(o.dtype)
        if 0 < r <= more:
            o[rows:, :] = extra[r - 1][...]


def split_product(nh, terms, name, us, extra=(), tile=512):
    T = terms[0][0].shape[-2]
    D = terms[0][1].shape[0 if terms[0][2] else 1]
    a_specs, b_specs = [], []
    for a, b, turned, col in terms:
        depth = b.shape[1 if turned else 0]
        if a.ndim == 3:
            a_specs.append(pl.BlockSpec((None, T, depth), lambda j, col=col: (col, 0, 0)))
        else:
            a_specs.append(pl.BlockSpec((T, depth), lambda j, col=col: (0, col)))
        b_specs.append(
            pl.BlockSpec((tile, depth), lambda j: (j, 0)) if turned else pl.BlockSpec((depth, tile), lambda j: (0, j))
        )
    n = T // nh
    rows = [2 * n if 0 < r <= len(extra) else n for r in range(nh)]
    return pl.pallas_call(
        functools.partial(split_kernel, [t[2] for t in terms], len(extra)),
        grid=(D // tile,),
        in_specs=a_specs + b_specs + [pl.BlockSpec((n, tile), lambda j: (0, j))] * len(extra),
        out_specs=[pl.BlockSpec((m, tile), lambda j: (0, j)) for m in rows],
        out_shape=[SDS((m, D), bf if r else f32) for r, m in enumerate(rows)],
        cost_estimate=cost(us),
        name=name,
    )(*[t[0] for t in terms], *[t[1] for t in terms], *extra)


def lay(target, arrays, plan):
    rows = target.shape[0] // len(plan)
    for i, (a, at) in enumerate(plan):
        target[i * rows : (i + 1) * rows, :] = arrays[a][at : at + rows, :]


def rows_kernel(*refs):
    out = refs[-1]
    n = refs[0].shape[0]
    for i, x in enumerate(refs[:-1]):
        out[i * n : (i + 1) * n, :] = x[...]


def top_rows(arrays, n):
    D = arrays[0].shape[1]
    return pl.pallas_call(
        rows_kernel,
        grid=(1,),
        in_specs=[pl.BlockSpec((n, D), lambda i: (0, 0))] * len(arrays),
        out_specs=pl.BlockSpec((n * len(arrays), D), lambda i: (0, 0)),
        out_shape=SDS((n * len(arrays), D), arrays[0].dtype),
        cost_estimate=cost(2),
        name="top_rows",
    )(*arrays)


def chunk_of(T):
    return T if T <= 576 else max(c for c in range(MB, 577, MB) if T % c == 0)


def feed_grad_kernel(many, chunk, *refs):
    w, back, flat = refs[many:]

    @pl.when(pl.program_id(0) == 0)
    def _():
        at = 0
        for a in refs[:many]:
            flat[at : at + a.shape[0], :] = a[...]
            at += a.shape[0]

    def body(i, _):
        rows = pl.ds(pl.multiple_of(i * chunk, MB), chunk)
        back[rows, :] = dot_nt(flat[rows, :], w[...]).astype(bf)
        return 0

    lax.fori_loop(0, back.shape[0] // chunk, body, 0)


def feed_grad(arrays, w, name, us, tile=512):
    T = sum(x.shape[0] for x in arrays)
    N, D = w.shape
    return pl.pallas_call(
        functools.partial(feed_grad_kernel, len(arrays), chunk_of(T)),
        grid=(pl.cdiv(N, tile),),
        in_specs=[whole(x) for x in arrays] + [pl.BlockSpec((tile, D), lambda j: (j, 0))],
        out_specs=pl.BlockSpec((T, tile), lambda j: (0, j)),
        out_shape=SDS((T, N), bf),
        scratch_shapes=[pltpu.VMEM((T, D), bf)],
        cost_estimate=cost(us),
        name=name,
    )(*arrays, w)


def feed_kernel(plan, many, chunk, *refs):
    arrays, backs = refs[:many], refs[many:-5]
    wg, wu, flat, out, grads = refs[-5:]

    @pl.when(pl.program_id(0) == 0)
    def _():
        lay(flat, arrays, plan)

    at = 0
    for b in backs:
        grads[at : at + b.shape[0], :] = b[...]
        at += b.shape[0]

    def body(i, _):
        rows = pl.ds(pl.multiple_of(i * chunk, MB), chunk)
        gate = dot_nt(flat[rows, :], wg[...])
        up = dot_nt(flat[rows, :], wu[...])
        grad = grads[rows, :].astype(f32)
        sig = jax.nn.sigmoid(gate)
        silu = gate * sig
        out[0, rows, :] = (grad * up * sig * (1.0 + gate * (1.0 - sig))).astype(bf)
        out[1, rows, :] = (grad * silu).astype(bf)
        out[2, rows, :] = (silu * up).astype(bf)
        return 0

    lax.fori_loop(0, flat.shape[0] // chunk, body, 0)


def feed(n, plan, arrays, backs, wg, wu, name, us, tile=512):
    T = n * len(plan)
    N, D = wg.shape
    row = pl.BlockSpec((tile, D), lambda j: (j, 0))
    return pl.pallas_call(
        functools.partial(feed_kernel, plan, len(arrays), chunk_of(T)),
        grid=(pl.cdiv(N, tile),),
        in_specs=[whole(x) for x in arrays]
        + [pl.BlockSpec((rows, tile), lambda j, at=at: (at, j)) for _, rows, at in backs]
        + [row, row],
        out_specs=[pl.BlockSpec((T, D), lambda j: (0, 0)), pl.BlockSpec((3, T, tile), lambda j: (0, 0, j))],
        out_shape=[SDS((T, D), bf), SDS((3, T, N), bf)],
        scratch_shapes=[pltpu.VMEM((T, tile), bf)],
        cost_estimate=cost(us),
        name=name,
    )(*arrays, *[x for x, _, _ in backs], wg, wu)


def feed_blocks_kernel(plans, many, begun, *refs):
    xs, ns = refs[1 : 1 + many], refs[1 + many : 1 + many + len(plans)]
    give, keep = refs[-2:]
    y = None
    for plan, m in zip(plans, ns):
        x = jnp.concatenate([xs[i][...] for i in plan], axis=0)
        p = dot_tn(x, m[...])
        y = p if y is None else y + p
    y = y.T

    @pl.when(pl.program_id(1) == 0)
    def _():
        give[...] = (y + refs[-4][...] if begun else y).astype(give.dtype)

    @pl.when(pl.program_id(1) == 1)
    def _():
        keep[...] = y + refs[-3][...] if begun else y


def feed_blocks(where, nz, xs, plans, ns, first, layers, wide, name, us, begun=(), kind=bf):
    N = ns[0].shape[2]
    x_specs = [
        pl.BlockSpec((x.shape[0], wide), lambda w, b, where: (0, where[3 + nz * (1 - b)])) for x in xs
    ]
    n_specs = [pl.BlockSpec((None, m.shape[1], N), lambda w, b, where: (first + w, 0, 0)) for m in ns]
    out = pl.BlockSpec((None, N, wide), lambda w, b, where: (w, 0, 0))
    return pl.pallas_call(
        functools.partial(feed_blocks_kernel, plans, len(xs), len(begun)),
        grid_spec=pltpu.PrefetchScalarGridSpec(
            num_scalar_prefetch=1,
            grid=(layers, 2),
            in_specs=x_specs + n_specs + [out] * len(begun),
            out_specs=[out, out],
        ),
        out_shape=[SDS((layers, N, wide), kind), SDS((layers, N, wide), f32)],
        cost_estimate=cost(us),
        name=name,
    )(where, *xs, *ns, *begun)


def branch_kernel(n, *refs):
    pieces = refs[:n]
    w, slope, flat, mg, dg = refs[n:]

    @pl.when(pl.program_id(0) == 0)
    def _():
        rows = flat.shape[0] // n
        for i, a in enumerate(pieces):
            flat[i * rows : (i + 1) * rows, :] = a[:rows, :]

    y = dot_nt(flat[...], w[...])
    mg[...] = y.astype(bf)
    dg[...] = (y * slope[...].astype(f32)).astype(bf)


def branch_back(pieces, n, w, slope, tile=256):
    T, C = slope.shape
    D = w.shape[1]
    out = pl.BlockSpec((T, tile), lambda j: (0, j))
    return pl.pallas_call(
        functools.partial(branch_kernel, len(pieces)),
        grid=(C // tile,),
        in_specs=[whole(x) for x in pieces] + [pl.BlockSpec((tile, D), lambda j: (j, 0)), out],
        out_specs=[pl.BlockSpec((T, D), lambda j: (0, 0)), out, out],
        out_shape=[SDS((T, D), bf), SDS((T, C), bf), SDS((T, C), bf)],
        cost_estimate=cost(4),
        name="branch_back",
    )(*pieces, w, slope)


def blocks_kernel(groups, turned, *refs):
    refs = refs[1:]
    n = sum(groups)
    xs, ns, outs = refs[:n], refs[n : 2 * n], refs[2 * n :]
    parts, at = [], 0
    for count in groups:
        y = None
        for i in range(at, at + count):
            p = dot_tn(xs[i][...], ns[i][...])
            y = p if y is None else y + p
        parts.append(y)
        at += count
    for k, o in enumerate(outs):
        @pl.when(pl.program_id(0) == k)
        def _(o=o):
            at = 0
            for y in parts:
                if turned:
                    o[at : at + y.shape[1], :] = y.T.astype(o.dtype)
                else:
                    o[:, at : at + y.shape[1]] = y.astype(o.dtype)
                at += y.shape[1]


def block_products(where, stride, groups, kinds, wide, name, us, turned=False):
    xs = [x for group in groups for x, _ in group]
    ns = [n for group in groups for _, n in group]
    N = sum(group[0][1].shape[1] for group in groups)
    x_specs = [pl.BlockSpec((x.shape[0], wide), lambda k, where: (0, where[3 + stride * k])) for x in xs]
    n_specs = [pl.BlockSpec(n.shape, lambda k, where: (0, 0)) for n in ns]
    shape = (N, wide) if turned else (wide, N)
    return pl.pallas_call(
        functools.partial(blocks_kernel, [len(group) for group in groups], turned),
        grid_spec=pltpu.PrefetchScalarGridSpec(
            num_scalar_prefetch=1,
            grid=(len(kinds),),
            in_specs=x_specs + n_specs,
            out_specs=[pl.BlockSpec(shape, lambda k, where: (0, 0))] * len(kinds),
        ),
        out_shape=[SDS(shape, kind) for kind in kinds],
        cost_estimate=cost(us),
        name=name,
    )(where, *xs, *ns)


def natural_kernel(n, plans, many, where, *refs):
    for plan, out in zip(plans, refs[many:]):
        for r, (i, at) in enumerate(plan):
            out[pl.ds(pl.multiple_of((where[0] ^ r) * n, MB), n), :] = refs[i][at : at + n, :]


def natural(where, arrays, n, plans):
    D = arrays[0].shape[1]
    return pl.pallas_call(
        functools.partial(natural_kernel, n, plans, len(arrays)),
        in_specs=[SM] + [VM] * len(arrays),
        out_specs=[VM] * len(plans),
        out_shape=[SDS((n * len(plan), D), arrays[0].dtype) for plan in plans],
        cost_estimate=cost(0.2),
        name="natural",
    )(where, *arrays)


def join_kernel(one, by_two, two, by_one, for_one, for_two):
    n = by_two.shape[0]
    for_one[:n, :] = (one[:n, :].astype(f32) + by_two[...].astype(f32)).astype(bf)
    for_one[n:, :] = one[n:, :]
    for_two[:n, :] = two[:n, :]
    for_two[n:, :] = (two[n:, :].astype(f32) + by_one[...].astype(f32)).astype(bf)


def join(one, by_two, two, by_one):
    return pl.pallas_call(
        join_kernel,
        in_specs=[VM] * 4,
        out_specs=[VM] * 2,
        out_shape=[SDS(one.shape, bf), SDS(two.shape, bf)],
        cost_estimate=cost(1),
        name="join",
    )(one, by_two, two, by_one)


def add_rows(x, row):
    high = row.astype(bf)
    low = (row - high.astype(f32)).astype(bf)
    rest = jnp.zeros((MB - 2, row.shape[0]), bf)
    return jnp.concatenate([x, high[None], low[None], rest], axis=0)


def last_rows(x):
    return x[-MB].astype(f32) + x[1 - MB].astype(f32)


def after(x, *others):
    return lax.optimization_barrier((x, others))[0]


def rms_inv(x):
    return lax.rsqrt(jnp.mean(x * x, axis=-1, keepdims=True) + EPS)


class Links:
    def __init__(self, mesh):
        self.nh = mesh.shape["head"]
        self.nq = mesh.shape["seq"]
        self.nz = self.nq // 2
        self.turns = tuple(range(self.nh - 1, 0, -1))

    def place(self):
        self.h = lax.axis_index("head")
        self.s = lax.axis_index("seq")
        self.c = self.s % 2
        self.z = self.s // 2

    def partner(self, x, r):
        return lax.ppermute(x, "head", [(i, i ^ r) for i in range(self.nh)])

    def sibling(self, x):
        return lax.ppermute(x, "seq", [(i, i ^ 1) for i in range(self.nq)])

    def along(self, x, k):
        n = self.nz
        return lax.ppermute(x, "seq", [(2 * p + c, 2 * ((p + k) % n) + c) for p in range(n) for c in range(2)])

    def head_sum(self, parts, hold=()):
        got = [after(self.partner(parts[r], r), *hold) for r in self.turns]
        total = parts[0]
        for x in got:
            total = total + x.astype(f32)
        return total

    def head_pieces(self, x):
        got = {r: self.partner(x, r) for r in self.turns}
        return [x] + [got[r] for r in range(1, self.nh)]

    def paired_start(self, parts, across, hold):
        if self.nh != 4:
            return parts[1:]
        by_two = after(self.partner(parts[3], 2), hold)
        by_one = after(self.partner(across, 1), hold)
        return join(parts[1], by_two, parts[2], by_one)

    def paired_pieces(self, x):
        if self.nh != 4:
            return self.head_pieces(x)
        return [x, self.partner(x, 1), self.partner(x, 2)]

    def paired_rest(self, pieces, n):
        if self.nh != 4:
            return pieces, tuple((r, 0) for r in range(self.nh)), tuple((r, n) for r in range(self.nh))
        upper, lower = self.partner(pieces[1][:n], 2), self.partner(pieces[2][n:], 1)
        return pieces + [upper, lower], ((0, 0), (1, 0), (2, 0), (3, 0)), ((0, n), (1, n), (2, n), (4, 0))

    def line_sum(self, parts):
        got = [self.along(parts[k], k) for k in self.line_order()]
        total = parts[0]
        for x in got:
            total = total + x.astype(f32)
        return total

    def line_order(self):
        half = self.nz // 2
        return sorted(range(1, self.nz), key=lambda k: abs(k - half))

    def ring(self, x):
        out = []
        for _ in range(1, self.nz):
            x = self.along(x, 1)
            out.append(x)
        return out

    def ring_sum(self, parts):
        total = parts[self.nz - 1]
        for k in range(self.nz - 2, -1, -1):
            total = parts[k] + self.along(total, 1).astype(f32)
            total = total if k == 0 else total.astype(bf)
        return total

    def relative(self, x):
        n = x.shape[0] // self.nh
        return jnp.concatenate(
            [lax.dynamic_slice_in_dim(x, (self.h ^ r) * n, n, axis=0) for r in range(self.nh)], axis=0
        )


def per_device(
    links,
    inputs,
    lengths,
    first_gain,
    query_weight,
    key_weight,
    value_weight,
    gate_weight,
    rate_weight,
    inner_weight,
    inner_offset,
    inner_gain,
    inner_shift,
    post_gain,
    post_shift,
    out_weight,
    second_gain,
    feed_gate,
    feed_up,
    feed_down,
    out_grad,
):
    links.place()
    nh, nz, nq = links.nh, links.nz, links.nq
    spot = jnp.arange(4 + nz, dtype=jnp.int32)
    cols = 2 * lax.rem(links.z + spot + (nz - 3), nz) + links.c
    cols = jnp.where(spot == 3 + nz, 2 * links.z + 1 - links.c, cols)
    spread = lax.pad(lengths.reshape(-1), jnp.int32(0), [(1, nz + 1, 0)])
    where = jnp.where(spot == 0, links.h, jnp.where(spot < 3, spread, cols))
    n = inputs.shape[0] // nh
    per = n // MB
    wide = inputs.shape[1] // nq
    heads, width = inner_offset.shape
    C = heads * width
    pg, ps = post_gain[None], post_shift[None]
    rate_turned = rate_weight.T
    feed_gate, feed_up = feed_gate.T, feed_up.T

    grad_rel = links.relative(out_grad)
    straight = [0] + list(range(3, nh))
    steps = nz - 1
    lead = jnp.concatenate([grad_rel[:n], grad_rel[3 * n :]], axis=0)
    grad_ring = [links.along(lead, 1)]
    grad_last = links.along(lead, nz - 1)
    steps = nz - 1
    grad_ring = [links.along(jnp.concatenate([grad_rel[:n], grad_rel[3 * n :]], axis=0), 1)]
    normed_one, query, key, value, gate, rate_logit = project(
        nh, where, inputs, first_gain[None], (query_weight, key_weight, value_weight, gate_weight), rate_turned
    )
    mixed, slope, zt, rt, wt, mt = mixer_fwd(
        where, per, query, key, value, gate, rate_logit, inner_weight, inner_offset, inner_gain, inner_shift, pg, ps
    )
    own_source = lax.dynamic_slice_in_dim(inputs, links.h * n, n, axis=0).astype(f32)
    own_upstream = grad_rel[:n].astype(f32)

    mixed = after(mixed, grad_ring[0])
    for k in range(2, nz - 1):
        grad_ring.append(links.along(after(grad_ring[-1], grad_last), 1))
    grad_ring.append(grad_last)
    out_parts = split_product(nh, [(mixed, out_weight, False, 0)], "out_product", 0.1, tile=1024)
    backs = [feed_grad([after(grad_ring[0], out_parts[0])], feed_down, "feed_grad_first", 1)]
    back_own = feed_grad([after(grad_rel, backs[0])], feed_down, "feed_grad_own", 1)
    hidden = own_source + links.head_sum(out_parts, (back_own,))
    r2 = rms_inv(hidden)
    two_own = (second_gain * (hidden * r2)).astype(bf)
    twos = links.head_pieces(two_own)
    lot = lead.shape[0]
    back_next = feed_grad([after(grad_ring[1], two_own), *grad_ring[2:]], feed_down, "feed_grad_next", 1, tile=256)
    grad_across = top_rows([after(grad_ring[0], back_next), *grad_ring[1:]], n)
    twos[1:] = [after(x, grad_across) for x in twos[1:]]
    grad_across = after(grad_across, *twos[1:])
    grad_across = [links.partner(grad_across, r) for r in (1, 2)]
    own_plan = tuple((r, 0) for r in range(nh))
    normed_two, feed_own = feed(n, own_plan, twos, [(back_own, n * nh, 0)], feed_gate, feed_up, "feed_own", 4)
    two_ring = [links.along(after(jnp.concatenate([twos[r] for r in straight], axis=0), *twos[1:]), 1)]
    back_parts = split_product(
        nh, [(feed_own, feed_gate, False, 0), (feed_own, feed_up, False, 1)], "feed_back", 3
    )
    two_ring[0] = after(two_ring[0], back_parts[0])
    for k in range(2, nz):
        two_ring.append(links.along(two_ring[-1], 1))
    back_parts = [back_parts[0]] + [after(x, two_ring[0], *grad_across) for x in back_parts[1:]]
    down_parts = list(split_product(nh, [(after(feed_own, back_parts[0]), feed_down, False, 2)], "feed_down", 1, tile=1024))
    back_last = feed_grad([after(grad_across[0], down_parts[0]), grad_across[1]], feed_down, "feed_grad_last", 1, tile=256)
    two = links.head_sum(back_parts, (back_last, two_ring[1]))
    u = two * second_gain
    hidden_grad = own_upstream + r2 * u - hidden * (r2 * r2 * r2) * jnp.mean(u * hidden, axis=-1, keepdims=True)
    second_part = jnp.sum(two * hidden * r2, axis=0)
    pieces = links.head_pieces(add_rows(hidden_grad.astype(bf), second_part))
    parts = range(len(straight))
    plan = tuple((k, i * n) for k in range(steps - 1) for i in parts)
    held = [after(two_ring[0], pieces[0]), *two_ring[1:-1]]
    first_backs = [(backs[0], lot, 0)] + [(back_next, lot, k) for k in range(steps - 2)]
    first = feed(n, plan, held, first_backs, feed_gate, feed_up, "feed_first", 1)
    begun = feed_blocks(
        where, nz, [normed_two, first[0]], ((0,), (1,)), [feed_own, first[1]], 0, 2, wide, "feed_in_begin", 0.5, kind=f32
    )
    pieces[1:] = [after(x, begun[1]) for x in pieces[1:]]
    second_part = (second_part, pieces[1:])
    pieces[0] = after(pieces[0], two_ring[-1])
    branch_grad, mixed_grad, dg = branch_back(pieces, n, out_weight, slope)
    across = top_rows(two_ring, n)
    across = [links.partner(across, r) for r in (1, 2)]

    one_sib = links.sibling(normed_one)
    groups = [
        [(normed_one, dg), (one_sib, links.sibling(dg))],
        [(branch_grad, mixed), (links.sibling(branch_grad), links.sibling(mixed))],
    ]
    pair = block_products(where, 1, groups, [f32] + [bf] * (nz - 1), wide, "gate_out_blocks", 8)
    pair_got = {k: links.along(pair[k], k) for k in (2, 1)}

    dqkv, drate, dw0, db0, dgain, dshift, dpg, dps = mixer_bwd(
        where, per, query, key, value, gate, rate_logit, after(mixed_grad, pair[0]),
        zt, rt, wt, mt, inner_gain, inner_shift, pg, ps
    )
    dqkv = after(dqkv, pair_got[2], *across)
    for k in range(3, nz):
        pair_got[k] = links.along(after(pair[k], dqkv), k)
    drate_low = drate
    dqkv_sib = links.sibling(dqkv)
    back_parts = split_product(
        nh,
        [
            (dqkv, query_weight, True, 0),
            (dqkv, key_weight, True, 1),
            (dqkv, value_weight, True, 2),
            (dg, gate_weight, True, 0),
            (drate_low, rate_turned, False, 0),
        ],
        "input_back",
        8,
        extra=down_parts[1 : 3 if nh == 4 else nh],
    )
    groups = [[(normed_one, after(dqkv, back_parts[0])), (one_sib, dqkv_sib)]]
    trio = block_products(where, 1, groups, [f32] + [bf] * (nz - 1), wide, "qkv_blocks", 8)
    parts_two = links.paired_start(back_parts, down_parts[3], (trio[0], pair_got[1]))
    trio_step = links.along(trio[-1], 1)

    plan = tuple((0, i * n) for i in parts) + tuple((1 + i, k * n) for i in range(2) for k in range(steps))
    held = [after(two_ring[-1], trio[0], parts_two[0]), *across]
    second_backs = [(back_next, lot, steps - 2), (back_last, 2 * steps * n, 0)]
    second = feed(n, plan, held, second_backs, feed_gate, feed_up, "feed_second", 15, tile=256)

    def rows_of(x):
        return x.reshape(nq, -1)

    def heads_of(x):
        return x.reshape((heads, nq, -1)).transpose(1, 0, 2).reshape(nq, -1)

    received = [links.partner(x, r + 1) for r, x in enumerate(parts_two)]
    second, trio_step, received, pair_got = lax.optimization_barrier((second, trio_step, received, pair_got))
    send = (trio[nz - 2].astype(f32) + trio_step.astype(f32)).astype(bf)
    sums = jnp.concatenate([back_parts[0], down_parts[0]], axis=0)
    for x in received:
        sums = sums + after(x, send).astype(f32)
    one, output = sums[:n], hidden + sums[n:]
    r1 = rms_inv(own_source)
    w = one * first_gain
    input_grad = hidden_grad + r1 * w - own_source * (r1 * r1 * r1) * jnp.mean(w * own_source, axis=-1, keepdims=True)
    input_low = input_grad.astype(bf)
    first_part = jnp.sum(one * own_source * r1, axis=0)
    packed = add_rows(jnp.concatenate([input_low, output.astype(bf)], axis=0), first_part)
    got = links.along(send, 1)
    outs = [feed_own, first[1], second[1]]
    give, keep = feed_blocks(
        where, nz, [after(second[0], packed)], ((0,),), outs[2:], 0, 2, wide, "feed_in_blocks", 6, begun=begun
    )
    for k in range(nz - 3, 0, -1):
        send = (trio[k].astype(f32) + after(got, keep).astype(f32)).astype(bf)
        got = links.along(send, 1)
    pieces, send = lax.optimization_barrier((links.paired_pieces(packed), send))
    arrays, upper, lower = links.paired_rest(pieces, n)
    xs = [after(grad_rel, keep, send, pieces), *grad_ring, *grad_across]
    plans = ((0,), tuple(range(1, steps)), tuple(range(steps, len(xs))))
    first_give = give
    give, keep_out = feed_blocks(where, nz, xs, plans, outs, 2, 1, wide, "feed_out_blocks", 4)
    arrays[1:] = [after(x, keep_out) for x in arrays[1:]]
    input_grad, output = natural(where, arrays, n, (upper, lower))
    other = links.sibling(after(first_give, keep_out)).astype(f32)
    feed_grads = [keep[0] + other[0], keep[1] + other[1]]
    second_part, held = second_part
    second_part = second_part + sum(last_rows(after(x, keep_out)) for x in held)
    rate_part = lax.dot_general(
        after(normed_one, output), drate_low, (((0,), (0,)), ((), ())), preferred_element_type=f32
    )
    dw0, db0, dgain, dshift, dpg, dps = after((dw0, db0, dgain, dshift, dpg, dps), output)
    small = [rows_of(second_part), rows_of(rate_part), heads_of(dw0)]
    small += [heads_of(x) for x in (db0, dgain, dshift)] + [rows_of(dpg), rows_of(dps)]
    sizes = [x.shape[1] for x in small]
    small = jnp.concatenate(small, axis=1)
    got, small = lax.optimization_barrier((after(got, keep_out), small))
    grad_qkv = trio[0] + got.astype(f32)
    feed_grads.append(keep_out[0] + links.sibling(after(give[0], grad_qkv)).astype(f32))
    first_part = first_part + sum(last_rows(arrays[i]) for i, _ in lower[1:])
    sizes = [wide] + sizes
    small = jnp.concatenate([rows_of(first_part), small], axis=1).reshape(nz, 2, -1)
    keep = lax.dynamic_index_in_dim(small, links.c, 1, keepdims=False)
    give = lax.dynamic_index_in_dim(small, 1 - links.c, 1, keepdims=False)
    small = keep + links.sibling(give)
    small = links.line_sum([lax.dynamic_index_in_dim(small, lax.rem(links.z + k, nz), 0, keepdims=False) for k in range(nz)])
    pair = pair[0] + sum(x.astype(f32) for x in pair_got.values())
    ends = [sum(sizes[: i + 1]) for i in range(len(sizes))]
    small = [small[e - n : e] for e, n in zip(ends, sizes)]
    part = width // nq
    return (
        output,
        input_grad,
        small[0],
        grad_qkv[:, :C],
        grad_qkv[:, C : 2 * C],
        grad_qkv[:, 2 * C :],
        pair[:, :C],
        small[2].reshape(-1, heads),
        small[3].reshape(heads, part, width),
        small[4].reshape(heads, part),
        small[5].reshape(heads, part),
        small[6].reshape(heads, part),
        small[7],
        small[8],
        pair[:, C:].T,
        small[1],
        feed_grads[0].T,
        feed_grads[1].T,
        feed_grads[2],
    )


def solution(mesh):
    in_specs = (
        P("seq", None),
        P("seq", None),
        P(),
        P(None, "head"),
        P(None, "head"),
        P(None, "head"),
        P(None, "head"),
        P(None, "head"),
        P("head", None, None),
        P("head", None),
        P("head", None),
        P("head", None),
        P("head"),
        P("head"),
        P("head", None),
        P(),
        P(None, "head"),
        P(None, "head"),
        P("head", None),
        P("seq", None),
    )
    out_specs = (
        P("seq", None),
        P("seq", None),
        P("seq"),
        P("seq", "head"),
        P("seq", "head"),
        P("seq", "head"),
        P("seq", "head"),
        P("seq", "head"),
        P("head", "seq", None),
        P("head", "seq"),
        P("head", "seq"),
        P("head", "seq"),
        P(("head", "seq")),
        P(("head", "seq")),
        P("head", "seq"),
        P("seq"),
        P("seq", "head"),
        P("seq", "head"),
        P("head", "seq"),
    )
    return jax.shard_map(
        functools.partial(per_device, Links(mesh)), mesh=mesh, in_specs=in_specs, out_specs=out_specs, check_vma=False
    )
```

```python
import functools

import jax
import jax.numpy as jnp
from jax import lax
from jax.experimental import pallas as pl
from jax.experimental.pallas import tpu as pltpu
from jax.sharding import PartitionSpec as P

MB=16; EPS=1e-6
bf=jnp.bfloat16; f32=jnp.float32

def dot_nn(a,b): return lax.dot_general(a,b,(((1,),(0,)),((),())),preferred_element_type=f32)
def dot_nt(a,b): return lax.dot_general(a,b,(((1,),(1,)),((),())),preferred_element_type=f32)
def dot_tn(a,b): return lax.dot_general(a,b,(((0,),(0,)),((),())),preferred_element_type=f32)

def mean0(x): return jnp.mean(x,axis=0,keepdims=True)

def norm_parts(x):
    c=x-mean0(x)
    inv=lax.rsqrt(mean0(c*c)+EPS)
    return c*inv,inv

def norm_back(dy,n,inv):
    return inv*(dy-mean0(dy)-n*mean0(dy*n))

def split2(x):
    hi=x.astype(bf)
    return jnp.concatenate([hi,(x-hi.astype(f32)).astype(bf)],axis=0)

def two_rows(x):
    h=x.shape[0]//2
    return x[:h]+x[h:]

def stack_heads(rows,F):
    H=rows.shape[1]//F
    r=rows.astype(f32)
    return jnp.concatenate([r[:,h*F:(h+1)*F] for h in range(H)],axis=0).T

GC=0.7978845608028654; GA=0.044715
def gelu_parts(x):
    u=GC*(x+GA*x*x*x)
    t=jnp.tanh(u)
    val=0.5*x*(1.0+t)
    der=0.5*(1.0+t)+0.5*x*(1.0-t*t)*GC*(1.0+3.0*GA*x*x)
    return val,der

def plan_blocks(where):
    n0=(where[1]+MB-1)//MB; n1=(where[2]+MB-1)//MB
    return (n0,n1),(0,n0)

def row_of(where,b,per):
    return pl.multiple_of(((lax.div(b,per)^where[0])*per+lax.rem(b,per))*MB,MB)

def lane_iota(shape,dim): return lax.broadcasted_iota(jnp.int32,shape,dim)

def valid_row(where,offs,blk,L):
    pos=blk*MB+lane_iota((1,L),1)%MB
    a=(pos>=offs[0]*MB)&(pos<offs[0]*MB+where[1])
    b=(pos>=offs[1]*MB)&(pos<offs[1]*MB+where[2])
    return a|b

def fill_bd(dst,blk,rows,row0,F):
    H=rows.shape[1]//F
    for h in range(H):
        dst[blk,row0+h*MB:row0+(h+1)*MB,h*F:(h+1)*F]=rows[:,h*F:(h+1)*F]

def fill_turned(dst,blk,kt,qt):
    F,L=kt.shape
    both=jnp.concatenate([kt,qt],axis=1).astype(bf)
    lane=lane_iota((F,2*L),1)%L//MB
    for h in range(L//MB):
        dst[blk,h*F:(h+1)*F,:]=jnp.where(lane==h,both,jnp.zeros_like(both))

def same_head(L):
    return lane_iota((L,L),0)//MB==lane_iota((L,L),1)//MB

def head_lanes(H,L):
    return (lane_iota((H,L),0)==lane_iota((H,L),1)//MB).astype(f32)

HIGH=lax.Precision.HIGHEST
def head_rows(ref,F):
    return jnp.concatenate([ref[:,i:i+F] for i in range(0,ref.shape[1],F)],axis=0)
def spread(per_head,rep):
    return lax.dot_general(per_head,rep,(((0,),(0,)),((),())),precision=HIGH,preferred_element_type=f32)
def gather_heads(x,rep):
    return lax.dot_general(rep,x,(((1,),(1,)),((),())),precision=HIGH,preferred_element_type=f32)

def fwd_kernel(UN,PER,where,q_ref,k_ref,v_ref,g_ref,rlh_ref,w0_ref,b0_ref,gainh_ref,shifth_ref,pgh_ref,psh_ref,
               mixed_ref,slope_ref,zt_ref,rt_ref,wt_ref,mt_ref,
               kq,kqt,tt,rate,mtb,wst,bst,rl_ref,gain_ref,shift_ref,pg_ref,ps_ref):
    T,C=q_ref.shape; H,F=b0_ref.shape; L=H*MB; NB=T//MB
    rep=head_lanes(H,L)
    rl_ref[...]=lax.dot_general(rlh_ref[...],rep,(((1,),(0,)),((),())),precision=HIGH,preferred_element_type=f32)
    gain_ref[...]=spread(gainh_ref[...],rep); shift_ref[...]=spread(shifth_ref[...],rep)
    pg_ref[...]=spread(head_rows(pgh_ref,F),rep); ps_ref[...]=spread(head_rows(psh_ref,F),rep)
    counts,offs=plan_blocks(where)
    zero_kq=jnp.zeros((2*L,C),bf)
    onesbd=same_head(L).astype(f32).astype(bf)
    keep=same_head(L)&(lane_iota((L,L),0)<=lane_iota((L,L),1))
    pick=lane_iota((MB,L),0)==lane_iota((MB,L),1)%MB
    def clear(b,_):
        kq[b]=zero_kq
        return 0
    lax.fori_loop(0,NB+1,clear,0)
    kqt[NB]=jnp.zeros((C,2*L),bf)
    tt[NB]=jnp.zeros((F,L),f32); rate[NB]=jnp.zeros((1,L),f32); mtb[NB]=jnp.zeros((L,2*L),bf)
    def pre_one(b):
        r=row_of(where,b,PER)
        kn=k_ref[pl.ds(r,MB),:]; qn=q_ref[pl.ds(r,MB),:]; vn=v_ref[pl.ds(r,MB),:]
        fill_bd(kq,b,kn,0,F); fill_bd(kq,b,qn,L,F)
        kt=stack_heads(kn,F); qt=stack_heads(qn,F)
        tt[b]=stack_heads(vn,F)-kt
        fill_turned(kqt,b,kt,qt)
        ok=valid_row(where,offs,b,L)
        rl=jnp.sum(jnp.where(pick,rl_ref[pl.ds(r,MB),:],0.0),axis=0,keepdims=True)
        rate[b]=jnp.where(ok,jax.nn.sigmoid(rl)*(1.0/F),0.0)
        st=dot_nn(kq[b,0:L,:],kqt[b,:,L:2*L])
        m=jnp.where(keep,st+1.0,0.0).astype(bf)
        mt_ref[b]=m
        mtb[b,:,0:L]=m; mtb[b,:,L:2*L]=onesbd
    def pre(i,_):
        for u in range(UN): pre_one(i*UN+u)
        return 0
    lax.fori_loop(0,NB//UN,pre,0)
    def unused(b,_):
        rt_ref[b]=jnp.zeros((F,L),f32)
        zt_ref[b]=jnp.zeros((F,L),f32)
        wt_ref[b]=jnp.zeros((F,C),bf)
        return 0
    lax.fori_loop(counts[0]+counts[1],NB,unused,0)
    bias0=spread(b0_ref[...],rep)
    for h in range(H):
        wh=w0_ref[h].T
        for s in range(2): wst[s,:,h*F:(h+1)*F]=wh
    for s in range(2): bst[s]=bias0
    gain2=jnp.concatenate([gain_ref[...]]*2,axis=1); shift2=jnp.concatenate([shift_ref[...]]*2,axis=1)
    def step(i,_):
        bs=[jnp.where(i<counts[s],offs[s]+i,NB) for s in range(2)]
        w=[wst[s] for s in range(2)]; bias=[bst[s] for s in range(2)]
        w2=[split2(x) for x in w]
        zq=[two_rows(dot_nn(w2[s],kqt[bs[s]])) for s in range(2)]
        z=[zq[s][:,:L]+bias[s] for s in range(2)]
        for s in range(2):
            wt_ref[bs[s]]=w2[s][:F]; zt_ref[bs[s]]=z[s]
        zz=jnp.concatenate(z,axis=1)
        n,inv=norm_parts(zz)
        t2=jnp.concatenate([tt[b] for b in bs],axis=1)
        p=(n*gain2+shift2-t2)*gain2
        g=inv*(p-mean0(p)-n*mean0(p*n))
        g=g*jnp.concatenate([rate[b] for b in bs],axis=1)
        gr=[g[:,s*L:(s+1)*L].astype(bf) for s in range(2)]
        up=[dot_nn(gr[s],kq[bs[s],0:L,:]) for s in range(2)]
        for s in range(2): wst[s]=w[s]-up[s]
        ob=[dot_nn(gr[s],mtb[bs[s]]) for s in range(2)]
        for s in range(2):
            bst[s]=bias[s]-ob[s][:,L:]
            rt_ref[bs[s]]=zq[s][:,L:]+bias[s]-ob[s][:,:L]
        return 0
    lax.fori_loop(0,jnp.maximum(counts[0],counts[1]),step,0)
    def post_one(b):
        r=row_of(where,b,PER)
        qt=stack_heads(q_ref[pl.ds(r,MB),:],F); gt=stack_heads(g_ref[pl.ds(r,MB),:],F)
        nr,_=norm_parts(rt_ref[b])
        io=qt+nr*gain_ref[...]+shift_ref[...]
        ni,_=norm_parts(io)
        act,der=gelu_parts(gt)
        ok=valid_row(where,offs,b,L)
        lo=jnp.where(ok,ni*pg_ref[...]+ps_ref[...],0.0)
        m=(act*lo).T; sl=(der*lo).T
        for h in range(H):
            mixed_ref[pl.ds(r,MB),h*F:(h+1)*F]=m[h*MB:(h+1)*MB,:].astype(bf)
            slope_ref[pl.ds(r,MB),h*F:(h+1)*F]=sl[h*MB:(h+1)*MB,:].astype(bf)
    def post(i,_):
        for u in range(UN): post_one(i*UN+u)
        return 0
    lax.fori_loop(0,NB//UN,post,0)

def bwd_kernel(UN,PER,where,q_ref,k_ref,v_ref,g_ref,rlh_ref,dm_ref,zt_ref,rt_ref,wt_ref,mt_ref,gainh_ref,shifth_ref,pgh_ref,psh_ref,
               dqkv_ref,drlh_ref,dw0_ref,db0h_ref,dgainh_ref,dshifth_ref,dpgh_ref,dpsh_ref,
               kq,kqt,rate,ns,ps_,gs,xs,rs,ios,rows,zs,es,dws,wst,bst,rl_ref,gain_ref,shift_ref,pg_ref,ps_ref,
               dgain_ref,dshift_ref,dpg_ref,dps_ref,drl_ref):
    T,C=q_ref.shape; H,F=gainh_ref.shape; L=H*MB; NB=T//MB
    rep=head_lanes(H,L)
    rl_ref[...]=lax.dot_general(rlh_ref[...],rep,(((1,),(0,)),((),())),precision=HIGH,preferred_element_type=f32)
    gain_ref[...]=spread(gainh_ref[...],rep); shift_ref[...]=spread(shifth_ref[...],rep)
    pg_ref[...]=spread(head_rows(pgh_ref,F),rep); ps_ref[...]=spread(head_rows(psh_ref,F),rep)
    counts,offs=plan_blocks(where)
    zero_kq=jnp.zeros((2*L,C),bf)
    onesbd=same_head(L).astype(f32).astype(bf)
    keep=same_head(L)&(lane_iota((L,L),0)<=lane_iota((L,L),1))
    keep_t=same_head(L)&(lane_iota((L,L),1)<=lane_iota((L,L),0))
    pick=lane_iota((MB,L),0)==lane_iota((MB,L),1)%MB
    zfl=jnp.zeros((F,L),f32)
    def clear(b,_):
        kq[b]=zero_kq
        return 0
    lax.fori_loop(0,NB+1,clear,0)
    for ref in (ns,ps_,gs,xs,rs): ref[NB]=zfl
    kqt[NB]=jnp.zeros((C,2*L),bf)
    rate[NB]=jnp.zeros((1,L),f32); rows[NB]=jnp.zeros((8,L),f32)
    for ref in (dgain_ref,dshift_ref,dpg_ref,dps_ref): ref[...]=zfl
    def pre_one(b):
        r=row_of(where,b,PER)
        kn=k_ref[pl.ds(r,MB),:]; qn=q_ref[pl.ds(r,MB),:]
        fill_bd(kq,b,kn,0,F); fill_bd(kq,b,qn,L,F)
        kt=stack_heads(kn,F); qt=stack_heads(qn,F)
        t=stack_heads(v_ref[pl.ds(r,MB),:],F)-kt
        fill_turned(kqt,b,kt,kt)
        gt=stack_heads(g_ref[pl.ds(r,MB),:],F)
        dm=stack_heads(dm_ref[pl.ds(r,MB),:],F)
        ok=valid_row(where,offs,b,L)
        rl=jnp.sum(jnp.where(pick,rl_ref[pl.ds(r,MB),:],0.0),axis=0,keepdims=True)
        sg=jax.nn.sigmoid(rl)
        rt=jnp.where(ok,sg*(1.0/F),0.0)
        rate[b]=rt
        gain=gain_ref[...]; shift=shift_ref[...]
        n,inv=norm_parts(zt_ref[b])
        e=n*gain+shift-t
        p=e*gain
        mpn=mean0(p*n)
        g=inv*(p-mean0(p)-n*mpn)
        nr,invr=norm_parts(rt_ref[b])
        io=qt+nr*gain+shift
        ni,invi=norm_parts(io)
        act,_=gelu_parts(gt)
        dl=jnp.where(ok,dm*act,0.0)
        dio=norm_back(dl*pg_ref[...],ni,invi)
        dr=norm_back(dio*gain,nr,invr)
        drb=dr.astype(bf)
        ns[b]=n; ps_[b]=e; gs[b]=g; rs[b]=dr; ios[b]=dio
        xs[b]=dot_nt(drb,mt_ref[b])
        rows[b]=jnp.concatenate([inv,mpn,sg*(1.0-sg)*jnp.where(ok,1.0/F,0.0),jnp.zeros((5,L),f32)],axis=0)
        return dl,dl*ni,dio,dio*nr
    def pre(i,_):
        acc=None
        for u in range(UN):
            x=pre_one(i*UN+u)
            acc=x if acc is None else tuple(a+c for a,c in zip(acc,x))
        dps_ref[...]+=acc[0]; dpg_ref[...]+=acc[1]; dshift_ref[...]+=acc[2]; dgain_ref[...]+=acc[3]
        return 0
    lax.fori_loop(0,NB//UN,pre,0)
    def unused(b,_):
        zs[b]=zfl; es[b]=zfl; dws[b]=jnp.zeros((F,C),bf)
        return 0
    lax.fori_loop(counts[0]+counts[1],NB,unused,0)
    for s in range(2):
        wst[s]=jnp.zeros((F,C),f32); bst[s]=zfl
    steps=jnp.maximum(counts[0],counts[1])
    gain2=jnp.concatenate([gain_ref[...]]*2,axis=1)
    def step(j,_):
        i=steps-1-j
        bs=[jnp.where(i<counts[s],offs[s]+i,NB) for s in range(2)]
        both=lambda ref: jnp.concatenate([ref[b] for b in bs],axis=1)
        w=[wst[s] for s in range(2)]; bias=[bst[s] for s in range(2)]
        w2=[split2(x) for x in w]
        xx=[two_rows(dot_nn(w2[s],kqt[bs[s],:,0:L])) for s in range(2)]
        x=jnp.concatenate(xx,axis=1)+jnp.concatenate(bias,axis=1)+both(xs)
        for s in range(2): dws[bs[s]]=w2[s][:F]
        g=both(gs); n=both(ns); p=both(ps_)*gain2; row=both(rows)
        inv=row[0:1]; mpn=row[1:2]
        h=-both(rate)*x
        da=inv*h
        m1=mean0(da*n); m2=mean0(da); m3=mean0(h*g)
        dp=da-m2-n*m1
        de=dp*gain2
        dn=de*gain2-da*mpn-p*m1
        dz=inv*(dn-mean0(dn)-n*(mean0(dn*n)+m3))
        dr=[rs[b] for b in bs]
        dzs=[dz[:,:L],dz[:,L:]]
        up=[dot_nn(jnp.concatenate([dzs[s],dr[s]],axis=1).astype(bf),kq[bs[s]]) for s in range(2)]
        ub=[dot_nn((dzs[s]+dr[s]).astype(bf),onesbd) for s in range(2)]
        out=-jnp.sum(g*x,axis=0,keepdims=True)*row[2:3]
        for s in range(2):
            wst[s]=w[s]+up[s]; bst[s]=bias[s]+ub[s]
            zs[bs[s]]=dzs[s]; es[bs[s]]=dp[:,s*L:(s+1)*L]
            rows[bs[s],3:4,:]=out[:,s*L:(s+1)*L]
        return 0
    lax.fori_loop(0,steps,step,0)
    for h in range(H):
        dw0_ref[h]=(wst[0,:,h*F:(h+1)*F]+wst[1,:,h*F:(h+1)*F]).T
    db0h_ref[...]=gather_heads(bst[0]+bst[1],jnp.where(lane_iota((H,L),1)%MB==0,rep,0.0))
    def post_one(b):
        r=row_of(where,b,PER)
        dp=es[b]; row=rows[b]
        de=dp*gain_ref[...]
        dgain=dp*ps_[b]+de*ns[b]
        gr=(gs[b]*rate[b])
        drb=rs[b].astype(bf); grb=gr.astype(bf); dzb=zs[b].astype(bf)
        dst=jnp.where(keep,-dot_tn(grb,drb),0.0).astype(bf)
        dss=jnp.where(keep_t,-dot_tn(drb,grb),0.0).astype(bf)
        wt=wt_ref[b]
        kb=kq[b,0:L,:]; qb=kq[b,L:2*L,:]
        dqf=dot_tn(jnp.concatenate([drb,dst],axis=0),jnp.concatenate([wt,kb],axis=0))
        dkf=dot_tn(jnp.concatenate([dzb,(-gr).astype(bf),dss],axis=0),jnp.concatenate([wt,dws[b],qb],axis=0))
        det=de.T; dit=ios[b].T
        for h in range(H):
            rr=slice(h*MB,(h+1)*MB); cc=slice(h*F,(h+1)*F)
            dqkv_ref[pl.ds(r,MB),h*F:(h+1)*F]=(dqf[rr,cc]+dit[rr,:]).astype(bf)
            dqkv_ref[pl.ds(r,MB),C+h*F:C+(h+1)*F]=(dkf[rr,cc]+det[rr,:]).astype(bf)
            dqkv_ref[pl.ds(r,MB),2*C+h*F:2*C+(h+1)*F]=(-det[rr,:]).astype(bf)
        drl_ref[pl.ds(r,MB),:]=jnp.where(pick,row[3:4],0.0)
        return dgain,de
    def post(i,_):
        acc=None
        for u in range(UN):
            x=post_one(i*UN+u)
            acc=x if acc is None else tuple(a+c for a,c in zip(acc,x))
        dgain_ref[...]+=acc[0]; dshift_ref[...]+=acc[1]
        return 0
    lax.fori_loop(0,NB//UN,post,0)
    dgainh_ref[...]=gather_heads(dgain_ref[...],rep); dshifth_ref[...]=gather_heads(dshift_ref[...],rep)
    dpgh_ref[...]=gather_heads(dpg_ref[...],rep); dpsh_ref[...]=gather_heads(dps_ref[...],rep)
    drlh_ref[...]=lax.dot_general(drl_ref[...],rep,(((1,),(1,)),((),())),precision=HIGH,preferred_element_type=f32).astype(bf)

VM=pl.BlockSpec(memory_space=pltpu.VMEM); SM=pl.BlockSpec(memory_space=pltpu.SMEM)

def mixer_fwd(where,per,q,k,v,g,rl,w0,b0,gain,shift,pg,ps,UN=3):
    T,C=q.shape; H,F=b0.shape; L=H*MB; NB=T//MB
    S=jax.ShapeDtypeStruct
    fl=pltpu.VMEM((F,L),f32)
    return pl.pallas_call(functools.partial(fwd_kernel,UN,per),
        out_shape=[S((T,C),bf),S((T,C),bf),S((NB+1,F,L),f32),S((NB+1,F,L),f32),S((NB+1,F,C),bf),S((NB,L,L),bf)],
        in_specs=[SM]+[VM]*11,out_specs=[VM]*6,
        scratch_shapes=[pltpu.VMEM((NB+1,2*L,C),bf),pltpu.VMEM((NB+1,C,2*L),bf),pltpu.VMEM((NB+1,F,L),f32),pltpu.VMEM((NB+1,1,L),f32),
            pltpu.VMEM((NB+1,L,2*L),bf),pltpu.VMEM((2,F,C),f32),pltpu.VMEM((2,F,L),f32),pltpu.VMEM((T,L),f32),fl,fl,fl,fl],
        cost_estimate=cost(28),
        name='mixer_forward')(where,q,k,v,g,rl,w0,b0,gain,shift,pg,ps)

def mixer_bwd(where,per,q,k,v,g,rl,dm,zt,rt,wt,mt,gain,shift,pg,ps,UN=3):
    T,C=q.shape; H,F=gain.shape; L=H*MB; NB=T//MB
    S=jax.ShapeDtypeStruct
    fls=pltpu.VMEM((NB+1,F,L),f32); fl=pltpu.VMEM((F,L),f32)
    return pl.pallas_call(functools.partial(bwd_kernel,UN,per),
        out_shape=[S((T,3*C),bf),S((T,H),bf),S((H,F,F),f32)]+[S((H,F),f32)]*5,
        in_specs=[SM]+[VM]*14,out_specs=[VM]*8,
        scratch_shapes=[pltpu.VMEM((NB+1,2*L,C),bf),pltpu.VMEM((NB+1,C,2*L),bf),pltpu.VMEM((NB+1,1,L),f32)]+[fls]*6+[
            pltpu.VMEM((NB+1,8,L),f32),fls,fls,pltpu.VMEM((NB+1,F,C),bf),pltpu.VMEM((2,F,C),f32),pltpu.VMEM((2,F,L),f32),
            pltpu.VMEM((T,L),f32)]+[fl]*8+[pltpu.VMEM((T,L),f32)],
        cost_estimate=cost(33),
        name='mixer_backward')(where,q,k,v,g,rl,dm,zt,rt,wt,mt,gain,shift,pg,ps)


def cost(us):
    return pl.CostEstimate(flops=int(us * 1e9), bytes_accessed=int(us * 1e6), transcendentals=0)


def whole(x):
    return pl.BlockSpec(x.shape, lambda *_: (0,) * x.ndim)


SDS = jax.ShapeDtypeStruct


def project_kernel(nh, where, x_ref, gain_ref, wq, wk, wv, wg, wr, xn, q, k, v, g, rl):
    n = x_ref.shape[0] // nh

    @pl.when(pl.program_id(0) == 0)
    def _():
        for r in range(nh):
            x = x_ref[pl.ds(pl.multiple_of((where[0] ^ r) * n, MB), n), :].astype(f32)
            inv = lax.rsqrt(jnp.mean(x * x, axis=-1, keepdims=True) + EPS)
            xn[r * n : (r + 1) * n, :] = (gain_ref[...] * (x * inv)).astype(bf)
        rl[...] = dot_nt(xn[...], wr[...])

    for w, o in ((wq, q), (wk, k), (wv, v), (wg, g)):
        o[...] = dot_nn(xn[...], w[...]).astype(bf)


def project(nh, where, x, gain, weights, wr, tile=256):
    T, D = x.shape
    C, H = weights[0].shape[1], wr.shape[0]
    col = pl.BlockSpec((D, tile), lambda j: (0, j))
    out = pl.BlockSpec((T, tile), lambda j: (0, j))
    return pl.pallas_call(
        functools.partial(project_kernel, nh),
        grid=(C // tile,),
        in_specs=[SM, whole(x), whole(gain)] + [col] * 4 + [whole(wr)],
        out_specs=[pl.BlockSpec((T, D), lambda j: (0, 0))] + [out] * 4 + [pl.BlockSpec((T, H), lambda j: (0, 0))],
        out_shape=[SDS((T, D), bf)] + [SDS((T, C), bf)] * 4 + [SDS((T, H), f32)],
        cost_estimate=cost(8),
        name="project",
    )(where, x, gain, *weights, wr)


def split_kernel(kinds, more, *refs):
    n = len(kinds)
    acc = None
    for turned, a, b in zip(kinds, refs[:n], refs[n : 2 * n]):
        y = (dot_nt if turned else dot_nn)(a[...], b[...])
        acc = y if acc is None else acc + y
    extra, outs = refs[2 * n : 2 * n + more], refs[2 * n + more :]
    rows = outs[0].shape[0]
    for r, o in enumerate(outs):
        o[:rows, :] = acc[r * rows : (r + 1) * rows].astype(o.dtype)
        if 0 < r <= more:
            o[rows:, :] = extra[r - 1][...]


def split_product(nh, terms, name, us, extra=(), tile=512):
    T = terms[0][0].shape[-2]
    D = terms[0][1].shape[0 if terms[0][2] else 1]
    a_specs, b_specs = [], []
    for a, b, turned, col in terms:
        depth = b.shape[1 if turned else 0]
        if a.ndim == 3:
            a_specs.append(pl.BlockSpec((None, T, depth), lambda j, col=col: (col, 0, 0)))
        else:
            a_specs.append(pl.BlockSpec((T, depth), lambda j, col=col: (0, col)))
        b_specs.append(
            pl.BlockSpec((tile, depth), lambda j: (j, 0)) if turned else pl.BlockSpec((depth, tile), lambda j: (0, j))
        )
    n = T // nh
    rows = [2 * n if 0 < r <= len(extra) else n for r in range(nh)]
    return pl.pallas_call(
        functools.partial(split_kernel, [t[2] for t in terms], len(extra)),
        grid=(D // tile,),
        in_specs=a_specs + b_specs + [pl.BlockSpec((n, tile), lambda j: (0, j))] * len(extra),
        out_specs=[pl.BlockSpec((m, tile), lambda j: (0, j)) for m in rows],
        out_shape=[SDS((m, D), bf if r else f32) for r, m in enumerate(rows)],
        cost_estimate=cost(us),
        name=name,
    )(*[t[0] for t in terms], *[t[1] for t in terms], *extra)


def lay(target, arrays, plan):
    rows = target.shape[0] // len(plan)
    for i, (a, at) in enumerate(plan):
        target[i * rows : (i + 1) * rows, :] = arrays[a][at : at + rows, :]


def rows_kernel(*refs):
    out = refs[-1]
    n = refs[0].shape[0]
    for i, x in enumerate(refs[:-1]):
        out[i * n : (i + 1) * n, :] = x[...]


def top_rows(arrays, n):
    D = arrays[0].shape[1]
    return pl.pallas_call(
        rows_kernel,
        grid=(1,),
        in_specs=[pl.BlockSpec((n, D), lambda i: (0, 0))] * len(arrays),
        out_specs=pl.BlockSpec((n * len(arrays), D), lambda i: (0, 0)),
        out_shape=SDS((n * len(arrays), D), arrays[0].dtype),
        cost_estimate=cost(2),
        name="top_rows",
    )(*arrays)


def chunk_of(T):
    return T if T <= 576 else max(c for c in range(MB, 577, MB) if T % c == 0)


def feed_grad_kernel(many, chunk, *refs):
    w, back, flat = refs[many:]

    @pl.when(pl.program_id(0) == 0)
    def _():
        at = 0
        for a in refs[:many]:
            flat[at : at + a.shape[0], :] = a[...]
            at += a.shape[0]

    def body(i, _):
        rows = pl.ds(pl.multiple_of(i * chunk, MB), chunk)
        back[rows, :] = dot_nt(flat[rows, :], w[...]).astype(bf)
        return 0

    lax.fori_loop(0, back.shape[0] // chunk, body, 0)


def feed_grad(arrays, w, name, us, tile=512):
    T = sum(x.shape[0] for x in arrays)
    N, D = w.shape
    return pl.pallas_call(
        functools.partial(feed_grad_kernel, len(arrays), chunk_of(T)),
        grid=(pl.cdiv(N, tile),),
        in_specs=[whole(x) for x in arrays] + [pl.BlockSpec((tile, D), lambda j: (j, 0))],
        out_specs=pl.BlockSpec((T, tile), lambda j: (0, j)),
        out_shape=SDS((T, N), bf),
        scratch_shapes=[pltpu.VMEM((T, D), bf)],
        cost_estimate=cost(us),
        name=name,
    )(*arrays, w)


def feed_kernel(plan, many, chunk, *refs):
    arrays, backs = refs[:many], refs[many:-5]
    wg, wu, flat, out, grads = refs[-5:]

    @pl.when(pl.program_id(0) == 0)
    def _():
        lay(flat, arrays, plan)

    at = 0
    for b in backs:
        grads[at : at + b.shape[0], :] = b[...]
        at += b.shape[0]

    def body(i, _):
        rows = pl.ds(pl.multiple_of(i * chunk, MB), chunk)
        gate = dot_nt(flat[rows, :], wg[...])
        up = dot_nt(flat[rows, :], wu[...])
        grad = grads[rows, :].astype(f32)
        sig = jax.nn.sigmoid(gate)
        silu = gate * sig
        out[0, rows, :] = (grad * up * sig * (1.0 + gate * (1.0 - sig))).astype(bf)
        out[1, rows, :] = (grad * silu).astype(bf)
        out[2, rows, :] = (silu * up).astype(bf)
        return 0

    lax.fori_loop(0, flat.shape[0] // chunk, body, 0)


def feed(n, plan, arrays, backs, wg, wu, name, us, tile=512):
    T = n * len(plan)
    N, D = wg.shape
    row = pl.BlockSpec((tile, D), lambda j: (j, 0))
    return pl.pallas_call(
        functools.partial(feed_kernel, plan, len(arrays), chunk_of(T)),
        grid=(pl.cdiv(N, tile),),
        in_specs=[whole(x) for x in arrays]
        + [pl.BlockSpec((rows, tile), lambda j, at=at: (at, j)) for _, rows, at in backs]
        + [row, row],
        out_specs=[pl.BlockSpec((T, D), lambda j: (0, 0)), pl.BlockSpec((3, T, tile), lambda j: (0, 0, j))],
        out_shape=[SDS((T, D), bf), SDS((3, T, N), bf)],
        scratch_shapes=[pltpu.VMEM((T, tile), bf)],
        cost_estimate=cost(us),
        name=name,
    )(*arrays, *[x for x, _, _ in backs], wg, wu)


def feed_blocks_kernel(plans, many, begun, *refs):
    xs, ns = refs[1 : 1 + many], refs[1 + many : 1 + many + len(plans)]
    give, keep = refs[-2:]
    y = None
    for plan, m in zip(plans, ns):
        x = jnp.concatenate([xs[i][...] for i in plan], axis=0)
        p = dot_tn(x, m[...])
        y = p if y is None else y + p
    y = y.T

    @pl.when(pl.program_id(1) == 0)
    def _():
        give[...] = (y + refs[-4][...] if begun else y).astype(give.dtype)

    @pl.when(pl.program_id(1) == 1)
    def _():
        keep[...] = y + refs[-3][...] if begun else y


def feed_blocks(where, nz, xs, plans, ns, first, layers, wide, name, us, begun=(), kind=bf):
    N = ns[0].shape[2]
    x_specs = [
        pl.BlockSpec((x.shape[0], wide), lambda w, b, where: (0, where[3 + nz * (1 - b)])) for x in xs
    ]
    n_specs = [pl.BlockSpec((None, m.shape[1], N), lambda w, b, where: (first + w, 0, 0)) for m in ns]
    out = pl.BlockSpec((None, N, wide), lambda w, b, where: (w, 0, 0))
    return pl.pallas_call(
        functools.partial(feed_blocks_kernel, plans, len(xs), len(begun)),
        grid_spec=pltpu.PrefetchScalarGridSpec(
            num_scalar_prefetch=1,
            grid=(layers, 2),
            in_specs=x_specs + n_specs + [out] * len(begun),
            out_specs=[out, out],
        ),
        out_shape=[SDS((layers, N, wide), kind), SDS((layers, N, wide), f32)],
        cost_estimate=cost(us),
        name=name,
    )(where, *xs, *ns, *begun)


def branch_kernel(n, *refs):
    pieces = refs[:n]
    w, slope, flat, mg, dg = refs[n:]

    @pl.when(pl.program_id(0) == 0)
    def _():
        rows = flat.shape[0] // n
        for i, a in enumerate(pieces):
            flat[i * rows : (i + 1) * rows, :] = a[:rows, :]

    y = dot_nt(flat[...], w[...])
    mg[...] = y.astype(bf)
    dg[...] = (y * slope[...].astype(f32)).astype(bf)


def branch_back(pieces, n, w, slope, tile=256):
    T, C = slope.shape
    D = w.shape[1]
    out = pl.BlockSpec((T, tile), lambda j: (0, j))
    return pl.pallas_call(
        functools.partial(branch_kernel, len(pieces)),
        grid=(C // tile,),
        in_specs=[whole(x) for x in pieces] + [pl.BlockSpec((tile, D), lambda j: (j, 0)), out],
        out_specs=[pl.BlockSpec((T, D), lambda j: (0, 0)), out, out],
        out_shape=[SDS((T, D), bf), SDS((T, C), bf), SDS((T, C), bf)],
        cost_estimate=cost(4),
        name="branch_back",
    )(*pieces, w, slope)


def blocks_kernel(groups, turned, *refs):
    refs = refs[1:]
    n = sum(groups)
    xs, ns, outs = refs[:n], refs[n : 2 * n], refs[2 * n :]
    parts, at = [], 0
    for count in groups:
        y = None
        for i in range(at, at + count):
            p = dot_tn(xs[i][...], ns[i][...])
            y = p if y is None else y + p
        parts.append(y)
        at += count
    for k, o in enumerate(outs):
        @pl.when(pl.program_id(0) == k)
        def _(o=o):
            at = 0
            for y in parts:
                if turned:
                    o[at : at + y.shape[1], :] = y.T.astype(o.dtype)
                else:
                    o[:, at : at + y.shape[1]] = y.astype(o.dtype)
                at += y.shape[1]


def block_products(where, stride, groups, kinds, wide, name, us, turned=False):
    xs = [x for group in groups for x, _ in group]
    ns = [n for group in groups for _, n in group]
    N = sum(group[0][1].shape[1] for group in groups)
    x_specs = [pl.BlockSpec((x.shape[0], wide), lambda k, where: (0, where[3 + stride * k])) for x in xs]
    n_specs = [pl.BlockSpec(n.shape, lambda k, where: (0, 0)) for n in ns]
    shape = (N, wide) if turned else (wide, N)
    return pl.pallas_call(
        functools.partial(blocks_kernel, [len(group) for group in groups], turned),
        grid_spec=pltpu.PrefetchScalarGridSpec(
            num_scalar_prefetch=1,
            grid=(len(kinds),),
            in_specs=x_specs + n_specs,
            out_specs=[pl.BlockSpec(shape, lambda k, where: (0, 0))] * len(kinds),
        ),
        out_shape=[SDS(shape, kind) for kind in kinds],
        cost_estimate=cost(us),
        name=name,
    )(where, *xs, *ns)


def natural_kernel(n, plans, many, where, *refs):
    for plan, out in zip(plans, refs[many:]):
        for r, (i, at) in enumerate(plan):
            out[pl.ds(pl.multiple_of((where[0] ^ r) * n, MB), n), :] = refs[i][at : at + n, :]


def natural(where, arrays, n, plans):
    D = arrays[0].shape[1]
    return pl.pallas_call(
        functools.partial(natural_kernel, n, plans, len(arrays)),
        in_specs=[SM] + [VM] * len(arrays),
        out_specs=[VM] * len(plans),
        out_shape=[SDS((n * len(plan), D), arrays[0].dtype) for plan in plans],
        cost_estimate=cost(0.2),
        name="natural",
    )(where, *arrays)


def join_kernel(one, by_two, two, by_one, for_one, for_two):
    n = by_two.shape[0]
    for_one[:n, :] = (one[:n, :].astype(f32) + by_two[...].astype(f32)).astype(bf)
    for_one[n:, :] = one[n:, :]
    for_two[:n, :] = two[:n, :]
    for_two[n:, :] = (two[n:, :].astype(f32) + by_one[...].astype(f32)).astype(bf)


def join(one, by_two, two, by_one):
    return pl.pallas_call(
        join_kernel,
        in_specs=[VM] * 4,
        out_specs=[VM] * 2,
        out_shape=[SDS(one.shape, bf), SDS(two.shape, bf)],
        cost_estimate=cost(1),
        name="join",
    )(one, by_two, two, by_one)


def add_rows(x, row):
    high = row.astype(bf)
    low = (row - high.astype(f32)).astype(bf)
    rest = jnp.zeros((MB - 2, row.shape[0]), bf)
    return jnp.concatenate([x, high[None], low[None], rest], axis=0)


def last_rows(x):
    return x[-MB].astype(f32) + x[1 - MB].astype(f32)


def after(x, *others):
    return lax.optimization_barrier((x, others))[0]


def rms_inv(x):
    return lax.rsqrt(jnp.mean(x * x, axis=-1, keepdims=True) + EPS)


class Links:
    def __init__(self, mesh):
        self.nh = mesh.shape["head"]
        self.nq = mesh.shape["seq"]
        self.nz = self.nq // 2
        self.turns = tuple(range(self.nh - 1, 0, -1))

    def place(self):
        self.h = lax.axis_index("head")
        self.s = lax.axis_index("seq")
        self.c = self.s % 2
        self.z = self.s // 2

    def partner(self, x, r):
        return lax.ppermute(x, "head", [(i, i ^ r) for i in range(self.nh)])

    def sibling(self, x):
        return lax.ppermute(x, "seq", [(i, i ^ 1) for i in range(self.nq)])

    def along(self, x, k):
        n = self.nz
        return lax.ppermute(x, "seq", [(2 * p + c, 2 * ((p + k) % n) + c) for p in range(n) for c in range(2)])

    def head_sum(self, parts, hold=()):
        got = [after(self.partner(parts[r], r), *hold) for r in self.turns]
        total = parts[0]
        for x in got:
            total = total + x.astype(f32)
        return total

    def head_pieces(self, x):
        got = {r: self.partner(x, r) for r in self.turns}
        return [x] + [got[r] for r in range(1, self.nh)]

    def paired_start(self, parts, across, hold):
        if self.nh != 4:
            return parts[1:]
        by_two = after(self.partner(parts[3], 2), hold)
        by_one = after(self.partner(across, 1), hold)
        return join(parts[1], by_two, parts[2], by_one)

    def paired_pieces(self, x):
        if self.nh != 4:
            return self.head_pieces(x)
        return [x, self.partner(x, 1), self.partner(x, 2)]

    def paired_rest(self, pieces, n):
        if self.nh != 4:
            return pieces, tuple((r, 0) for r in range(self.nh)), tuple((r, n) for r in range(self.nh))
        upper, lower = self.partner(pieces[1][:n], 2), self.partner(pieces[2][n:], 1)
        return pieces + [upper, lower], ((0, 0), (1, 0), (2, 0), (3, 0)), ((0, n), (1, n), (2, n), (4, 0))

    def line_sum(self, parts):
        got = [self.along(parts[k], k) for k in self.line_order()]
        total = parts[0]
        for x in got:
            total = total + x.astype(f32)
        return total

    def line_order(self):
        half = self.nz // 2
        return sorted(range(1, self.nz), key=lambda k: abs(k - half))

    def ring(self, x):
        out = []
        for _ in range(1, self.nz):
            x = self.along(x, 1)
            out.append(x)
        return out

    def ring_sum(self, parts):
        total = parts[self.nz - 1]
        for k in range(self.nz - 2, -1, -1):
            total = parts[k] + self.along(total, 1).astype(f32)
            total = total if k == 0 else total.astype(bf)
        return total

    def relative(self, x):
        n = x.shape[0] // self.nh
        return jnp.concatenate(
            [lax.dynamic_slice_in_dim(x, (self.h ^ r) * n, n, axis=0) for r in range(self.nh)], axis=0
        )


def per_device(
    links,
    inputs,
    lengths,
    first_gain,
    query_weight,
    key_weight,
    value_weight,
    gate_weight,
    rate_weight,
    inner_weight,
    inner_offset,
    inner_gain,
    inner_shift,
    post_gain,
    post_shift,
    out_weight,
    second_gain,
    feed_gate,
    feed_up,
    feed_down,
    out_grad,
):
    links.place()
    nh, nz, nq = links.nh, links.nz, links.nq
    spot = jnp.arange(4 + nz, dtype=jnp.int32)
    cols = 2 * lax.rem(links.z + spot + (nz - 3), nz) + links.c
    cols = jnp.where(spot == 3 + nz, 2 * links.z + 1 - links.c, cols)
    spread = lax.pad(lengths.reshape(-1), jnp.int32(0), [(1, nz + 1, 0)])
    where = jnp.where(spot == 0, links.h, jnp.where(spot < 3, spread, cols))
    n = inputs.shape[0] // nh
    per = n // MB
    wide = inputs.shape[1] // nq
    heads, width = inner_offset.shape
    C = heads * width
    pg, ps = post_gain[None], post_shift[None]
    rate_turned = rate_weight.T
    feed_gate, feed_up = feed_gate.T, feed_up.T

    grad_rel = links.relative(out_grad)
    straight = [0] + list(range(3, nh))
    steps = nz - 1
    lead = jnp.concatenate([grad_rel[:n], grad_rel[3 * n :]], axis=0)
    grad_ring = [links.along(lead, 1)]
    grad_last = links.along(lead, nz - 1)
    steps = nz - 1
    grad_ring = [links.along(jnp.concatenate([grad_rel[:n], grad_rel[3 * n :]], axis=0), 1)]
    normed_one, query, key, value, gate, rate_logit = project(
        nh, where, inputs, first_gain[None], (query_weight, key_weight, value_weight, gate_weight), rate_turned
    )
    mixed, slope, zt, rt, wt, mt = mixer_fwd(
        where, per, query, key, value, gate, rate_logit, inner_weight, inner_offset, inner_gain, inner_shift, pg, ps
    )
    own_source = lax.dynamic_slice_in_dim(inputs, links.h * n, n, axis=0).astype(f32)
    own_upstream = grad_rel[:n].astype(f32)

    mixed = after(mixed, grad_ring[0])
    for k in range(2, nz - 1):
        grad_ring.append(links.along(after(grad_ring[-1], grad_last), 1))
    grad_ring.append(grad_last)
    out_parts = split_product(nh, [(mixed, out_weight, False, 0)], "out_product", 0.1, tile=1024)
    backs = [feed_grad([after(grad_ring[0], out_parts[0])], feed_down, "feed_grad_first", 1)]
    back_own = feed_grad([after(grad_rel, backs[0])], feed_down, "feed_grad_own", 1)
    hidden = own_source + links.head_sum(out_parts, (back_own,))
    r2 = rms_inv(hidden)
    two_own = (second_gain * (hidden * r2)).astype(bf)
    twos = links.head_pieces(two_own)
    lot = lead.shape[0]
    back_next = feed_grad([after(grad_ring[1], two_own), *grad_ring[2:]], feed_down, "feed_grad_next", 1, tile=256)
    grad_across = top_rows([after(grad_ring[0], back_next), *grad_ring[1:]], n)
    twos[1:] = [after(x, grad_across) for x in twos[1:]]
    grad_across = after(grad_across, *twos[1:])
    grad_across = [links.partner(grad_across, r) for r in (1, 2)]
    own_plan = tuple((r, 0) for r in range(nh))
    normed_two, feed_own = feed(n, own_plan, twos, [(back_own, n * nh, 0)], feed_gate, feed_up, "feed_own", 4)
    two_ring = [links.along(after(jnp.concatenate([twos[r] for r in straight], axis=0), *twos[1:]), 1)]
    back_parts = split_product(
        nh, [(feed_own, feed_gate, False, 0), (feed_own, feed_up, False, 1)], "feed_back", 3
    )
    two_ring[0] = after(two_ring[0], back_parts[0])
    for k in range(2, nz):
        two_ring.append(links.along(two_ring[-1], 1))
    back_parts = [back_parts[0]] + [after(x, two_ring[0], *grad_across) for x in back_parts[1:]]
    down_parts = list(split_product(nh, [(after(feed_own, back_parts[0]), feed_down, False, 2)], "feed_down", 1, tile=1024))
    back_last = feed_grad([after(grad_across[0], down_parts[0]), grad_across[1]], feed_down, "feed_grad_last", 1, tile=256)
    two = links.head_sum(back_parts, (back_last, two_ring[1]))
    u = two * second_gain
    hidden_grad = own_upstream + r2 * u - hidden * (r2 * r2 * r2) * jnp.mean(u * hidden, axis=-1, keepdims=True)
    second_part = jnp.sum(two * hidden * r2, axis=0)
    pieces = links.head_pieces(add_rows(hidden_grad.astype(bf), second_part))
    parts = range(len(straight))
    plan = tuple((k, i * n) for k in range(steps - 1) for i in parts)
    held = [after(two_ring[0], pieces[0]), *two_ring[1:-1]]
    first_backs = [(backs[0], lot, 0)] + [(back_next, lot, k) for k in range(steps - 2)]
    first = feed(n, plan, held, first_backs, feed_gate, feed_up, "feed_first", 1)
    begun = feed_blocks(
        where, nz, [normed_two, first[0]], ((0,), (1,)), [feed_own, first[1]], 0, 2, wide, "feed_in_begin", 0.5, kind=bf
    )
    pieces[1:] = [after(x, begun[1]) for x in pieces[1:]]
    second_part = (second_part, pieces[1:])
    pieces[0] = after(pieces[0], two_ring[-1])
    branch_grad, mixed_grad, dg = branch_back(pieces, n, out_weight, slope)
    across = top_rows(two_ring, n)
    across = [links.partner(across, r) for r in (1, 2)]

    one_sib = links.sibling(normed_one)
    groups = [
        [(normed_one, dg), (one_sib, links.sibling(dg))],
        [(branch_grad, mixed), (links.sibling(branch_grad), links.sibling(mixed))],
    ]
    pair = block_products(where, 1, groups, [f32] + [bf] * (nz - 1), wide, "gate_out_blocks", 8)
    pair_got = {k: links.along(pair[k], k) for k in (2, 1)}

    dqkv, drate, dw0, db0, dgain, dshift, dpg, dps = mixer_bwd(
        where, per, query, key, value, gate, rate_logit, after(mixed_grad, pair[0]),
        zt, rt, wt, mt, inner_gain, inner_shift, pg, ps
    )
    dqkv = after(dqkv, pair_got[2], *across)
    for k in range(3, nz):
        pair_got[k] = links.along(after(pair[k], dqkv), k)
    drate_low = drate
    dqkv_sib = links.sibling(dqkv)
    back_parts = split_product(
        nh,
        [
            (dqkv, query_weight, True, 0),
            (dqkv, key_weight, True, 1),
            (dqkv, value_weight, True, 2),
            (dg, gate_weight, True, 0),
            (drate_low, rate_turned, False, 0),
        ],
        "input_back",
        8,
        extra=down_parts[1 : 3 if nh == 4 else nh],
    )
    groups = [[(normed_one, after(dqkv, back_parts[0])), (one_sib, dqkv_sib)]]
    trio = block_products(where, 1, groups, [f32] + [bf] * (nz - 1), wide, "qkv_blocks", 8)
    parts_two = links.paired_start(back_parts, down_parts[3], (trio[0], pair_got[1]))
    trio_step = links.along(trio[-1], 1)

    plan = tuple((0, i * n) for i in parts) + tuple((1 + i, k * n) for i in range(2) for k in range(steps))
    held = [after(two_ring[-1], trio[0], parts_two[0]), *across]
    second_backs = [(back_next, lot, steps - 2), (back_last, 2 * steps * n, 0)]
    second = feed(n, plan, held, second_backs, feed_gate, feed_up, "feed_second", 15, tile=256)

    def rows_of(x):
        return x.reshape(nq, -1)

    def heads_of(x):
        return x.reshape((heads, nq, -1)).transpose(1, 0, 2).reshape(nq, -1)

    received = [links.partner(x, r + 1) for r, x in enumerate(parts_two)]
    second, trio_step, received, pair_got = lax.optimization_barrier((second, trio_step, received, pair_got))
    send = (trio[nz - 2].astype(f32) + trio_step.astype(f32)).astype(bf)
    sums = jnp.concatenate([back_parts[0], down_parts[0]], axis=0)
    for x in received:
        sums = sums + after(x, send).astype(f32)
    one, output = sums[:n], hidden + sums[n:]
    r1 = rms_inv(own_source)
    w = one * first_gain
    input_grad = hidden_grad + r1 * w - own_source * (r1 * r1 * r1) * jnp.mean(w * own_source, axis=-1, keepdims=True)
    input_low = input_grad.astype(bf)
    first_part = jnp.sum(one * own_source * r1, axis=0)
    packed = add_rows(jnp.concatenate([input_low, output.astype(bf)], axis=0), first_part)
    got = links.along(send, 1)
    outs = [feed_own, first[1], second[1]]
    give, keep = feed_blocks(
        where, nz, [after(second[0], packed)], ((0,),), outs[2:], 0, 2, wide, "feed_in_blocks", 6, begun=begun
    )
    for k in range(nz - 3, 0, -1):
        send = (trio[k].astype(f32) + after(got, keep).astype(f32)).astype(bf)
        got = links.along(send, 1)
    pieces, send = lax.optimization_barrier((links.paired_pieces(packed), send))
    arrays, upper, lower = links.paired_rest(pieces, n)
    xs = [after(grad_rel, keep, send, pieces), *grad_ring, *grad_across]
    plans = ((0,), tuple(range(1, steps)), tuple(range(steps, len(xs))))
    first_give = give
    give, keep_out = feed_blocks(where, nz, xs, plans, outs, 2, 1, wide, "feed_out_blocks", 4)
    arrays[1:] = [after(x, keep_out) for x in arrays[1:]]
    input_grad, output = natural(where, arrays, n, (upper, lower))
    other = links.sibling(after(first_give, keep_out)).astype(f32)
    feed_grads = [keep[0] + other[0], keep[1] + other[1]]
    second_part, held = second_part
    second_part = second_part + sum(last_rows(after(x, keep_out)) for x in held)
    rate_part = lax.dot_general(
        after(normed_one, output), drate_low, (((0,), (0,)), ((), ())), preferred_element_type=f32
    )
    dw0, db0, dgain, dshift, dpg, dps = after((dw0, db0, dgain, dshift, dpg, dps), output)
    small = [rows_of(second_part), rows_of(rate_part), heads_of(dw0)]
    small += [heads_of(x) for x in (db0, dgain, dshift)] + [rows_of(dpg), rows_of(dps)]
    sizes = [x.shape[1] for x in small]
    small = jnp.concatenate(small, axis=1)
    got, small = lax.optimization_barrier((after(got, keep_out), small))
    grad_qkv = trio[0] + got.astype(f32)
    feed_grads.append(keep_out[0] + links.sibling(after(give[0], grad_qkv)).astype(f32))
    first_part = first_part + sum(last_rows(arrays[i]) for i, _ in lower[1:])
    sizes = [wide] + sizes
    small = jnp.concatenate([rows_of(first_part), small], axis=1).reshape(nz, 2, -1)
    keep = lax.dynamic_index_in_dim(small, links.c, 1, keepdims=False)
    give = lax.dynamic_index_in_dim(small, 1 - links.c, 1, keepdims=False)
    small = keep + links.sibling(give)
    small = links.line_sum([lax.dynamic_index_in_dim(small, lax.rem(links.z + k, nz), 0, keepdims=False) for k in range(nz)])
    pair = pair[0] + sum(x.astype(f32) for x in pair_got.values())
    ends = [sum(sizes[: i + 1]) for i in range(len(sizes))]
    small = [small[e - n : e] for e, n in zip(ends, sizes)]
    part = width // nq
    return (
        output,
        input_grad,
        small[0],
        grad_qkv[:, :C],
        grad_qkv[:, C : 2 * C],
        grad_qkv[:, 2 * C :],
        pair[:, :C],
        small[2].reshape(-1, heads),
        small[3].reshape(heads, part, width),
        small[4].reshape(heads, part),
        small[5].reshape(heads, part),
        small[6].reshape(heads, part),
        small[7],
        small[8],
        pair[:, C:].T,
        small[1],
        feed_grads[0].T,
        feed_grads[1].T,
        feed_grads[2],
    )


def solution(mesh):
    in_specs = (
        P("seq", None),
        P("seq", None),
        P(),
        P(None, "head"),
        P(None, "head"),
        P(None, "head"),
        P(None, "head"),
        P(None, "head"),
        P("head", None, None),
        P("head", None),
        P("head", None),
        P("head", None),
        P("head"),
        P("head"),
        P("head", None),
        P(),
        P(None, "head"),
        P(None, "head"),
        P("head", None),
        P("seq", None),
    )
    out_specs = (
        P("seq", None),
        P("seq", None),
        P("seq"),
        P("seq", "head"),
        P("seq", "head"),
        P("seq", "head"),
        P("seq", "head"),
        P("seq", "head"),
        P("head", "seq", None),
        P("head", "seq"),
        P("head", "seq"),
        P("head", "seq"),
        P(("head", "seq")),
        P(("head", "seq")),
        P("head", "seq"),
        P("seq"),
        P("seq", "head"),
        P("seq", "head"),
        P("head", "seq"),
    )
    return jax.shard_map(
        functools.partial(per_device, Links(mesh)), mesh=mesh, in_specs=in_specs, out_specs=out_specs, check_vma=False
    )
```
